32 devices in a mesh: slab: 8 (over y, x, core), rep: 4 (over z).
Axes of the slice: x: 2, y: 2, z: 4, core: 2. Of those that a mesh axis runs over, the one named last changes fastest.
Arguments:
- features: bfloat16 [4, 4096, 256], P('rep', 'slab'), may hold values from -6 to 6
- cotangent: bfloat16 [4, 4096, 256], P('rep', 'slab'), may hold values from -6 to 6
- frac_pos: float32 [4, 3, 4096], P('rep', None, 'slab'), may hold values from 0 to 1
- k_vectors: int32 [3, 1024], replicated, may hold values from -6 to 6
- k_filter: float32 [1024, 256], replicated, may hold values from -4 to 4
- w_out: bfloat16 [256, 256], replicated, may hold values from -0.375 to 0.375
- w_short: bfloat16 [256, 256], replicated, may hold values from -0.375 to 0.375
- edge_src: int32 [4, 32768], P('rep', 'slab'), may hold values from 0 to 1023
- edge_dst: int32 [4, 32768], P('rep', 'slab'), may hold values from 0 to 511
- distance: float32 [4, 32768], P('rep', 'slab'), may hold values from 0.5 to 6
- halo_idx: int32 [4, 16, 256], P('rep', 'slab'), may hold values from 0 to 511
Outputs:
- grad_features: bfloat16 [4, 4096, 256], P('rep', 'slab')
- grad_wout: float32 [256, 256], replicated
- grad_wshort: float32 [256, 256], replicated
- grad_filter: float32 [1024, 256], P('slab')
The draws below stay inside these ranges and needn't reach their ends.
Inputs may be any that keep to these rules, and one draw needn't show every extreme that they name: `edge_src`: edge sources index the slab's extended rows: its 512 atoms, then 256 lower rim rows, then 256 upper rim rows. `edge_dst`: edge targets are atoms of the slab that holds the slot. `halo_idx`: row numbers within the sending slab; list 2s goes from slab s to slab s-1, list 2s+1 to slab s+1, cyclically; repeats may occur.
All inputs are finite; a program needn't handle non-finite values.
Results may differ from the reference program's by a relative error of at most 0.0059.
Values may be sent and summed in bfloat16 or wider, within the bound.
No kernel may reach another device: no remote copies, remote signals or barrier semaphores. Data moves between devices by JAX's collectives and lax.ppermute only.
A program may use at most 64 MiB of HBM per device.

```python
import math
import jax
import jax.numpy as jnp
from jax import lax

C = 256
K = 1024
A_DEV = 512
HALO = 256
E_DEV = 4096
NATOMS = 4096
EDGES = 32768
SLOTS = 16
REPS = 4
N_SLAB = 8


def plant(array, rng, smallest, top_value):
    extent = array.shape
    place = [jax.random.randint(jax.random.fold_in(rng, axis), (), 0, extent[axis]) for axis in range(len(extent))]
    array = array.at[tuple(place)].set(smallest)
    longest = extent.index(max(extent))
    place[longest] = (place[longest] + 1) % extent[longest]
    return array.at[tuple(place)].set(top_value)


def steps_of(own_key, dims, split, smallest, top_value):
    level, own = 1.0, jax.random.fold_in(own_key, 6)
    for axis_at, parts in split:
        draws = jnp.exp(jax.random.uniform(jax.random.fold_in(own, axis_at), (parts,), jnp.float32, smallest / len(split), top_value / len(split)))
        level = level * jnp.repeat(draws, dims[axis_at] // parts).reshape([-1 if axis == axis_at else 1 for axis in range(len(dims))])
    return level


def noise(key, extent, deviation, most, cuts=(), held_as=jnp.bfloat16):
    drawn = deviation * jax.random.normal(key, extent, jnp.float32)
    if cuts:
        drawn = drawn * steps_of(key, extent, cuts, -0.22, 0.18)
    return jnp.clip(drawn, -most, most).astype(held_as)


def setup_inputs(seed: int = 0) -> dict:
    keys = jax.random.split(jax.random.key(seed), 12)
    return {
        "features": noise(keys[0], (REPS, NATOMS, C), 1.0, 6.0, ((0, 4), (1, 8))),
        "cotangent": noise(keys[1], (REPS, NATOMS, C), 1.0, 6.0, ((0, 4), (1, 8))),
        "frac_pos": jnp.clip(1.0 * jax.random.uniform(keys[2], (REPS, 3, NATOMS), jnp.float32) ** steps_of(keys[2], (REPS, 3, NATOMS), ((0, 4), (2, 8)), -0.2, 0.2), 0.0, 1.0),
        "k_vectors": plant(jax.random.randint(keys[3], (3, K), -6, 7), jax.random.fold_in(keys[3], 1), -6, 6).astype(jnp.int32),
        "k_filter": noise(keys[4], (K, C), 1.0, 4.0, (), jnp.float32),
        "w_out": noise(keys[5], (C, C), C ** -0.5, 0.375),
        "w_short": noise(keys[6], (C, C), C ** -0.5, 0.375),
        "edge_src": plant(jax.random.randint(keys[7], (REPS, EDGES), 0, A_DEV + 2 * HALO), jax.random.fold_in(keys[7], 1), 0, (A_DEV + 2 * HALO) - 1).astype(jnp.int32),
        "edge_dst": plant(jax.random.randint(keys[8], (REPS, EDGES), 0, A_DEV), jax.random.fold_in(keys[8], 1), 0, A_DEV - 1).astype(jnp.int32),
        "distance": jnp.clip(0.5 + 5.5 * jax.random.uniform(keys[9], (REPS, EDGES), jnp.float32) ** steps_of(keys[9], (REPS, EDGES), ((0, 4), (1, 8)), -0.2, 0.2), 0.5, 6.0),
        "halo_idx": plant(jax.random.randint(keys[10], (REPS, SLOTS, HALO), 0, A_DEV), jax.random.fold_in(keys[10], 1), 0, A_DEV - 1).astype(jnp.int32),
    }


cutoff_radius = 5.0

def phase_tables(k_vectors, positions):
    k_float = k_vectors.astype(jnp.float32)
    theta = k_float[0][:, None] * positions[0][None, :] + k_float[1][:, None] * positions[1][None, :] + k_float[2][:, None] * positions[2][None, :]
    theta = 2.0 * math.pi * theta
    return (jnp.cos(theta).astype(jnp.bfloat16), jnp.sin(theta).astype(jnp.bfloat16))

def contract_rows(left, right):
    return lax.dot_general(left, right, (((0,), (0,)), ((), ())), preferred_element_type=jnp.float32)

def envelope(lengths):
    return jnp.maximum(1.0 - lengths / cutoff_radius, 0.0) ** 2

def fold_rims(owned, lists, from_above, from_below):
    return owned.at[lists[1]].add(from_above).at[lists[0]].add(from_below)

def reference(features, cotangent, frac_pos, k_vectors, k_filter, w_out, w_short, edge_src, edge_dst, distance, halo_idx):
    norm = 1.0 / math.sqrt(K * NATOMS)
    scale = 1.0 / math.sqrt(REPS * NATOMS)
    grad_wout = jnp.zeros((C, C), jnp.float32)
    grad_wshort = jnp.zeros((C, C), jnp.float32)
    grad_filter = jnp.zeros((K, C), jnp.float32)
    w_short32 = w_short.astype(jnp.float32)
    grad_rows = []
    for replica in range(REPS):
        slab_rows = features[replica].reshape(N_SLAB, A_DEV, C)
        slab_cotan = cotangent[replica].reshape(N_SLAB, A_DEV, C)
        slab_pos = frac_pos[replica].reshape(3, N_SLAB, A_DEV).transpose(1, 0, 2)

        def struct_step(total, items):
            rows_block, pos_block = items
            cos_table, sin_table = phase_tables(k_vectors, pos_block)
            term = jnp.stack([jnp.dot(cos_table, rows_block, preferred_element_type=jnp.float32), jnp.dot(sin_table, rows_block, preferred_element_type=jnp.float32)])
            return (total + term, None)
        structure, _ = lax.scan(struct_step, jnp.zeros((2, K, C), jnp.float32), (slab_rows, slab_pos))
        filtered = (norm * structure * k_filter[None]).astype(jnp.bfloat16)

        def response_step(carry, items):
            total, weight_sum = carry
            cotan_block, pos_block = items
            cos_table, sin_table = phase_tables(k_vectors, pos_block)
            message = (contract_rows(cos_table, filtered[0]) + contract_rows(sin_table, filtered[1])).astype(jnp.bfloat16)
            weight_sum = weight_sum + contract_rows(message, cotan_block)
            dmessage = lax.dot_general(cotan_block, w_out, (((1,), (1,)), ((), ())), preferred_element_type=jnp.float32).astype(jnp.bfloat16)
            term = jnp.stack([jnp.dot(cos_table, dmessage, preferred_element_type=jnp.float32), jnp.dot(sin_table, dmessage, preferred_element_type=jnp.float32)])
            return ((total + term, weight_sum), None)
        (response, weight_sum), _ = lax.scan(response_step, (jnp.zeros((2, K, C), jnp.float32), jnp.zeros((C, C), jnp.float32)), (slab_cotan, slab_pos))
        grad_wout = grad_wout + weight_sum
        grad_filter = grad_filter + norm * lax.optimization_barrier(jnp.sum(structure * response, axis=0))
        adjoint = (norm * k_filter[None] * response).astype(jnp.bfloat16)

        def long_block(pos_block):
            cos_table, sin_table = phase_tables(k_vectors, pos_block)
            return contract_rows(cos_table, adjoint[0]) + contract_rows(sin_table, adjoint[1])
        long_grad = lax.map(long_block, slab_pos)
        sources = edge_src[replica].reshape(N_SLAB, E_DEV)
        targets = edge_dst[replica].reshape(N_SLAB, E_DEV)
        weights = envelope(distance[replica].reshape(N_SLAB, E_DEV))

        def edge_block(items):
            cotan_block, source_block, target_block, weight_block = items
            weighted = weight_block[:, None] * cotan_block[target_block].astype(jnp.float32)
            return jax.ops.segment_sum(weighted, source_block, num_segments=A_DEV + 2 * HALO)
        row_grad = lax.map(edge_block, (slab_cotan, sources, targets, weights))
        rim_lists = halo_idx[replica].reshape(N_SLAB, 2, HALO)
        from_above = jnp.roll(row_grad[:, A_DEV:A_DEV + HALO], -1, axis=0)
        from_below = jnp.roll(row_grad[:, A_DEV + HALO:], 1, axis=0)
        owned_grad = jax.vmap(fold_rims)(row_grad[:, :A_DEV], rim_lists, from_above, from_below)
        grad_wshort = grad_wshort + jnp.einsum('sac,sad->cd', slab_rows.astype(jnp.float32), owned_grad, precision=lax.Precision.HIGHEST)
        short_grad = jnp.einsum('sac,dc->sad', owned_grad, w_short32, precision=lax.Precision.HIGHEST)
        summed = slab_cotan.astype(jnp.float32) + long_grad + short_grad
        grad_rows.append(summed.reshape(NATOMS, C).astype(jnp.bfloat16))
    return (jnp.stack(grad_rows), grad_wout * scale, grad_wshort * scale, grad_filter / REPS)
```

```python
import functools
import math

import jax
import jax.numpy as jnp
from jax import lax
from jax.experimental import pallas as pl
from jax.experimental.pallas import tpu as pltpu
from jax.sharding import PartitionSpec as P

cutoff_radius = 5.0
f32, bf16 = jnp.float32, jnp.bfloat16

sin_coefs = (3.1415926401307073, -5.167710083507895, 2.550077523214559, -0.5982912856198396, 0.0776576603038396)
cos_coefs = (0.9999999532476077, -4.934792830619641, 4.058411352862562, -1.331876568080612, 0.21968961109715823)

VMEM = pl.BlockSpec(memory_space=pltpu.VMEM)
SMEM = pl.BlockSpec(memory_space=pltpu.SMEM)


def params():
    return pltpu.CompilerParams(vmem_limit_bytes=48 * 1024 * 1024)


def xor_permute(value, axis, bits):
    count = lax.axis_size(axis)
    return lax.ppermute(value, axis, [(source, source ^ bits) for source in range(count)])


def shifted(value, axis, steps):
    count = lax.axis_size(axis)
    return lax.ppermute(value, axis, [(source, (source + steps) % count) for source in range(count)])


def exchange_groups(count):
    groups, base = [], 1
    while base < count:
        width = 2 if base == 1 else min(4, count // base)
        groups.append([base * g for g in range(width)])
        base *= width
    return groups


def horner(coefs, z):
    total = coefs[-1]
    for c in coefs[-2::-1]:
        total = total * z + c
    return total


def dot(left, right, left_dim=1, right_dim=0):
    return lax.dot_general(left, right, (((left_dim,), (right_dim,)), ((), ())), preferred_element_type=f32)


def tables_kernel(order, slab_ref, kv_ref, pos_ref, rows_ref, cot_ref, table_ref, part_ref, k_rows, k_cols, p_rows):
    share = table_ref.shape[0] // (2 * len(order))
    channels = rows_ref.shape[1]
    slab = slab_ref[0]
    pos = pos_ref[...]
    high = pos.astype(bf16).astype(f32)
    middle = (pos - high).astype(bf16).astype(f32)
    low = pos - high - middle
    kv = kv_ref[...].astype(f32)
    k_rows[...] = jnp.zeros_like(k_rows)
    p_rows[...] = jnp.zeros_like(p_rows)
    for i, piece in enumerate((high, middle, low)):
        k_rows[3 * i : 3 * i + 3, :] = kv
        p_rows[3 * i : 3 * i + 3, :] = piece
    k_cols[...] = k_rows[...].T
    positions = p_rows[...].astype(bf16)

    def block(place, owner):
        k_block = k_cols[pl.ds(pl.multiple_of(owner * share, 8), share), :].astype(bf16)
        turns = dot(k_block, positions)
        r = turns - jnp.floor(turns + 0.5)
        z = r * r
        s = r * horner(sin_coefs, z)
        c = horner(cos_coefs, z)
        cos = 1.0 - 2.0 * s * s
        sin = 2.0 * s * c
        table = jnp.concatenate([cos, sin], axis=0).astype(bf16)
        at = pl.ds(place * 2 * share, 2 * share)
        table_ref[at, :] = table
        part_ref[at, :channels] = dot(table, rows_ref[...]).astype(bf16)
        part_ref[at, channels:] = dot(table, cot_ref[...]).astype(bf16)

    for place, offset in enumerate(order):
        block(place, slab ^ offset)


def tables(order, slab, k_vectors, positions, rows, cotan, share):
    atoms, channels = rows.shape
    kcount = k_vectors.shape[1]
    height = 2 * share * len(order)
    return pl.pallas_call(
        functools.partial(tables_kernel, order),
        name="tables",
        out_shape=(
            jax.ShapeDtypeStruct((height, atoms), bf16),
            jax.ShapeDtypeStruct((height, 2 * channels), bf16),
        ),
        in_specs=[SMEM, VMEM, VMEM, VMEM, VMEM],
        out_specs=(VMEM, VMEM),
        scratch_shapes=[
            pltpu.VMEM((16, kcount), f32),
            pltpu.VMEM((kcount, 16), f32),
            pltpu.VMEM((16, atoms), f32),
        ],
        compiler_params=params(),
        cost_estimate=pl.CostEstimate(
            flops=2 * height * atoms * 2 * channels, bytes_accessed=4 * height * atoms, transcendentals=0
        ),
    )(slab, k_vectors, positions, rows, cotan)


def edge_kernel(block, src_ref, dst_ref, dist_ref, cot_ref, own_ref, low_ref, up_ref, total):
    atoms, _ = cot_ref.shape
    rim = low_ref.shape[0]
    edges = src_ref.shape[1]
    cot_t = cot_ref[...].T
    for start in range(0, edges, block):
        at = slice(start, start + block)
        source, target = src_ref[:, at], dst_ref[:, at]
        weight = jnp.maximum(1.0 - dist_ref[:, at] / cutoff_radius, 0.0)
        weight = weight * weight
        pick = lax.broadcasted_iota(jnp.int32, (atoms, block), 0) == target
        taken = dot(cot_t, pick.astype(f32).astype(bf16))
        weighted = (taken * weight).astype(bf16)
        put = lax.broadcasted_iota(jnp.int32, (total.shape[0], block), 0) == source
        part = dot(put.astype(f32).astype(bf16), weighted, 1, 1)
        total[...] = part if start == 0 else total[...] + part
    own_ref[...] = total[:atoms, :]
    low_ref[...] = total[atoms : atoms + rim, :].astype(bf16)
    up_ref[...] = total[atoms + rim :, :].astype(bf16)


def edge_rows(sources, targets, lengths, cotan, rim):
    atoms, channels = cotan.shape
    edges = sources.shape[1]
    rows = atoms + 2 * rim
    block = math.gcd(edges, 512)
    return pl.pallas_call(
        functools.partial(edge_kernel, block),
        name="edges",
        out_shape=(
            jax.ShapeDtypeStruct((atoms, channels), f32),
            jax.ShapeDtypeStruct((rim, channels), bf16),
            jax.ShapeDtypeStruct((rim, channels), bf16),
        ),
        in_specs=[VMEM] * 4,
        out_specs=(VMEM,) * 3,
        scratch_shapes=[pltpu.VMEM((rows, channels), f32)],
        compiler_params=params(),
        cost_estimate=pl.CostEstimate(
            flops=2 * edges * (rows + atoms) * channels, bytes_accessed=edges * 12, transcendentals=0
        ),
    )(sources, targets, lengths, cotan)


def short_kernel(own_ref, above_ref, below_ref, lists_ref, rows_ref, cot_ref, w_ref, base_ref, grad_ref):
    atoms = own_ref.shape[0]
    lists = lists_ref[...]
    shape = (atoms, lists.shape[1])
    row_at = lax.broadcasted_iota(jnp.int32, shape, 0)
    to_lower = (row_at == lists[0:1, :]).astype(f32).astype(bf16)
    to_upper = (row_at == lists[1:2, :]).astype(f32).astype(bf16)
    owned = own_ref[...] + dot(to_upper, above_ref[...]) + dot(to_lower, below_ref[...])
    owned = owned.astype(bf16)
    base_ref[...] = cot_ref[...].astype(f32) + dot(owned, w_ref[...], 1, 1)
    grad_ref[...] = dot(rows_ref[...], owned, 0, 0)


def short_range(own, above, below, lists, rows, cotan, w_short):
    atoms, channels = rows.shape
    return pl.pallas_call(
        short_kernel,
        name="short",
        out_shape=(
            jax.ShapeDtypeStruct((atoms, channels), f32),
            jax.ShapeDtypeStruct((channels, channels), f32),
        ),
        in_specs=[VMEM] * 7,
        out_specs=(VMEM, VMEM),
        compiler_params=params(),
        cost_estimate=pl.CostEstimate(
            flops=8 * atoms * channels * channels, bytes_accessed=8 * atoms * channels, transcendentals=0
        ),
    )(own, above, below, lists, rows, cotan, w_short)


def share_kernel(order, norm, count, slab_ref, filter_ref, w_ref, short_ref, own_ref, *refs):
    parts, (adj_ref, gfilter_ref, send_ref, keep_ref, full) = refs[:count], refs[count:]
    channels = w_ref.shape[0]
    height = 2 * channels // len(order)
    slab = slab_ref[0]
    total = own_ref[...].astype(f32)
    for part in parts:
        total = total + part[...].astype(f32)
    structure = total[:, :channels]
    moved = total[:, channels:].astype(bf16)
    response = dot(moved, w_ref[...], 1, 1)
    k_filter = filter_ref[...]
    double = jnp.concatenate([k_filter, k_filter], axis=0) * norm
    filtered = (structure * double).astype(bf16)
    full[:channels, :] = dot(filtered, moved, 0, 0)
    full[channels:, :] = short_ref[...]
    half = len(order) // 2
    for place, offset in enumerate(order):
        ref = send_ref if place < half else keep_ref
        at = (place % half) * height
        rows = pl.ds(pl.multiple_of((slab ^ offset) * height, height), height)
        ref[at : at + height, :] = full[rows, :].astype(ref.dtype)
    adj_ref[...] = (response * double).T.astype(bf16)
    product = structure * response
    share = k_filter.shape[0]
    gfilter_ref[...] = norm * (product[:share] + product[share:])


def own_share(order, norm, slab, k_filter, w_out, short_grad, own, parts):
    height, channels = own.shape[0], w_out.shape[0]
    share = height // 2
    whole = lambda shape: pl.BlockSpec(shape, lambda i, slab_ref: (0, 0))
    grid_spec = pltpu.PrefetchScalarGridSpec(
        num_scalar_prefetch=1,
        grid=(1,),
        in_specs=[
            pl.BlockSpec((share, channels), lambda i, slab_ref: (slab_ref[0], 0)),
            whole(w_out.shape),
            whole(short_grad.shape),
            whole(own.shape),
        ]
        + [whole(own.shape)] * len(parts),
        out_specs=(
            whole((channels, height)),
            whole((share, channels)),
            whole((channels, channels)),
            whole((channels, channels)),
        ),
        scratch_shapes=[pltpu.VMEM((2 * channels, channels), f32)],
    )
    return pl.pallas_call(
        functools.partial(share_kernel, order, norm, len(parts)),
        name="share",
        out_shape=(
            jax.ShapeDtypeStruct((channels, height), bf16),
            jax.ShapeDtypeStruct((share, channels), f32),
            jax.ShapeDtypeStruct((channels, channels), bf16),
            jax.ShapeDtypeStruct((channels, channels), f32),
        ),
        grid_spec=grid_spec,
        compiler_params=params(),
        cost_estimate=pl.CostEstimate(
            flops=4 * height * channels * channels, bytes_accessed=16 * height * channels, transcendentals=0
        ),
    )(slab, k_filter, w_out, short_grad, own, *parts)


def back_kernel(base_ref, even_ref, odd_ref, even_adj_ref, odd_adj_ref, out_ref):
    total = None
    for table_ref, adj_ref in ((even_ref, even_adj_ref), (odd_ref, odd_adj_ref)):
        count, _, width = adj_ref.shape
        for i in range(count):
            part = dot(adj_ref[i], table_ref[i * width : (i + 1) * width, :])
            total = part if total is None else total + part
    out_ref[...] = (base_ref[...] + total.T).astype(bf16)


def back_project(base, even, odd, even_adj, odd_adj):
    atoms, channels = base.shape
    return pl.pallas_call(
        back_kernel,
        name="back",
        out_shape=jax.ShapeDtypeStruct((atoms, channels), bf16),
        in_specs=[VMEM] * 5,
        out_specs=VMEM,
        compiler_params=params(),
        cost_estimate=pl.CostEstimate(
            flops=4 * even.shape[0] * atoms * channels, bytes_accessed=4 * even.shape[0] * atoms, transcendentals=0
        ),
    )(base, even, odd, even_adj, odd_adj)


def place_kernel(order, scale, slab_ref, even_ref, odd_ref, wout_ref, wshort_ref, full):
    channels = wout_ref.shape[0]
    height = 2 * channels // len(order)
    slab = slab_ref[0]
    half = len(order) // 2
    for place, offset in enumerate(order):
        ref = odd_ref if place < half else even_ref
        at = (place % half) * height
        rows = pl.ds(pl.multiple_of((slab ^ offset) * height, height), height)
        full[rows, :] = ref[at : at + height, :].astype(f32) * scale
    wout_ref[...] = full[:channels, :]
    wshort_ref[...] = full[channels:, :]


def place_grads(order, scale, slab, even, odd):
    channels = even.shape[1]
    return pl.pallas_call(
        functools.partial(place_kernel, order, scale),
        name="place",
        out_shape=(jax.ShapeDtypeStruct((channels, channels), f32),) * 2,
        in_specs=[SMEM, VMEM, VMEM],
        out_specs=(VMEM, VMEM),
        scratch_shapes=[pltpu.VMEM((2 * channels, channels), f32)],
        compiler_params=params(),
    )(slab, even, odd)


def scatter_blocks(blocks, groups):
    parts = []
    for group in groups:
        if parts:
            blocks = sum((part.astype(f32) for part in parts), blocks.astype(f32))
        width = len(group)
        split = blocks.reshape(-1, width, *blocks.shape[1:])
        parts = [xor_permute(split[:, g].astype(bf16), "slab", group[g]) for g in range(1, width)]
        blocks = split[:, 0]
    return blocks, parts


def gather_blocks(block, groups):
    blocks, order = block[None], [0]
    for group in reversed(groups):
        pieces = [blocks] + [xor_permute(blocks, "slab", offset) for offset in group[1:]]
        blocks = jnp.concatenate(pieces, axis=0)
        order = [offset ^ held for offset in group for held in order]
    return blocks, order


def sum_replicas(value):
    count = lax.axis_size("rep")
    sent = value.astype(bf16)
    terms = [sent] + [xor_permute(sent, "rep", offset) for offset in range(1, count)]
    terms = [term.astype(f32) for term in terms]
    while len(terms) > 1:
        terms = [terms[i] + terms[i + 1] for i in range(0, len(terms), 2)]
    return terms[0]


def body(
    features,
    cotangent,
    frac_pos,
    k_vectors,
    k_filter,
    w_out,
    w_short,
    edge_src,
    edge_dst,
    distance,
    halo_idx,
):
    rows = features[0]
    cotan = cotangent[0]
    atoms, channels = rows.shape
    kcount = k_filter.shape[0]
    count = lax.axis_size("slab")
    replicas = lax.axis_size("rep")
    norm = 1.0 / math.sqrt(kcount * atoms * count)
    scale = 1.0 / math.sqrt(replicas * atoms * count)
    share = kcount // count
    slab = lax.axis_index("slab").astype(jnp.int32)[None]
    pair, *rest = exchange_groups(count)

    even = [0]
    for group in reversed(rest):
        even = [offset ^ held for offset in group for held in even]
    keep_order = sorted(even)
    odd = [offset ^ 1 for offset in keep_order]
    order = odd + keep_order

    odd_table, odd_part = tables(tuple(odd), slab, k_vectors, frac_pos[0], rows, cotan, share)
    from_pair = xor_permute(odd_part, "slab", 1)
    even_table, even_part = tables(tuple(keep_order), slab, k_vectors, frac_pos[0], rows, cotan, share)

    own_rows, lower, upper = edge_rows(edge_src, edge_dst, distance, cotan, halo_idx.shape[2])
    from_above = shifted(lower, "slab", -1)
    from_below = shifted(upper, "slab", 1)
    base, short_grad = short_range(own_rows, from_above, from_below, halo_idx[0], rows, cotan, w_short)

    half = count // 2
    paired = even_part.astype(f32) + from_pair.astype(f32)
    own, parts = scatter_blocks(paired.reshape(half, 2 * share, 2 * channels), rest)
    adj, gfilter, send, keep = own_share(
        tuple(order), norm, slab, k_filter, w_out, short_grad, own[0], [part[0] for part in parts]
    )

    summed = keep + xor_permute(send, "slab", 1).astype(f32)
    own_grad, grad_parts = scatter_blocks(summed.reshape(half, -1, channels), rest)
    own_grad = sum((part.astype(f32) for part in grad_parts), own_grad)[0]

    adj_even, held = gather_blocks(adj, rest)
    place_of = [held.index(offset) for offset in keep_order]
    if place_of != list(range(half)):
        adj_even = jnp.stack([adj_even[i] for i in place_of])
    adj_odd = xor_permute(adj_even, "slab", 1)
    grad_features = back_project(base, even_table, odd_table, adj_even, adj_odd)

    own_grad = sum_replicas(own_grad).astype(bf16)
    grad_filter = sum_replicas(gfilter) / replicas
    grad_even, _ = gather_blocks(own_grad, rest)
    if place_of != list(range(half)):
        grad_even = jnp.stack([grad_even[i] for i in place_of])
    grad_even = grad_even.reshape(-1, channels)
    grad_odd = xor_permute(grad_even, "slab", 1)
    grad_wout, grad_wshort = place_grads(tuple(order), scale, slab, grad_even, grad_odd)
    return (grad_features[None], grad_wout, grad_wshort, grad_filter)


def solution(mesh):
    return jax.shard_map(
        body,
        mesh=mesh,
        in_specs=(
            P("rep", "slab", None),
            P("rep", "slab", None),
            P("rep", None, "slab"),
            P(),
            P(),
            P(),
            P(),
            P("rep", "slab"),
            P("rep", "slab"),
            P("rep", "slab"),
            P("rep", "slab", None),
        ),
        out_specs=(P("rep", "slab", None), P(), P(), P("slab", None)),
        check_vma=False,
    )
```

```python
import functools
import math

import jax
import jax.numpy as jnp
from jax import lax
from jax.experimental import pallas as pl
from jax.experimental.pallas import tpu as pltpu
from jax.sharding import PartitionSpec as P


cutoff_radius = 5.0
f32, bf16 = jnp.float32, jnp.bfloat16

sin_coefs = (3.1415926401307073, -5.167710083507895, 2.550077523214559, -0.5982912856198396, 0.0776576603038396)
cos_coefs = (0.9999999532476077, -4.934792830619641, 4.058411352862562, -1.331876568080612, 0.21968961109715823)

VMEM = pl.BlockSpec(memory_space=pltpu.VMEM)
SMEM = pl.BlockSpec(memory_space=pltpu.SMEM)
HBM = pl.BlockSpec(memory_space=pltpu.HBM)


def params():
    return pltpu.CompilerParams(vmem_limit_bytes=48 * 1024 * 1024)


def xor_permute(value, axis, bits):
    count = lax.axis_size(axis)
    return lax.ppermute(value, axis, [(source, source ^ bits) for source in range(count)])


def shifted(value, axis, steps):
    count = lax.axis_size(axis)
    return lax.ppermute(value, axis, [(source, (source + steps) % count) for source in range(count)])


def exchange_groups(count):
    groups, base = [], 1
    while base < count:
        width = 2 if base == 1 else min(4, count // base)
        groups.append([base * g for g in range(width)])
        base *= width
    return groups


def horner(coefs, z):
    total = coefs[-1]
    for c in coefs[-2::-1]:
        total = total * z + c
    return total


def halves(value):
    high = value.astype(bf16)
    return high, (value - high.astype(f32)).astype(bf16)


def dot(left, right, left_dim=1, right_dim=0):
    return lax.dot_general(left, right, (((left_dim,), (right_dim,)), ((), ())), preferred_element_type=f32)


def table_blocks(order, slab, k_cols, positions, rows_ref, cot_ref, table_ref, part_ref):
    share = table_ref.shape[0] // (2 * len(order))
    channels = rows_ref.shape[1]
    for place, offset in enumerate(order):
        start = pl.multiple_of((slab ^ offset) * share, 8)
        turns = dot(k_cols[pl.ds(start, share), :].astype(bf16), positions)
        r = turns - jnp.floor(turns + 0.5)
        z = r * r
        s = r * horner(sin_coefs, z)
        c = horner(cos_coefs, z)
        table = jnp.concatenate([1.0 - 2.0 * s * s, 2.0 * s * c], axis=0).astype(bf16)
        at = pl.ds(place * 2 * share, 2 * share)
        table_ref[at, :] = table
        part_ref[at, :channels] = dot(table, rows_ref[...]).astype(part_ref.dtype)
        part_ref[at, channels:] = dot(table, cot_ref[...]).astype(part_ref.dtype)


def first_kernel(order, fetched, slab_ref, kv_hbm, pos_hbm, rows_hbm, cot_hbm, filter_hbm, *refs):
    sources, refs = refs[:fetched], refs[fetched:]
    table_ref, part_ref, k_cols, positions, rows_ref, cot_ref, filter_ref, *refs = refs
    copies_to, (kv_ref, pos_ref, k_rows, p_rows, sems) = refs[:fetched], refs[fetched:]
    slab = slab_ref[0]
    share = filter_ref.shape[0]
    filter_rows = pl.ds(pl.multiple_of(slab * share, 8), share)
    pairs = [
        (kv_hbm, kv_ref),
        (pos_hbm.at[:, 0], pos_ref),
        (rows_hbm.at[0], rows_ref),
        (cot_hbm.at[0], cot_ref),
        (filter_hbm.at[filter_rows, :], filter_ref),
        *zip(sources, copies_to),
    ]
    copies = [pltpu.make_async_copy(source, target, sems.at[i]) for i, (source, target) in enumerate(pairs)]
    for copy in copies:
        copy.start()
    k_rows[...] = jnp.zeros_like(k_rows)
    p_rows[...] = jnp.zeros_like(p_rows)
    copies[0].wait()
    copies[1].wait()
    pos = pos_ref[...]
    high = pos.astype(bf16).astype(f32)
    middle = (pos - high).astype(bf16).astype(f32)
    kv = kv_ref[...].astype(f32)
    for i, piece in enumerate((high, middle, pos - high - middle)):
        k_rows[3 * i : 3 * i + 3, :] = kv
        p_rows[3 * i : 3 * i + 3, :] = piece
    k_cols[...] = k_rows[...].T
    positions[...] = p_rows[...].astype(bf16)
    copies[2].wait()
    copies[3].wait()
    table_blocks(order, slab, k_cols, positions[...], rows_ref, cot_ref, table_ref, part_ref)
    for copy in copies[4:]:
        copy.wait()


def first_tables(order, slab, k_vectors, frac_pos, features, cotangent, k_filter, others, share):
    _, atoms, channels = features.shape
    kcount = k_vectors.shape[1]
    height = 2 * share * len(order)
    operands = (k_vectors, frac_pos.transpose(1, 0, 2), features, cotangent, k_filter, *others)
    shapes = [
        ((height, atoms), bf16),
        ((height, 2 * channels), bf16),
        ((kcount, 16), f32),
        ((16, atoms), bf16),
        ((atoms, channels), bf16),
        ((atoms, channels), bf16),
        ((share, channels), f32),
    ] + [(other.shape, other.dtype) for other in others]
    return pl.pallas_call(
        functools.partial(first_kernel, order, len(others)),
        name="first",
        out_shape=tuple(jax.ShapeDtypeStruct(shape, dtype) for shape, dtype in shapes),
        in_specs=[SMEM] + [HBM] * (5 + len(others)),
        out_specs=(VMEM,) * len(shapes),
        scratch_shapes=[
            pltpu.VMEM((3, kcount), jnp.int32),
            pltpu.VMEM((3, atoms), f32),
            pltpu.VMEM((16, kcount), f32),
            pltpu.VMEM((16, atoms), f32),
            pltpu.SemaphoreType.DMA((5 + len(others),)),
        ],
        compiler_params=params(),
        cost_estimate=pl.CostEstimate(
            flops=4 * height * atoms * channels, bytes_accessed=4 * height * atoms, transcendentals=0
        ),
    )(slab, *(pltpu.with_memory_space_constraint(value, pltpu.HBM) for value in operands))


def second_kernel(order, slab_ref, k_cols, positions, rows_ref, cot_ref, table_ref, part_ref):
    table_blocks(order, slab_ref[0], k_cols, positions[...], rows_ref, cot_ref, table_ref, part_ref)


def second_tables(order, slab, k_cols, positions, rows, cotan, share):
    atoms, channels = rows.shape
    height = 2 * share * len(order)
    return pl.pallas_call(
        functools.partial(second_kernel, order),
        name="second",
        out_shape=(
            jax.ShapeDtypeStruct((height, atoms), bf16),
            jax.ShapeDtypeStruct((height, 2 * channels), f32),
        ),
        in_specs=[SMEM] + [VMEM] * 4,
        out_specs=(VMEM, VMEM),
        compiler_params=params(),
        cost_estimate=pl.CostEstimate(
            flops=4 * height * atoms * channels, bytes_accessed=4 * height * atoms, transcendentals=0
        ),
    )(slab, k_cols, positions, rows, cotan)


def edge_kernel(block, src_ref, dst_ref, dist_ref, cot_ref, own_ref, low_ref, up_ref, total):
    atoms, _ = cot_ref.shape
    rim = low_ref.shape[0]
    edges = src_ref.shape[1]
    cot_t = cot_ref[...].T
    for start in range(0, edges, block):
        at = slice(start, start + block)
        source, target = src_ref[:, at], dst_ref[:, at]
        weight = jnp.maximum(1.0 - dist_ref[:, at] / cutoff_radius, 0.0)
        weight = weight * weight
        pick = lax.broadcasted_iota(jnp.int32, (atoms, block), 0) == target
        taken = dot(cot_t, pick.astype(f32).astype(bf16))
        weighted = (taken * weight).astype(bf16)
        put = lax.broadcasted_iota(jnp.int32, (total.shape[0], block), 0) == source
        part = dot(put.astype(f32).astype(bf16), weighted, 1, 1)
        total[...] = part if start == 0 else total[...] + part
    own_ref[...] = total[:atoms, :]
    low_ref[...] = total[atoms : atoms + rim, :].astype(bf16)
    up_ref[...] = total[atoms + rim :, :].astype(bf16)


def edge_rows(sources, targets, lengths, cotan, rim):
    atoms, channels = cotan.shape
    edges = sources.shape[1]
    rows = atoms + 2 * rim
    block = math.gcd(edges, 512)
    return pl.pallas_call(
        functools.partial(edge_kernel, block),
        name="edges",
        out_shape=(
            jax.ShapeDtypeStruct((atoms, channels), f32),
            jax.ShapeDtypeStruct((rim, channels), bf16),
            jax.ShapeDtypeStruct((rim, channels), bf16),
        ),
        in_specs=[VMEM] * 4,
        out_specs=(VMEM,) * 3,
        scratch_shapes=[pltpu.VMEM((rows, channels), f32)],
        compiler_params=params(),
        cost_estimate=pl.CostEstimate(
            flops=2 * edges * (rows + atoms) * channels, bytes_accessed=edges * 12, transcendentals=0
        ),
    )(sources, targets, lengths, cotan)


def short_kernel(own_ref, above_ref, below_ref, lists_ref, rows_ref, cot_ref, w_ref, base_ref, grad_ref):
    atoms = own_ref.shape[0]
    lists = lists_ref[0]
    shape = (atoms, lists.shape[1])
    row_at = lax.broadcasted_iota(jnp.int32, shape, 0)
    to_lower = (row_at == lists[0:1, :]).astype(f32).astype(bf16)
    to_upper = (row_at == lists[1:2, :]).astype(f32).astype(bf16)
    owned = own_ref[...] + dot(to_upper, above_ref[...]) + dot(to_lower, below_ref[...])
    high, low = halves(owned)
    w = w_ref[...]
    base_ref[...] = cot_ref[...].astype(f32) + (dot(high, w, 1, 1) + dot(low, w, 1, 1))
    rows = rows_ref[...].T
    grad_ref[...] = dot(rows, high) + dot(rows, low)


def short_range(own, above, below, lists, rows, cotan, w_short):
    atoms, channels = rows.shape
    return pl.pallas_call(
        short_kernel,
        name="short",
        out_shape=(
            jax.ShapeDtypeStruct((atoms, channels), f32),
            jax.ShapeDtypeStruct((channels, channels), f32),
        ),
        in_specs=[VMEM] * 7,
        out_specs=(VMEM, VMEM),
        compiler_params=params(),
        cost_estimate=pl.CostEstimate(
            flops=8 * atoms * channels * channels, bytes_accessed=8 * atoms * channels, transcendentals=0
        ),
    )(own, above, below, lists, rows, cotan, w_short)


def share_kernel(order, norm, count, slab_ref, filter_ref, w_ref, short_ref, own_ref, *refs):
    parts, (adj_ref, gfilter_ref, send_ref, keep_ref, full) = refs[:count], refs[count:]
    channels = w_ref.shape[0]
    height = 2 * channels // len(order)
    slab = slab_ref[0]
    total = own_ref[...].astype(f32)
    for part in parts:
        total = total + part[...].astype(f32)
    structure = total[:, :channels]
    moved, moved_low = halves(total[:, channels:])
    response = dot(moved, w_ref[...], 1, 1) + dot(moved_low, w_ref[...], 1, 1)
    k_filter = filter_ref[...]
    double = jnp.concatenate([k_filter, k_filter], axis=0) * norm
    filtered, filtered_low = halves((structure * double).T)
    full[:channels, :] = dot(filtered, moved) + (dot(filtered, moved_low) + dot(filtered_low, moved))
    full[channels:, :] = short_ref[...]
    half = len(order) // 2
    for place, offset in enumerate(order):
        ref = send_ref if place < half else keep_ref
        at = (place % half) * height
        rows = pl.ds(pl.multiple_of((slab ^ offset) * height, height), height)
        ref[at : at + height, :] = full[rows, :].astype(ref.dtype)
    adj_ref[...] = (response * double).T.astype(bf16)
    product = structure * response
    share = k_filter.shape[0]
    gfilter_ref[...] = norm * (product[:share] + product[share:])


def own_share(order, norm, slab, k_filter, w_out, short_grad, own, parts):
    height, channels = own.shape[0], w_out.shape[0]
    share = height // 2
    return pl.pallas_call(
        functools.partial(share_kernel, order, norm, len(parts)),
        name="share",
        out_shape=(
            jax.ShapeDtypeStruct((channels, height), bf16),
            jax.ShapeDtypeStruct((share, channels), f32),
            jax.ShapeDtypeStruct((channels, channels), bf16),
            jax.ShapeDtypeStruct((channels, channels), f32),
        ),
        in_specs=[SMEM] + [VMEM] * (4 + len(parts)),
        out_specs=(VMEM,) * 4,
        scratch_shapes=[pltpu.VMEM((2 * channels, channels), f32)],
        compiler_params=params(),
        cost_estimate=pl.CostEstimate(
            flops=4 * height * channels * channels, bytes_accessed=16 * height * channels, transcendentals=0
        ),
    )(slab, k_filter, w_out, short_grad, own, *parts)


def back_kernel(base_ref, even_ref, odd_ref, even_adj_ref, odd_adj_ref, out_ref):
    total = None
    for table_ref, adj_ref in ((even_ref, even_adj_ref), (odd_ref, odd_adj_ref)):
        count, _, width = adj_ref.shape
        for i in range(count):
            part = dot(adj_ref[i], table_ref[i * width : (i + 1) * width, :])
            total = part if total is None else total + part
    out_ref[...] = (base_ref[...] + total.T).astype(bf16)


def back_project(base, even, odd, even_adj, odd_adj):
    atoms, channels = base.shape
    return pl.pallas_call(
        back_kernel,
        name="back",
        out_shape=jax.ShapeDtypeStruct((atoms, channels), bf16),
        in_specs=[VMEM] * 5,
        out_specs=VMEM,
        compiler_params=params(),
        cost_estimate=pl.CostEstimate(
            flops=4 * even.shape[0] * atoms * channels, bytes_accessed=4 * even.shape[0] * atoms, transcendentals=0
        ),
    )(base, even, odd, even_adj, odd_adj)


def place_kernel(order, scale, slab_ref, even_ref, odd_ref, wout_ref, wshort_ref, full):
    channels = wout_ref.shape[0]
    height = 2 * channels // len(order)
    slab = slab_ref[0]
    half = len(order) // 2
    for place, offset in enumerate(order):
        ref = odd_ref if place < half else even_ref
        at = (place % half) * height
        rows = pl.ds(pl.multiple_of((slab ^ offset) * height, height), height)
        full[rows, :] = ref[at : at + height, :].astype(f32) * scale
    wout_ref[...] = full[:channels, :]
    wshort_ref[...] = full[channels:, :]


def place_grads(order, scale, slab, even, odd):
    channels = even.shape[1]
    return pl.pallas_call(
        functools.partial(place_kernel, order, scale),
        name="place",
        out_shape=(jax.ShapeDtypeStruct((channels, channels), f32),) * 2,
        in_specs=[SMEM, VMEM, VMEM],
        out_specs=(VMEM, VMEM),
        scratch_shapes=[pltpu.VMEM((2 * channels, channels), f32)],
        compiler_params=params(),
    )(slab, even, odd)


def scatter_blocks(blocks, groups):
    parts = []
    for group in groups:
        if parts:
            blocks = sum((part.astype(f32) for part in parts), blocks.astype(f32))
        width = len(group)
        split = blocks.reshape(-1, width, *blocks.shape[1:])
        parts = []
        for g in range(1, width):
            parts.append(xor_permute(split[:, g].astype(bf16), "slab", group[g]))
        blocks = split[:, 0]
    return blocks, parts


def gather_blocks(block, groups):
    blocks, order = block[None], [0]
    for group in reversed(groups):
        pieces = [blocks]
        for g in range(1, len(group)):
            pieces.append(xor_permute(blocks, "slab", group[g]))
        blocks = jnp.concatenate(pieces, axis=0)
        order = [offset ^ held for offset in group for held in order]
    place_of = [order.index(offset) for offset in sorted(order)]
    if place_of != list(range(len(order))):
        blocks = jnp.stack([blocks[i] for i in place_of])
    return blocks


def sum_replicas(value):
    count = lax.axis_size("rep")
    sent = value.astype(bf16)
    terms = [sent]
    for offset in range(1, count):
        terms.append(xor_permute(sent, "rep", offset))
    terms = [term.astype(f32) for term in terms]
    while len(terms) > 1:
        terms = [terms[i] + terms[i + 1] for i in range(0, len(terms), 2)]
    return terms[0]


def block(
    features,
    cotangent,
    frac_pos,
    k_vectors,
    k_filter,
    w_out,
    w_short,
    edge_src,
    edge_dst,
    distance,
    halo_idx,
):
    _, atoms, channels = features.shape
    kcount = k_filter.shape[0]
    count = lax.axis_size("slab")
    replicas = lax.axis_size("rep")
    norm = 1.0 / math.sqrt(kcount * atoms * count)
    scale = 1.0 / math.sqrt(replicas * atoms * count)
    share = kcount // count
    slab = lax.axis_index("slab").astype(jnp.int32)[None]
    _, *rest = exchange_groups(count)

    even = tuple(range(0, count, 2))
    odd = tuple(offset + 1 for offset in even)
    order = odd + even
    half = count // 2

    odd_table, odd_part, k_cols, positions, rows, cotan, own_filter, src, dst, dist, lists, w_out, w_short = (
        first_tables(
            odd,
            slab,
            k_vectors,
            frac_pos,
            features,
            cotangent,
            k_filter,
            (edge_src, edge_dst, distance, halo_idx, w_out, w_short),
            share,
        )
    )
    from_pair = xor_permute(odd_part, "slab", 1)
    even_table, even_part = second_tables(even, slab, k_cols, positions, rows, cotan, share)
    paired = even_part + from_pair.astype(f32)
    own, parts = scatter_blocks(paired.reshape(half, 2 * share, 2 * channels), rest)

    own_rows, lower, upper = edge_rows(src, dst, dist, cotan, lists.shape[2])
    from_above = shifted(lower, "slab", -1)
    from_below = shifted(upper, "slab", 1)
    base, short_grad = short_range(own_rows, from_above, from_below, lists, rows, cotan, w_short)

    adj, gfilter, send, keep = own_share(
        order, norm, slab, own_filter, w_out, short_grad, own[0], [part[0] for part in parts]
    )

    from_pair = xor_permute(send, "slab", 1)
    summed = keep + from_pair.astype(f32)
    own_grad, grad_parts = scatter_blocks(summed.reshape(half, -1, channels), rest)
    own_grad = sum((part.astype(f32) for part in grad_parts), own_grad)[0]

    adj_even = gather_blocks(adj, rest)
    adj_odd = xor_permute(adj_even, "slab", 1)
    grad_features = back_project(base, even_table, odd_table, adj_even, adj_odd)

    own_grad = sum_replicas(own_grad).astype(bf16)
    grad_filter = sum_replicas(gfilter) / replicas
    grad_even = gather_blocks(own_grad, rest).reshape(-1, channels)
    grad_odd = xor_permute(grad_even, "slab", 1)
    grad_wout, grad_wshort = place_grads(order, scale, slab, grad_even, grad_odd)
    return (grad_features[None], grad_wout, grad_wshort, grad_filter)


def solution(mesh):
    return jax.shard_map(
        block,
        mesh=mesh,
        in_specs=(
            P("rep", "slab", None),
            P("rep", "slab", None),
            P("rep", None, "slab"),
            P(),
            P(),
            P(),
            P(),
            P("rep", "slab"),
            P("rep", "slab"),
            P("rep", "slab"),
            P("rep", "slab", None),
        ),
        out_specs=(P("rep", "slab", None), P(), P(), P("slab", None)),
        check_vma=False,
    )
```

```python
import functools
import math

import jax
import jax.numpy as jnp
from jax import lax
from jax.experimental import pallas as pl
from jax.experimental.pallas import tpu as pltpu
from jax.sharding import PartitionSpec as P


cutoff_radius = 5.0
f32, bf16 = jnp.float32, jnp.bfloat16

sin_coefs = (3.1415926401307073, -5.167710083507895, 2.550077523214559, -0.5982912856198396, 0.0776576603038396)
cos_coefs = (0.9999999532476077, -4.934792830619641, 4.058411352862562, -1.331876568080612, 0.21968961109715823)

VMEM = pl.BlockSpec(memory_space=pltpu.VMEM)
SMEM = pl.BlockSpec(memory_space=pltpu.SMEM)
HBM = pl.BlockSpec(memory_space=pltpu.HBM)


def params():
    return pltpu.CompilerParams(vmem_limit_bytes=48 * 1024 * 1024)


def xor_permute(value, axis, bits):
    count = lax.axis_size(axis)
    return lax.ppermute(value, axis, [(source, source ^ bits) for source in range(count)])


def shifted(value, axis, steps):
    count = lax.axis_size(axis)
    return lax.ppermute(value, axis, [(source, (source + steps) % count) for source in range(count)])


def halving_order(count):
    order, bit = [0], count // 2
    while bit > 1:
        order = order + [offset | bit for offset in order]
        bit //= 2
    return tuple(order)


def plane_order(count):
    width = min(4, count // 2)
    offsets = [[offset for offset in range(0, count, 2) if offset // 2 % width == g] for g in range(width)]
    return offsets[: width // 2], offsets[width // 2 :]


def horner(coefs, z):
    total = coefs[-1]
    for c in coefs[-2::-1]:
        total = total * z + c
    return total


def halves(value):
    high = value.astype(bf16)
    return high, (value - high.astype(f32)).astype(bf16)


def dot(left, right, left_dim=1, right_dim=0):
    return lax.dot_general(left, right, (((left_dim,), (right_dim,)), ((), ())), preferred_element_type=f32)


def table_blocks(order, slab, k_cols, positions, rows_ref, cot_ref, table_ref, part_ref):
    share = table_ref.shape[0] // (2 * len(order))
    channels = rows_ref.shape[1]
    for place, offset in enumerate(order):
        start = pl.multiple_of((slab ^ offset) * share, 8)
        turns = dot(k_cols[pl.ds(start, share), :].astype(bf16), positions)
        r = turns - jnp.floor(turns + 0.5)
        z = r * r
        s = r * horner(sin_coefs, z)
        c = horner(cos_coefs, z)
        table = jnp.concatenate([1.0 - 2.0 * s * s, 2.0 * s * c], axis=0).astype(bf16)
        at = pl.ds(place * 2 * share, 2 * share)
        table_ref[at, :] = table
        part_ref[at, :channels] = dot(table, rows_ref[...]).astype(part_ref.dtype)
        part_ref[at, channels:] = dot(table, cot_ref[...]).astype(part_ref.dtype)


def first_kernel(order, fetched, slab_ref, kv_hbm, pos_hbm, rows_hbm, cot_hbm, filter_hbm, *refs):
    sources, refs = refs[:fetched], refs[fetched:]
    table_ref, part_ref, k_cols, positions, rows_ref, cot_ref, filter_ref, *refs = refs
    copies_to, (kv_ref, pos_ref, k_rows, p_rows, sems) = refs[:fetched], refs[fetched:]
    slab = slab_ref[0]
    share = filter_ref.shape[0]
    filter_rows = pl.ds(pl.multiple_of(slab * share, 8), share)
    pairs = [
        (kv_hbm, kv_ref),
        (pos_hbm.at[:, 0], pos_ref),
        (rows_hbm.at[0], rows_ref),
        (cot_hbm.at[0], cot_ref),
        (filter_hbm.at[filter_rows, :], filter_ref),
        *zip(sources, copies_to),
    ]
    copies = [pltpu.make_async_copy(source, target, sems.at[i]) for i, (source, target) in enumerate(pairs)]
    for copy in copies:
        copy.start()
    k_rows[...] = jnp.zeros_like(k_rows)
    p_rows[...] = jnp.zeros_like(p_rows)
    copies[0].wait()
    copies[1].wait()
    pos = pos_ref[...]
    high = pos.astype(bf16).astype(f32)
    middle = (pos - high).astype(bf16).astype(f32)
    kv = kv_ref[...].astype(f32)
    for i, piece in enumerate((high, middle, pos - high - middle)):
        k_rows[3 * i : 3 * i + 3, :] = kv
        p_rows[3 * i : 3 * i + 3, :] = piece
    k_cols[...] = k_rows[...].T
    positions[...] = p_rows[...].astype(bf16)
    copies[2].wait()
    copies[3].wait()
    table_blocks(order, slab, k_cols, positions[...], rows_ref, cot_ref, table_ref, part_ref)
    for copy in copies[4:]:
        copy.wait()


def first_tables(order, slab, k_vectors, frac_pos, features, cotangent, k_filter, others, share):
    _, atoms, channels = features.shape
    kcount = k_vectors.shape[1]
    height = 2 * share * len(order)
    operands = (k_vectors, frac_pos.transpose(1, 0, 2), features, cotangent, k_filter, *others)
    shapes = [
        ((height, atoms), bf16),
        ((height, 2 * channels), bf16),
        ((kcount, 16), f32),
        ((16, atoms), bf16),
        ((atoms, channels), bf16),
        ((atoms, channels), bf16),
        ((share, channels), f32),
    ] + [(other.shape, other.dtype) for other in others]
    return pl.pallas_call(
        functools.partial(first_kernel, order, len(others)),
        name="first",
        out_shape=tuple(jax.ShapeDtypeStruct(shape, dtype) for shape, dtype in shapes),
        in_specs=[SMEM] + [HBM] * (5 + len(others)),
        out_specs=(VMEM,) * len(shapes),
        scratch_shapes=[
            pltpu.VMEM((3, kcount), jnp.int32),
            pltpu.VMEM((3, atoms), f32),
            pltpu.VMEM((16, kcount), f32),
            pltpu.VMEM((16, atoms), f32),
            pltpu.SemaphoreType.DMA((5 + len(others),)),
        ],
        compiler_params=params(),
        cost_estimate=pl.CostEstimate(
            flops=4 * height * atoms * channels, bytes_accessed=4 * height * atoms, transcendentals=0
        ),
    )(slab, *(pltpu.with_memory_space_constraint(value, pltpu.HBM) for value in operands))


def second_kernel(order, slab_ref, k_cols, positions, rows_ref, cot_ref, table_ref, part_ref):
    table_blocks(order, slab_ref[0], k_cols, positions[...], rows_ref, cot_ref, table_ref, part_ref)


def next_tables(dtype, order, slab, k_cols, positions, rows, cotan, share):
    atoms, channels = rows.shape
    height = 2 * share * len(order)
    return pl.pallas_call(
        functools.partial(second_kernel, order),
        out_shape=(
            jax.ShapeDtypeStruct((height, atoms), bf16),
            jax.ShapeDtypeStruct((height, 2 * channels), dtype),
        ),
        in_specs=[SMEM] + [VMEM] * 4,
        out_specs=(VMEM, VMEM),
        compiler_params=params(),
        cost_estimate=pl.CostEstimate(
            flops=4 * height * atoms * channels, bytes_accessed=4 * height * atoms, transcendentals=0
        ),
    )(slab, k_cols, positions, rows, cotan)


def edge_kernel(block, src_ref, dst_ref, dist_ref, cot_ref, own_ref, low_ref, up_ref, total):
    atoms, _ = cot_ref.shape
    rim = low_ref.shape[0]
    edges = src_ref.shape[1]
    cot_t = cot_ref[...].T
    for start in range(0, edges, block):
        at = slice(start, start + block)
        source, target = src_ref[:, at], dst_ref[:, at]
        weight = jnp.maximum(1.0 - dist_ref[:, at] / cutoff_radius, 0.0)
        weight = weight * weight
        pick = lax.broadcasted_iota(jnp.int32, (atoms, block), 0) == target
        taken = dot(cot_t, pick.astype(f32).astype(bf16))
        weighted = (taken * weight).astype(bf16)
        put = lax.broadcasted_iota(jnp.int32, (total.shape[0], block), 0) == source
        part = dot(put.astype(f32).astype(bf16), weighted, 1, 1)
        total[...] = part if start == 0 else total[...] + part
    own_ref[...] = total[:atoms, :]
    low_ref[...] = total[atoms : atoms + rim, :].astype(bf16)
    up_ref[...] = total[atoms + rim :, :].astype(bf16)


def edge_rows(sources, targets, lengths, cotan, rim):
    atoms, channels = cotan.shape
    edges = sources.shape[1]
    rows = atoms + 2 * rim
    block = math.gcd(edges, 512)
    return pl.pallas_call(
        functools.partial(edge_kernel, block),
        name="edges",
        out_shape=(
            jax.ShapeDtypeStruct((atoms, channels), f32),
            jax.ShapeDtypeStruct((rim, channels), bf16),
            jax.ShapeDtypeStruct((rim, channels), bf16),
        ),
        in_specs=[VMEM] * 4,
        out_specs=(VMEM,) * 3,
        scratch_shapes=[pltpu.VMEM((rows, channels), f32)],
        compiler_params=params(),
        cost_estimate=pl.CostEstimate(
            flops=2 * edges * (rows + atoms) * channels, bytes_accessed=edges * 12, transcendentals=0
        ),
    )(sources, targets, lengths, cotan)


def split_blocks(order, slab, value, send_ref, keep_ref, blocks):
    count, height, _ = blocks.shape
    for i in range(count):
        blocks[i] = value[i * height : (i + 1) * height, :]
    for place, offset in enumerate(order):
        keep_ref[place] = blocks[slab ^ offset]
        send_ref[place] = blocks[slab ^ offset ^ 1]


def short_kernel(
    order, slab_ref, own_ref, above_ref, below_ref, lists_ref, rows_ref, cot_ref, w_ref, base_ref, send_ref, keep_ref, blocks
):
    atoms = own_ref.shape[0]
    lists = lists_ref[0]
    shape = (atoms, lists.shape[1])
    row_at = lax.broadcasted_iota(jnp.int32, shape, 0)
    to_lower = (row_at == lists[0:1, :]).astype(f32).astype(bf16)
    to_upper = (row_at == lists[1:2, :]).astype(f32).astype(bf16)
    owned = own_ref[...] + dot(to_upper, above_ref[...]) + dot(to_lower, below_ref[...])
    high, low = halves(owned)
    w = w_ref[...]
    base_ref[...] = cot_ref[...].astype(f32) + (dot(high, w, 1, 1) + dot(low, w, 1, 1))
    rows = rows_ref[...].T
    split_blocks(order, slab_ref[0], dot(rows, high) + dot(rows, low), send_ref, keep_ref, blocks)


def short_range(order, slab, own, above, below, lists, rows, cotan, w_short):
    atoms, channels = rows.shape
    half = len(order)
    height = channels // (2 * half)
    return pl.pallas_call(
        functools.partial(short_kernel, order),
        name="short",
        out_shape=(
            jax.ShapeDtypeStruct((atoms, channels), f32),
            jax.ShapeDtypeStruct((half, height, channels), f32),
            jax.ShapeDtypeStruct((half, height, channels), f32),
        ),
        in_specs=[SMEM] + [VMEM] * 7,
        out_specs=(VMEM,) * 3,
        scratch_shapes=[pltpu.VMEM((2 * half, height, channels), f32)],
        compiler_params=params(),
        cost_estimate=pl.CostEstimate(
            flops=8 * atoms * channels * channels, bytes_accessed=8 * atoms * channels, transcendentals=0
        ),
    )(slab, own, above, below, lists, rows, cotan, w_short)


def share_kernel(order, norm, count, slab_ref, filter_ref, w_ref, *refs):
    parts, (adj_ref, gfilter_ref, send_ref, keep_ref, blocks) = refs[:count], refs[count:]
    channels = w_ref.shape[0]
    total = parts[0][...].astype(f32)
    for part in parts[1:]:
        total = total + part[...].astype(f32)
    structure = total[:, :channels]
    moved, moved_low = halves(total[:, channels:])
    response = dot(moved, w_ref[...], 1, 1) + dot(moved_low, w_ref[...], 1, 1)
    k_filter = filter_ref[...]
    double = jnp.concatenate([k_filter, k_filter], axis=0) * norm
    filtered, filtered_low = halves((structure * double).T)
    wout = dot(filtered, moved) + (dot(filtered, moved_low) + dot(filtered_low, moved))
    split_blocks(order, slab_ref[0], wout, send_ref, keep_ref, blocks)
    adj_ref[...] = (response * double).T.astype(bf16)
    product = structure * response
    share = k_filter.shape[0]
    gfilter_ref[...] = norm * (product[:share] + product[share:])


def own_share(order, norm, slab, k_filter, w_out, parts):
    height, channels = parts[0].shape[0], w_out.shape[0]
    half = len(order)
    rows = channels // (2 * half)
    return pl.pallas_call(
        functools.partial(share_kernel, order, norm, len(parts)),
        name="share",
        out_shape=(
            jax.ShapeDtypeStruct((channels, height), bf16),
            jax.ShapeDtypeStruct((height // 2, channels), f32),
            jax.ShapeDtypeStruct((half, rows, channels), f32),
            jax.ShapeDtypeStruct((half, rows, channels), f32),
        ),
        in_specs=[SMEM] + [VMEM] * (2 + len(parts)),
        out_specs=(VMEM,) * 4,
        scratch_shapes=[pltpu.VMEM((2 * half, rows, channels), f32)],
        compiler_params=params(),
        cost_estimate=pl.CostEstimate(
            flops=8 * height * channels * channels, bytes_accessed=16 * height * channels, transcendentals=0
        ),
    )(slab, k_filter, w_out, *parts)


def back_kernel(orders, order, base_ref, even_adj_ref, odd_adj_ref, *refs):
    table_refs, out_ref = refs[:-1], refs[-1]
    width = even_adj_ref.shape[2]
    total = None
    for offsets, table_ref in zip(orders, table_refs):
        for place, offset in enumerate(offsets):
            adj = (odd_adj_ref if offset & 1 else even_adj_ref)[order.index(offset & ~1)]
            part = dot(adj, table_ref[place * width : (place + 1) * width, :])
            total = part if total is None else total + part
    out_ref[...] = (base_ref[...] + total.T).astype(bf16)


def back_project(orders, order, base, even_adj, odd_adj, tables):
    atoms, channels = base.shape
    height = sum(table.shape[0] for table in tables)
    return pl.pallas_call(
        functools.partial(back_kernel, orders, order),
        name="back",
        out_shape=jax.ShapeDtypeStruct((atoms, channels), bf16),
        in_specs=[VMEM] * (3 + len(tables)),
        out_specs=VMEM,
        compiler_params=params(),
        cost_estimate=pl.CostEstimate(
            flops=2 * height * atoms * channels, bytes_accessed=2 * height * atoms, transcendentals=0
        ),
    )(base, even_adj, odd_adj, *tables)


def place_kernel(order, scale, slab_ref, even_ref, odd_ref, wout_ref, wshort_ref, blocks):
    count, height, _ = blocks.shape
    half = height // 2
    slab = slab_ref[0]
    for place, offset in enumerate(order):
        blocks[slab ^ offset] = even_ref[place].astype(f32) * scale
        blocks[slab ^ offset ^ 1] = odd_ref[place].astype(f32) * scale
    for i in range(count):
        wout_ref[i * half : (i + 1) * half, :] = blocks[i, :half, :]
        wshort_ref[i * half : (i + 1) * half, :] = blocks[i, half:, :]


def place_grads(order, scale, slab, even, odd):
    half, height, channels = even.shape
    return pl.pallas_call(
        functools.partial(place_kernel, order, scale),
        name="place",
        out_shape=(jax.ShapeDtypeStruct((channels, channels), f32),) * 2,
        in_specs=[SMEM, VMEM, VMEM],
        out_specs=(VMEM, VMEM),
        scratch_shapes=[pltpu.VMEM((2 * half, height, channels), f32)],
        compiler_params=params(),
    )(slab, even, odd)


def halving_sum(blocks):
    bit = 2
    while blocks.shape[0] > 1:
        half = blocks.shape[0] // 2
        moved = xor_permute(blocks[half:].astype(bf16), "slab", bit)
        blocks = blocks[:half] + moved.astype(f32)
        bit = 2 * bit
    return blocks


def doubling_gather(blocks):
    count = lax.axis_size("slab")
    bit = count // 2
    while bit > 1:
        moved = xor_permute(blocks, "slab", bit)
        blocks = jnp.concatenate([blocks, moved], axis=0)
        bit = bit // 2
    return blocks


def sum_replicas(value):
    bit = 1
    while bit < lax.axis_size("rep"):
        sent = value.astype(bf16)
        moved = xor_permute(sent, "rep", bit)
        value = sent.astype(f32) + moved.astype(f32)
        bit = 2 * bit
    return value


def plane_sum(blocks):
    count = lax.axis_size("slab")
    bit = 2
    terms = None
    while bit < count:
        width = min(4, count // bit)
        sent = {g: [] for g in range(width)}
        for offset in sorted(blocks):
            sent[offset // bit % width].append(offset)
        received = {offset: [] for offset in sent[0]}
        for g in range(width - 1, 0, -1):
            pieces = [blocks[offset].astype(bf16) for offset in sent[g]]
            payload = pieces[0] if len(pieces) == 1 else jnp.concatenate(pieces, axis=0)
            moved = xor_permute(payload, "slab", g * bit)
            height = moved.shape[0] // len(pieces)
            for i, offset in enumerate(sent[0]):
                received[offset].append(moved[i * height : (i + 1) * height])
        terms = [blocks[0], *received[0]]
        blocks = {
            offset: sum((piece.astype(f32) for piece in received[offset]), blocks[offset].astype(f32))
            for offset in sent[0]
        }
        bit = bit * width
    return terms


def block(
    features,
    cotangent,
    frac_pos,
    k_vectors,
    k_filter,
    w_out,
    w_short,
    edge_src,
    edge_dst,
    distance,
    halo_idx,
):
    _, atoms, _ = features.shape
    kcount = k_filter.shape[0]
    count = lax.axis_size("slab")
    replicas = lax.axis_size("rep")
    norm = 1.0 / math.sqrt(kcount * atoms * count)
    scale = 1.0 / math.sqrt(replicas * atoms * count)
    share = kcount // count
    slab = lax.axis_index("slab").astype(jnp.int32)[None]

    near, far = plane_order(count)
    near, far = (tuple(offset for group in groups for offset in group) for groups in (near, far))
    flip = lambda offsets: tuple(offset ^ 1 for offset in offsets)
    orders = (flip(far), far, flip(near), near)
    order = halving_order(count)

    odda, odda_part, k_cols, positions, rows, cotan, own_filter, src, dst, dist, lists, w_out, w_short = first_tables(
        orders[0],
        slab,
        k_vectors,
        frac_pos,
        features,
        cotangent,
        k_filter,
        (edge_src, edge_dst, distance, halo_idx, w_out, w_short),
        share,
    )
    moveda = xor_permute(odda_part, "slab", 1)
    operands = (slab, k_cols, positions, rows, cotan, share)
    evena, evena_part = next_tables(f32, orders[1], *operands)
    oddb, oddb_part = next_tables(bf16, orders[2], *operands)
    movedb = xor_permute(oddb_part, "slab", 1)
    evenb, evenb_part = next_tables(f32, orders[3], *operands)
    blocks = {}
    for offsets, part, moved in ((far, evena_part, moveda), (near, evenb_part, movedb)):
        paired = part + moved.astype(f32)
        for i, offset in enumerate(offsets):
            blocks[offset] = paired[i * 2 * share : (i + 1) * 2 * share]
    parts = plane_sum(blocks)

    own_rows, lower, upper = edge_rows(src, dst, dist, cotan, lists.shape[2])
    from_above = shifted(lower, "slab", -1)
    from_below = shifted(upper, "slab", 1)
    adj, gfilter, wout_send, wout_keep = own_share(order, norm, slab, own_filter, w_out, parts)
    wout_moved = xor_permute(wout_send, "slab", 1)
    base, wshort_send, wshort_keep = short_range(
        order, slab, own_rows, from_above, from_below, lists, rows, cotan, w_short
    )
    wshort_moved = xor_permute(wshort_send, "slab", 1)
    grads = jnp.concatenate([wout_keep + wout_moved, wshort_keep + wshort_moved], axis=1)
    own_grad = halving_sum(grads)

    adj_even = doubling_gather(adj[None])
    adj_odd = xor_permute(adj_even, "slab", 1)
    grad_features = back_project(orders, order, base, adj_even, adj_odd, (odda, evena, oddb, evenb))

    own_grad = sum_replicas(own_grad).astype(bf16)
    filter_sum = sum_replicas(gfilter)
    grad_filter = filter_sum / replicas
    grad_even = doubling_gather(own_grad)
    grad_odd = xor_permute(grad_even, "slab", 1)
    grad_wout, grad_wshort = place_grads(order, scale, slab, grad_even, grad_odd)
    return (grad_features[None], grad_wout, grad_wshort, grad_filter)


def solution(mesh):
    return jax.shard_map(
        block,
        mesh=mesh,
        in_specs=(
            P("rep", "slab", None),
            P("rep", "slab", None),
            P("rep", None, "slab"),
            P(),
            P(),
            P(),
            P(),
            P("rep", "slab"),
            P("rep", "slab"),
            P("rep", "slab"),
            P("rep", "slab", None),
        ),
        out_specs=(P("rep", "slab", None), P(), P(), P("slab", None)),
        check_vma=False,
    )
```

```python
import functools
import math

import jax
import jax.numpy as jnp
from jax import lax
from jax.experimental import pallas as pl
from jax.experimental.pallas import tpu as pltpu
from jax.sharding import PartitionSpec as P


cutoff_radius = 5.0
f32, bf16 = jnp.float32, jnp.bfloat16

sin_coefs = (3.1415926401307073, -5.167710083507895, 2.550077523214559, -0.5982912856198396, 0.0776576603038396)
cos_coefs = (0.9999999532476077, -4.934792830619641, 4.058411352862562, -1.331876568080612, 0.21968961109715823)

VMEM = pl.BlockSpec(memory_space=pltpu.VMEM)
SMEM = pl.BlockSpec(memory_space=pltpu.SMEM)
HBM = pl.BlockSpec(memory_space=pltpu.HBM)


def params():
    return pltpu.CompilerParams(vmem_limit_bytes=48 * 1024 * 1024)


def xor_permute(value, axis, bits):
    count = lax.axis_size(axis)
    return lax.ppermute(value, axis, [(source, source ^ bits) for source in range(count)])


def shifted(value, axis, steps):
    count = lax.axis_size(axis)
    return lax.ppermute(value, axis, [(source, (source + steps) % count) for source in range(count)])


def halving_order(count):
    order, bit = [0], count // 2
    while bit > 1:
        order = order + [offset | bit for offset in order]
        bit //= 2
    return tuple(order)


def plane_order(count):
    width = min(4, count // 2)
    offsets = [[offset for offset in range(0, count, 2) if offset // 2 % width == g] for g in range(width)]
    return offsets[: width // 2], offsets[width // 2 :]


def horner(coefs, z):
    total = coefs[-1]
    for c in coefs[-2::-1]:
        total = total * z + c
    return total


def halves(value):
    high = value.astype(bf16)
    return high, (value - high.astype(f32)).astype(bf16)


def dot(left, right, left_dim=1, right_dim=0):
    return lax.dot_general(left, right, (((left_dim,), (right_dim,)), ((), ())), preferred_element_type=f32)


def table_blocks(order, slab, k_cols, positions, rows_ref, cot_ref, table_ref, part_ref):
    share = table_ref.shape[0] // (2 * len(order))
    channels = rows_ref.shape[1]
    for place, offset in enumerate(order):
        start = pl.multiple_of((slab ^ offset) * share, 8)
        turns = dot(k_cols[pl.ds(start, share), :].astype(bf16), positions)
        r = turns - jnp.floor(turns + 0.5)
        z = r * r
        s = r * horner(sin_coefs, z)
        c = horner(cos_coefs, z)
        table = jnp.concatenate([1.0 - 2.0 * s * s, 2.0 * s * c], axis=0).astype(bf16)
        at = pl.ds(place * 2 * share, 2 * share)
        table_ref[at, :] = table
        part_ref[at, :channels] = dot(table, rows_ref[...]).astype(part_ref.dtype)
        part_ref[at, channels:] = dot(table, cot_ref[...]).astype(part_ref.dtype)


def first_kernel(order, fetched, slab_ref, kv_hbm, pos_hbm, rows_hbm, cot_hbm, filter_hbm, *refs):
    sources, refs = refs[:fetched], refs[fetched:]
    table_ref, part_ref, k_cols, positions, rows_ref, cot_ref, filter_ref, *refs = refs
    copies_to, (kv_ref, pos_ref, k_rows, p_rows, sems) = refs[:fetched], refs[fetched:]
    slab = slab_ref[0]
    share = filter_ref.shape[0]
    filter_rows = pl.ds(pl.multiple_of(slab * share, 8), share)
    pairs = [
        (kv_hbm, kv_ref),
        (pos_hbm.at[:, 0], pos_ref),
        (rows_hbm.at[0], rows_ref),
        (cot_hbm.at[0], cot_ref),
        (filter_hbm.at[filter_rows, :], filter_ref),
        *zip(sources, copies_to),
    ]
    copies = [pltpu.make_async_copy(source, target, sems.at[i]) for i, (source, target) in enumerate(pairs)]
    for copy in copies:
        copy.start()
    k_rows[...] = jnp.zeros_like(k_rows)
    p_rows[...] = jnp.zeros_like(p_rows)
    copies[0].wait()
    copies[1].wait()
    pos = pos_ref[...]
    high = pos.astype(bf16).astype(f32)
    middle = (pos - high).astype(bf16).astype(f32)
    kv = kv_ref[...].astype(f32)
    for i, piece in enumerate((high, middle, pos - high - middle)):
        k_rows[3 * i : 3 * i + 3, :] = kv
        p_rows[3 * i : 3 * i + 3, :] = piece
    k_cols[...] = k_rows[...].T
    positions[...] = p_rows[...].astype(bf16)
    copies[2].wait()
    copies[3].wait()
    table_blocks(order, slab, k_cols, positions[...], rows_ref, cot_ref, table_ref, part_ref)
    for copy in copies[4:]:
        copy.wait()


def first_tables(order, slab, k_vectors, frac_pos, features, cotangent, k_filter, others, share):
    _, atoms, channels = features.shape
    kcount = k_vectors.shape[1]
    height = 2 * share * len(order)
    operands = (k_vectors, frac_pos.transpose(1, 0, 2), features, cotangent, k_filter, *others)
    shapes = [
        ((height, atoms), bf16),
        ((height, 2 * channels), bf16),
        ((kcount, 16), f32),
        ((16, atoms), bf16),
        ((atoms, channels), bf16),
        ((atoms, channels), bf16),
        ((share, channels), f32),
    ] + [(other.shape, other.dtype) for other in others]
    return pl.pallas_call(
        functools.partial(first_kernel, order, len(others)),
        name="first",
        out_shape=tuple(jax.ShapeDtypeStruct(shape, dtype) for shape, dtype in shapes),
        in_specs=[SMEM] + [HBM] * (5 + len(others)),
        out_specs=(VMEM,) * len(shapes),
        scratch_shapes=[
            pltpu.VMEM((3, kcount), jnp.int32),
            pltpu.VMEM((3, atoms), f32),
            pltpu.VMEM((16, kcount), f32),
            pltpu.VMEM((16, atoms), f32),
            pltpu.SemaphoreType.DMA((5 + len(others),)),
        ],
        compiler_params=params(),
        cost_estimate=pl.CostEstimate(
            flops=4 * height * atoms * channels, bytes_accessed=4 * height * atoms, transcendentals=0
        ),
    )(slab, *(pltpu.with_memory_space_constraint(value, pltpu.HBM) for value in operands))


def second_kernel(order, slab_ref, k_cols, positions, rows_ref, cot_ref, table_ref, part_ref):
    table_blocks(order, slab_ref[0], k_cols, positions[...], rows_ref, cot_ref, table_ref, part_ref)


def next_tables(dtype, order, slab, k_cols, positions, rows, cotan, share):
    atoms, channels = rows.shape
    height = 2 * share * len(order)
    return pl.pallas_call(
        functools.partial(second_kernel, order),
        out_shape=(
            jax.ShapeDtypeStruct((height, atoms), bf16),
            jax.ShapeDtypeStruct((height, 2 * channels), dtype),
        ),
        in_specs=[SMEM] + [VMEM] * 4,
        out_specs=(VMEM, VMEM),
        compiler_params=params(),
        cost_estimate=pl.CostEstimate(
            flops=4 * height * atoms * channels, bytes_accessed=4 * height * atoms, transcendentals=0
        ),
    )(slab, k_cols, positions, rows, cotan)


def edge_kernel(block, src_ref, dst_ref, dist_ref, cot_ref, own_ref, low_ref, up_ref, total):
    atoms, _ = cot_ref.shape
    rim = low_ref.shape[0]
    edges = src_ref.shape[1]
    cot_t = cot_ref[...].T
    for start in range(0, edges, block):
        at = slice(start, start + block)
        source, target = src_ref[:, at], dst_ref[:, at]
        weight = jnp.maximum(1.0 - dist_ref[:, at] / cutoff_radius, 0.0)
        weight = weight * weight
        pick = lax.broadcasted_iota(jnp.int32, (atoms, block), 0) == target
        taken = dot(cot_t, pick.astype(f32).astype(bf16))
        weighted = (taken * weight).astype(bf16)
        put = lax.broadcasted_iota(jnp.int32, (total.shape[0], block), 0) == source
        part = dot(put.astype(f32).astype(bf16), weighted, 1, 1)
        total[...] = part if start == 0 else total[...] + part
    own_ref[...] = total[:atoms, :]
    low_ref[...] = total[atoms : atoms + rim, :].astype(bf16)
    up_ref[...] = total[atoms + rim :, :].astype(bf16)


def edge_rows(sources, targets, lengths, cotan, rim):
    atoms, channels = cotan.shape
    edges = sources.shape[1]
    rows = atoms + 2 * rim
    block = math.gcd(edges, 512)
    return pl.pallas_call(
        functools.partial(edge_kernel, block),
        name="edges",
        out_shape=(
            jax.ShapeDtypeStruct((atoms, channels), f32),
            jax.ShapeDtypeStruct((rim, channels), bf16),
            jax.ShapeDtypeStruct((rim, channels), bf16),
        ),
        in_specs=[VMEM] * 4,
        out_specs=(VMEM,) * 3,
        scratch_shapes=[pltpu.VMEM((rows, channels), f32)],
        compiler_params=params(),
        cost_estimate=pl.CostEstimate(
            flops=2 * edges * (rows + atoms) * channels, bytes_accessed=edges * 12, transcendentals=0
        ),
    )(sources, targets, lengths, cotan)


def split_blocks(order, slab, value, send_ref, keep_ref, blocks):
    count, height, _ = blocks.shape
    for i in range(count):
        blocks[i] = value[i * height : (i + 1) * height, :]
    for place, offset in enumerate(order):
        keep_ref[place] = blocks[slab ^ offset]
        send_ref[place] = blocks[slab ^ offset ^ 1]


def short_kernel(
    order, slab_ref, own_ref, above_ref, below_ref, lists_ref, rows_ref, cot_ref, w_ref, base_ref, send_ref, keep_ref, blocks
):
    atoms = own_ref.shape[0]
    lists = lists_ref[0]
    shape = (atoms, lists.shape[1])
    row_at = lax.broadcasted_iota(jnp.int32, shape, 0)
    to_lower = (row_at == lists[0:1, :]).astype(f32).astype(bf16)
    to_upper = (row_at == lists[1:2, :]).astype(f32).astype(bf16)
    owned = own_ref[...] + dot(to_upper, above_ref[...]) + dot(to_lower, below_ref[...])
    high, low = halves(owned)
    w = w_ref[...]
    base_ref[...] = cot_ref[...].astype(f32) + (dot(high, w, 1, 1) + dot(low, w, 1, 1))
    rows = rows_ref[...].T
    split_blocks(order, slab_ref[0], dot(rows, high) + dot(rows, low), send_ref, keep_ref, blocks)


def short_range(order, slab, own, above, below, lists, rows, cotan, w_short):
    atoms, channels = rows.shape
    half = len(order)
    height = channels // (2 * half)
    return pl.pallas_call(
        functools.partial(short_kernel, order),
        name="short",
        out_shape=(
            jax.ShapeDtypeStruct((atoms, channels), f32),
            jax.ShapeDtypeStruct((half, height, channels), f32),
            jax.ShapeDtypeStruct((half, height, channels), f32),
        ),
        in_specs=[SMEM] + [VMEM] * 7,
        out_specs=(VMEM,) * 3,
        scratch_shapes=[pltpu.VMEM((2 * half, height, channels), f32)],
        compiler_params=params(),
        cost_estimate=pl.CostEstimate(
            flops=8 * atoms * channels * channels, bytes_accessed=8 * atoms * channels, transcendentals=0
        ),
    )(slab, own, above, below, lists, rows, cotan, w_short)


def share_kernel(order, norm, count, slab_ref, filter_ref, w_ref, *refs):
    parts, (adj_ref, gfilter_ref, send_ref, keep_ref, blocks) = refs[:count], refs[count:]
    channels = w_ref.shape[0]
    total = parts[0][...].astype(f32)
    for part in parts[1:]:
        total = total + part[...].astype(f32)
    structure = total[:, :channels]
    moved, moved_low = halves(total[:, channels:])
    response = dot(moved, w_ref[...], 1, 1) + dot(moved_low, w_ref[...], 1, 1)
    k_filter = filter_ref[...]
    double = jnp.concatenate([k_filter, k_filter], axis=0) * norm
    filtered, filtered_low = halves((structure * double).T)
    wout = dot(filtered, moved) + (dot(filtered, moved_low) + dot(filtered_low, moved))
    split_blocks(order, slab_ref[0], wout, send_ref, keep_ref, blocks)
    adj_ref[...] = (response * double).T.astype(bf16)
    product = structure * response
    share = k_filter.shape[0]
    gfilter_ref[...] = norm * (product[:share] + product[share:])


def own_share(order, norm, slab, k_filter, w_out, parts):
    height, channels = parts[0].shape[0], w_out.shape[0]
    half = len(order)
    rows = channels // (2 * half)
    return pl.pallas_call(
        functools.partial(share_kernel, order, norm, len(parts)),
        name="share",
        out_shape=(
            jax.ShapeDtypeStruct((channels, height), bf16),
            jax.ShapeDtypeStruct((height // 2, channels), f32),
            jax.ShapeDtypeStruct((half, rows, channels), f32),
            jax.ShapeDtypeStruct((half, rows, channels), f32),
        ),
        in_specs=[SMEM] + [VMEM] * (2 + len(parts)),
        out_specs=(VMEM,) * 4,
        scratch_shapes=[pltpu.VMEM((2 * half, rows, channels), f32)],
        compiler_params=params(),
        cost_estimate=pl.CostEstimate(
            flops=8 * height * channels * channels, bytes_accessed=16 * height * channels, transcendentals=0
        ),
    )(slab, k_filter, w_out, *parts)


def back_kernel(orders, order, base_ref, even_adj_ref, odd_adj_ref, *refs):
    table_refs, out_ref = refs[:-1], refs[-1]
    width = even_adj_ref.shape[2]
    total = None
    for offsets, table_ref in zip(orders, table_refs):
        for place, offset in enumerate(offsets):
            adj = (odd_adj_ref if offset & 1 else even_adj_ref)[order.index(offset & ~1)]
            part = dot(adj, table_ref[place * width : (place + 1) * width, :])
            total = part if total is None else total + part
    out_ref[...] = (base_ref[...] + total.T).astype(bf16)


def back_project(orders, order, base, even_adj, odd_adj, tables):
    atoms, channels = base.shape
    height = sum(table.shape[0] for table in tables)
    return pl.pallas_call(
        functools.partial(back_kernel, orders, order),
        name="back",
        out_shape=jax.ShapeDtypeStruct((atoms, channels), bf16),
        in_specs=[VMEM] * (3 + len(tables)),
        out_specs=VMEM,
        compiler_params=params(),
        cost_estimate=pl.CostEstimate(
            flops=2 * height * atoms * channels, bytes_accessed=2 * height * atoms, transcendentals=0
        ),
    )(base, even_adj, odd_adj, *tables)


def place_kernel(order, scale, slab_ref, even_ref, odd_ref, wout_ref, wshort_ref, blocks):
    count, height, _ = blocks.shape
    half = height // 2
    slab = slab_ref[0]
    for place, offset in enumerate(order):
        blocks[slab ^ offset] = even_ref[place].astype(f32) * scale
        blocks[slab ^ offset ^ 1] = odd_ref[place].astype(f32) * scale
    for i in range(count):
        wout_ref[i * half : (i + 1) * half, :] = blocks[i, :half, :]
        wshort_ref[i * half : (i + 1) * half, :] = blocks[i, half:, :]


def place_grads(order, scale, slab, even, odd):
    half, height, channels = even.shape
    return pl.pallas_call(
        functools.partial(place_kernel, order, scale),
        name="place",
        out_shape=(jax.ShapeDtypeStruct((channels, channels), f32),) * 2,
        in_specs=[SMEM, VMEM, VMEM],
        out_specs=(VMEM, VMEM),
        scratch_shapes=[pltpu.VMEM((2 * half, height, channels), f32)],
        compiler_params=params(),
    )(slab, even, odd)


def doubling_gather(blocks):
    count = lax.axis_size("slab")
    bit = count // 2
    while bit > 1:
        moved = xor_permute(blocks, "slab", bit)
        blocks = jnp.concatenate([blocks, moved], axis=0)
        bit = bit // 2
    return blocks


def sum_replicas(value):
    bit = 1
    while bit < lax.axis_size("rep"):
        sent = value.astype(bf16)
        moved = xor_permute(sent, "rep", bit)
        value = sent.astype(f32) + moved.astype(f32)
        bit = 2 * bit
    return value


def plane_gather(block, order):
    count = lax.axis_size("slab")
    planes, bit = [], 2
    while bit < count:
        planes.append((bit, min(4, count // bit)))
        bit *= planes[-1][1]
    held = {0: block}
    for bit, width in reversed(planes):
        offsets = sorted(held)
        payload = held[0] if len(held) == 1 else jnp.stack([held[offset] for offset in offsets])
        for g in range(width - 1, 0, -1):
            moved = xor_permute(payload, "slab", g * bit)
            for i, offset in enumerate(offsets):
                held[offset ^ g * bit] = moved if len(offsets) == 1 else moved[i]
    return jnp.stack([held[offset] for offset in order])


def plane_sum(blocks):
    count = lax.axis_size("slab")
    bit = 2
    terms = None
    while bit < count:
        width = min(4, count // bit)
        sent = {g: [] for g in range(width)}
        for offset in sorted(blocks):
            sent[offset // bit % width].append(offset)
        received = {offset: [] for offset in sent[0]}
        for g in range(width - 1, 0, -1):
            pieces = [blocks[offset].astype(bf16) for offset in sent[g]]
            payload = pieces[0] if len(pieces) == 1 else jnp.concatenate(pieces, axis=0)
            moved = xor_permute(payload, "slab", g * bit)
            height = moved.shape[0] // len(pieces)
            for i, offset in enumerate(sent[0]):
                received[offset].append(moved[i * height : (i + 1) * height])
        terms = [blocks[0], *received[0]]
        blocks = {
            offset: sum((piece.astype(f32) for piece in received[offset]), blocks[offset].astype(f32))
            for offset in sent[0]
        }
        bit = bit * width
    return terms


def block(
    features,
    cotangent,
    frac_pos,
    k_vectors,
    k_filter,
    w_out,
    w_short,
    edge_src,
    edge_dst,
    distance,
    halo_idx,
):
    _, atoms, _ = features.shape
    kcount = k_filter.shape[0]
    count = lax.axis_size("slab")
    replicas = lax.axis_size("rep")
    norm = 1.0 / math.sqrt(kcount * atoms * count)
    scale = 1.0 / math.sqrt(replicas * atoms * count)
    share = kcount // count
    slab = lax.axis_index("slab").astype(jnp.int32)[None]

    near, far = plane_order(count)
    near, far = (tuple(offset for group in groups for offset in group) for groups in (near, far))
    flip = lambda offsets: tuple(offset ^ 1 for offset in offsets)
    orders = (flip(far), far, flip(near), near)
    order = halving_order(count)

    odda, odda_part, k_cols, positions, rows, cotan, own_filter, src, dst, dist, lists, w_out, w_short = first_tables(
        orders[0],
        slab,
        k_vectors,
        frac_pos,
        features,
        cotangent,
        k_filter,
        (edge_src, edge_dst, distance, halo_idx, w_out, w_short),
        share,
    )
    moveda = xor_permute(odda_part, "slab", 1)
    operands = (slab, k_cols, positions, rows, cotan, share)
    evena, evena_part = next_tables(f32, orders[1], *operands)
    oddb, oddb_part = next_tables(bf16, orders[2], *operands)
    movedb = xor_permute(oddb_part, "slab", 1)
    evenb, evenb_part = next_tables(f32, orders[3], *operands)
    blocks = {}
    for offsets, part, moved in ((far, evena_part, moveda), (near, evenb_part, movedb)):
        paired = part + moved.astype(f32)
        for i, offset in enumerate(offsets):
            blocks[offset] = paired[i * 2 * share : (i + 1) * 2 * share]
    parts = plane_sum(blocks)

    own_rows, lower, upper = edge_rows(src, dst, dist, cotan, lists.shape[2])
    from_above = shifted(lower, "slab", -1)
    from_below = shifted(upper, "slab", 1)
    adj, gfilter, wout_send, wout_keep = own_share(order, norm, slab, own_filter, w_out, parts)
    wout_moved = xor_permute(wout_send, "slab", 1)
    base, wshort_send, wshort_keep = short_range(
        order, slab, own_rows, from_above, from_below, lists, rows, cotan, w_short
    )
    wshort_moved = xor_permute(wshort_send, "slab", 1)
    grads = jnp.concatenate([wout_keep + wout_moved, wshort_keep + wshort_moved], axis=1)
    terms = plane_sum({offset: grads[i] for i, offset in enumerate(order)})
    own_grad = sum((term.astype(f32) for term in terms[1:]), terms[0])

    adj_even = doubling_gather(adj[None])
    adj_odd = xor_permute(adj_even, "slab", 1)
    grad_features = back_project(orders, order, base, adj_even, adj_odd, (odda, evena, oddb, evenb))

    own_grad = sum_replicas(own_grad).astype(bf16)
    filter_sum = sum_replicas(gfilter)
    grad_filter = filter_sum / replicas
    grad_even = plane_gather(own_grad, order)
    grad_odd = xor_permute(grad_even, "slab", 1)
    grad_wout, grad_wshort = place_grads(order, scale, slab, grad_even, grad_odd)
    return (grad_features[None], grad_wout, grad_wshort, grad_filter)


def solution(mesh):
    return jax.shard_map(
        block,
        mesh=mesh,
        in_specs=(
            P("rep", "slab", None),
            P("rep", "slab", None),
            P("rep", None, "slab"),
            P(),
            P(),
            P(),
            P(),
            P("rep", "slab"),
            P("rep", "slab"),
            P("rep", "slab"),
            P("rep", "slab", None),
        ),
        out_specs=(P("rep", "slab", None), P(), P(), P("slab", None)),
        check_vma=False,
    )
```

```python
import functools
import math

import jax
import jax.numpy as jnp
from jax import lax
from jax.experimental import pallas as pl
from jax.experimental.pallas import tpu as pltpu
from jax.sharding import PartitionSpec as P


cutoff_radius = 5.0
f32, bf16 = jnp.float32, jnp.bfloat16

sin_coefs = (3.1415926401307073, -5.167710083507895, 2.550077523214559, -0.5982912856198396, 0.0776576603038396)
cos_coefs = (0.9999999532476077, -4.934792830619641, 4.058411352862562, -1.331876568080612, 0.21968961109715823)

VMEM = pl.BlockSpec(memory_space=pltpu.VMEM)
SMEM = pl.BlockSpec(memory_space=pltpu.SMEM)
HBM = pl.BlockSpec(memory_space=pltpu.HBM)


def params():
    return pltpu.CompilerParams(vmem_limit_bytes=48 * 1024 * 1024)


def xor_permute(value, axis, bits):
    count = lax.axis_size(axis)
    return lax.ppermute(value, axis, [(source, source ^ bits) for source in range(count)])


def shifted(value, axis, steps):
    count = lax.axis_size(axis)
    return lax.ppermute(value, axis, [(source, (source + steps) % count) for source in range(count)])


def halving_order(count):
    order, bit = [0], count // 2
    while bit > 1:
        order = order + [offset | bit for offset in order]
        bit //= 2
    return tuple(order)


def plane_order(count):
    width = min(4, count // 2)
    offsets = [[offset for offset in range(0, count, 2) if offset // 2 % width == g] for g in range(width)]
    return offsets[: width // 2], offsets[width // 2 :]


def horner(coefs, z):
    total = coefs[-1]
    for c in coefs[-2::-1]:
        total = total * z + c
    return total


def halves(value):
    high = value.astype(bf16)
    return high, (value - high.astype(f32)).astype(bf16)


def dot(left, right, left_dim=1, right_dim=0):
    return lax.dot_general(left, right, (((left_dim,), (right_dim,)), ((), ())), preferred_element_type=f32)


def table_blocks(order, slab, k_cols, positions, rows_ref, cot_ref, table_ref, part_ref):
    share = table_ref.shape[0] // (2 * len(order))
    channels = rows_ref.shape[1]
    for place, offset in enumerate(order):
        start = pl.multiple_of((slab ^ offset) * share, 8)
        turns = dot(k_cols[pl.ds(start, share), :].astype(bf16), positions)
        r = turns - jnp.floor(turns + 0.5)
        z = r * r
        s = r * horner(sin_coefs, z)
        c = horner(cos_coefs, z)
        table = jnp.concatenate([1.0 - 2.0 * s * s, 2.0 * s * c], axis=0).astype(bf16)
        at = pl.ds(place * 2 * share, 2 * share)
        table_ref[at, :] = table
        part_ref[at, :channels] = dot(table, rows_ref[...]).astype(part_ref.dtype)
        part_ref[at, channels:] = dot(table, cot_ref[...]).astype(part_ref.dtype)


def first_kernel(order, fetched, slab_ref, kv_hbm, pos_hbm, rows_hbm, cot_hbm, filter_hbm, *refs):
    sources, refs = refs[:fetched], refs[fetched:]
    table_ref, part_ref, k_cols, positions, rows_ref, cot_ref, filter_ref, *refs = refs
    copies_to, (kv_ref, pos_ref, k_rows, p_rows, sems) = refs[:fetched], refs[fetched:]
    slab = slab_ref[0]
    share = filter_ref.shape[0]
    filter_rows = pl.ds(pl.multiple_of(slab * share, 8), share)
    pairs = [
        (kv_hbm, kv_ref),
        (pos_hbm.at[:, 0], pos_ref),
        (rows_hbm.at[0], rows_ref),
        (cot_hbm.at[0], cot_ref),
        (filter_hbm.at[filter_rows, :], filter_ref),
        *zip(sources, copies_to),
    ]
    copies = [pltpu.make_async_copy(source, target, sems.at[i]) for i, (source, target) in enumerate(pairs)]
    for copy in copies:
        copy.start()
    k_rows[...] = jnp.zeros_like(k_rows)
    p_rows[...] = jnp.zeros_like(p_rows)
    copies[0].wait()
    copies[1].wait()
    pos = pos_ref[...]
    high = pos.astype(bf16).astype(f32)
    middle = (pos - high).astype(bf16).astype(f32)
    kv = kv_ref[...].astype(f32)
    for i, piece in enumerate((high, middle, pos - high - middle)):
        k_rows[3 * i : 3 * i + 3, :] = kv
        p_rows[3 * i : 3 * i + 3, :] = piece
    k_cols[...] = k_rows[...].T
    positions[...] = p_rows[...].astype(bf16)
    copies[2].wait()
    copies[3].wait()
    table_blocks(order, slab, k_cols, positions[...], rows_ref, cot_ref, table_ref, part_ref)
    for copy in copies[4:]:
        copy.wait()


def first_tables(order, slab, k_vectors, frac_pos, features, cotangent, k_filter, others, share):
    _, atoms, channels = features.shape
    kcount = k_vectors.shape[1]
    height = 2 * share * len(order)
    operands = (k_vectors, frac_pos.transpose(1, 0, 2), features, cotangent, k_filter, *others)
    shapes = [
        ((height, atoms), bf16),
        ((height, 2 * channels), bf16),
        ((kcount, 16), f32),
        ((16, atoms), bf16),
        ((atoms, channels), bf16),
        ((atoms, channels), bf16),
        ((share, channels), f32),
    ] + [(other.shape, other.dtype) for other in others]
    return pl.pallas_call(
        functools.partial(first_kernel, order, len(others)),
        name="first",
        out_shape=tuple(jax.ShapeDtypeStruct(shape, dtype) for shape, dtype in shapes),
        in_specs=[SMEM] + [HBM] * (5 + len(others)),
        out_specs=(VMEM,) * len(shapes),
        scratch_shapes=[
            pltpu.VMEM((3, kcount), jnp.int32),
            pltpu.VMEM((3, atoms), f32),
            pltpu.VMEM((16, kcount), f32),
            pltpu.VMEM((16, atoms), f32),
            pltpu.SemaphoreType.DMA((5 + len(others),)),
        ],
        compiler_params=params(),
        cost_estimate=pl.CostEstimate(
            flops=4 * height * atoms * channels, bytes_accessed=4 * height * atoms, transcendentals=0
        ),
    )(slab, *(pltpu.with_memory_space_constraint(value, pltpu.HBM) for value in operands))


def second_kernel(order, slab_ref, k_cols, positions, rows_ref, cot_ref, table_ref, part_ref):
    table_blocks(order, slab_ref[0], k_cols, positions[...], rows_ref, cot_ref, table_ref, part_ref)


def next_tables(dtype, order, slab, k_cols, positions, rows, cotan, share):
    atoms, channels = rows.shape
    height = 2 * share * len(order)
    return pl.pallas_call(
        functools.partial(second_kernel, order),
        out_shape=(
            jax.ShapeDtypeStruct((height, atoms), bf16),
            jax.ShapeDtypeStruct((height, 2 * channels), dtype),
        ),
        in_specs=[SMEM] + [VMEM] * 4,
        out_specs=(VMEM, VMEM),
        compiler_params=params(),
        cost_estimate=pl.CostEstimate(
            flops=4 * height * atoms * channels, bytes_accessed=4 * height * atoms, transcendentals=0
        ),
    )(slab, k_cols, positions, rows, cotan)


def one_hot(row_count, indices):
    rows = lax.broadcasted_iota(jnp.int32, (row_count, indices.shape[1]), 0)
    return (rows == indices).astype(f32).astype(bf16)


def rims_kernel(rows_ref, lists_ref, rows_t_ref, prev_ref, next_ref):
    atoms = rows_ref.shape[0]
    lists = lists_ref[0]
    rows_t = rows_ref[...].T
    rows_t_ref[...] = rows_t
    prev_ref[...] = dot(rows_t, one_hot(atoms, lists[0:1, :])).astype(bf16)
    next_ref[...] = dot(rows_t, one_hot(atoms, lists[1:2, :])).astype(bf16)


def rim_features(rows, lists):
    atoms, channels = rows.shape
    rim = lists.shape[2]
    return pl.pallas_call(
        rims_kernel,
        name="rims",
        out_shape=(
            jax.ShapeDtypeStruct((channels, atoms), bf16),
            jax.ShapeDtypeStruct((channels, rim), bf16),
            jax.ShapeDtypeStruct((channels, rim), bf16),
        ),
        in_specs=[VMEM] * 2,
        out_specs=(VMEM,) * 3,
        compiler_params=params(),
        cost_estimate=pl.CostEstimate(
            flops=4 * atoms * channels * rim, bytes_accessed=4 * atoms * channels, transcendentals=0
        ),
    )(rows, lists)


def edge_kernel(block, src_ref, dst_ref, dist_ref, cot_ref, rows_t_ref, own_ref, low_ref, up_ref, grad_ref, total):
    atoms, _ = cot_ref.shape
    rim = low_ref.shape[0]
    edges = src_ref.shape[1]
    cot_t = cot_ref[...].T
    for start in range(0, edges, block):
        at = slice(start, start + block)
        weight = jnp.maximum(1.0 - dist_ref[:, at] / cutoff_radius, 0.0)
        weight = weight * weight
        taken = dot(cot_t, one_hot(atoms, dst_ref[:, at]))
        weighted = (taken * weight).astype(bf16)
        part = dot(one_hot(total.shape[0], src_ref[:, at]), weighted, 1, 1)
        total[...] = part if start == 0 else total[...] + part
    own = total[:atoms, :]
    own_ref[...] = own
    low_ref[...] = total[atoms : atoms + rim, :].astype(bf16)
    up_ref[...] = total[atoms + rim :, :].astype(bf16)
    high, low = halves(own)
    grad_ref[...] = dot(rows_t_ref[...], high) + dot(rows_t_ref[...], low)


def edge_rows(sources, targets, lengths, cotan, rows_t, rim):
    atoms, channels = cotan.shape
    edges = sources.shape[1]
    rows = atoms + 2 * rim
    block = math.gcd(edges, 512)
    return pl.pallas_call(
        functools.partial(edge_kernel, block),
        name="edges",
        out_shape=(
            jax.ShapeDtypeStruct((atoms, channels), f32),
            jax.ShapeDtypeStruct((rim, channels), bf16),
            jax.ShapeDtypeStruct((rim, channels), bf16),
            jax.ShapeDtypeStruct((channels, channels), f32),
        ),
        in_specs=[VMEM] * 5,
        out_specs=(VMEM,) * 4,
        scratch_shapes=[pltpu.VMEM((rows, channels), f32)],
        compiler_params=params(),
        cost_estimate=pl.CostEstimate(
            flops=2 * edges * (rows + atoms) * channels, bytes_accessed=edges * 12, transcendentals=0
        ),
    )(sources, targets, lengths, cotan, rows_t)


def split_blocks(order, slab, values, send_ref, keep_ref, blocks):
    count, height, _ = blocks.shape
    height = height // len(values)
    for i in range(count):
        for j, value in enumerate(values):
            blocks[i, j * height : (j + 1) * height] = value[i * height : (i + 1) * height, :]
    for place, offset in enumerate(order):
        keep_ref[place] = blocks[slab ^ offset]
        send_ref[place] = blocks[slab ^ offset ^ 1]


def short_kernel(own_ref, above_ref, below_ref, lists_ref, cot_ref, w_ref, base_ref):
    atoms = own_ref.shape[0]
    lists = lists_ref[0]
    owned = own_ref[...] + dot(one_hot(atoms, lists[1:2, :]), above_ref[...])
    owned = owned + dot(one_hot(atoms, lists[0:1, :]), below_ref[...])
    high, low = halves(owned)
    w = w_ref[...]
    base_ref[...] = cot_ref[...].astype(f32) + (dot(high, w, 1, 1) + dot(low, w, 1, 1))


def short_range(own, above, below, lists, cotan, w_short):
    atoms, channels = cotan.shape
    return pl.pallas_call(
        short_kernel,
        name="short",
        out_shape=jax.ShapeDtypeStruct((atoms, channels), f32),
        in_specs=[VMEM] * 6,
        out_specs=VMEM,
        compiler_params=params(),
        cost_estimate=pl.CostEstimate(
            flops=8 * atoms * channels * channels, bytes_accessed=8 * atoms * channels, transcendentals=0
        ),
    )(own, above, below, lists, cotan, w_short)


def share_kernel(
    order, norm, count, slab_ref, filter_ref, w_ref, grad_ref, lower_t, upper_t, low_ref, up_ref, *refs
):
    parts, (adj_ref, gfilter_ref, send_ref, keep_ref, blocks) = refs[:count], refs[count:]
    channels = w_ref.shape[0]
    total = parts[0][...].astype(f32)
    for part in parts[1:]:
        total = total + part[...].astype(f32)
    structure = total[:, :channels]
    moved, moved_low = halves(total[:, channels:])
    response = dot(moved, w_ref[...], 1, 1) + dot(moved_low, w_ref[...], 1, 1)
    k_filter = filter_ref[...]
    double = jnp.concatenate([k_filter, k_filter], axis=0) * norm
    filtered, filtered_low = halves((structure * double).T)
    wout = dot(filtered, moved) + (dot(filtered, moved_low) + dot(filtered_low, moved))
    wshort = grad_ref[...] + (dot(lower_t[...], low_ref[...]) + dot(upper_t[...], up_ref[...]))
    split_blocks(order, slab_ref[0], (wout, wshort), send_ref, keep_ref, blocks)
    adj_ref[...] = (response * double).T.astype(bf16)
    product = structure * response
    share = k_filter.shape[0]
    gfilter_ref[...] = norm * (product[:share] + product[share:])


def own_share(order, norm, slab, k_filter, w_out, short_terms, parts):
    height, channels = parts[0].shape[0], w_out.shape[0]
    half = len(order)
    rows = 2 * channels // (2 * half)
    return pl.pallas_call(
        functools.partial(share_kernel, order, norm, len(parts)),
        name="share",
        out_shape=(
            jax.ShapeDtypeStruct((channels, height), bf16),
            jax.ShapeDtypeStruct((height // 2, channels), f32),
            jax.ShapeDtypeStruct((half, rows, channels), f32),
            jax.ShapeDtypeStruct((half, rows, channels), f32),
        ),
        in_specs=[SMEM] + [VMEM] * (2 + len(short_terms) + len(parts)),
        out_specs=(VMEM,) * 4,
        scratch_shapes=[pltpu.VMEM((2 * half, rows, channels), f32)],
        compiler_params=params(),
        cost_estimate=pl.CostEstimate(
            flops=8 * height * channels * channels, bytes_accessed=16 * height * channels, transcendentals=0
        ),
    )(slab, k_filter, w_out, *short_terms, *parts)


def back_kernel(orders, order, base_ref, even_adj_ref, odd_adj_ref, *refs):
    table_refs, out_ref = refs[:-1], refs[-1]
    width = even_adj_ref.shape[2]
    total = None
    for offsets, table_ref in zip(orders, table_refs):
        for place, offset in enumerate(offsets):
            adj = (odd_adj_ref if offset & 1 else even_adj_ref)[order.index(offset & ~1)]
            part = dot(adj, table_ref[place * width : (place + 1) * width, :])
            total = part if total is None else total + part
    out_ref[...] = (base_ref[...] + total.T).astype(bf16)


def back_project(orders, order, base, even_adj, odd_adj, tables):
    atoms, channels = base.shape
    height = sum(table.shape[0] for table in tables)
    return pl.pallas_call(
        functools.partial(back_kernel, orders, order),
        name="back",
        out_shape=jax.ShapeDtypeStruct((atoms, channels), bf16),
        in_specs=[VMEM] * (3 + len(tables)),
        out_specs=VMEM,
        compiler_params=params(),
        cost_estimate=pl.CostEstimate(
            flops=2 * height * atoms * channels, bytes_accessed=2 * height * atoms, transcendentals=0
        ),
    )(base, even_adj, odd_adj, *tables)


def place_kernel(order, scale, slab_ref, even_ref, odd_ref, wout_ref, wshort_ref, blocks):
    count, height, _ = blocks.shape
    half = height // 2
    slab = slab_ref[0]
    for place, offset in enumerate(order):
        blocks[slab ^ offset] = even_ref[place].astype(f32) * scale
        blocks[slab ^ offset ^ 1] = odd_ref[place].astype(f32) * scale
    for i in range(count):
        wout_ref[i * half : (i + 1) * half, :] = blocks[i, :half, :]
        wshort_ref[i * half : (i + 1) * half, :] = blocks[i, half:, :]


def place_grads(order, scale, slab, even, odd):
    half, height, channels = even.shape
    return pl.pallas_call(
        functools.partial(place_kernel, order, scale),
        name="place",
        out_shape=(jax.ShapeDtypeStruct((channels, channels), f32),) * 2,
        in_specs=[SMEM, VMEM, VMEM],
        out_specs=(VMEM, VMEM),
        scratch_shapes=[pltpu.VMEM((2 * half, height, channels), f32)],
        compiler_params=params(),
    )(slab, even, odd)


def doubling_gather(blocks):
    count = lax.axis_size("slab")
    bit = count // 2
    while bit > 1:
        moved = xor_permute(blocks, "slab", bit)
        blocks = jnp.concatenate([blocks, moved], axis=0)
        bit = bit // 2
    return blocks


def sum_replicas(value):
    bit = 1
    while bit < lax.axis_size("rep"):
        sent = value.astype(bf16)
        moved = xor_permute(sent, "rep", bit)
        value = sent.astype(f32) + moved.astype(f32)
        bit = 2 * bit
    return value


def plane_gather(block, order):
    count = lax.axis_size("slab")
    planes, bit = [], 2
    while bit < count:
        planes.append((bit, min(4, count // bit)))
        bit *= planes[-1][1]
    held = {0: block}
    for bit, width in reversed(planes):
        offsets = sorted(held)
        payload = held[0] if len(held) == 1 else jnp.stack([held[offset] for offset in offsets])
        for g in range(width - 1, 0, -1):
            moved = xor_permute(payload, "slab", g * bit)
            for i, offset in enumerate(offsets):
                held[offset ^ g * bit] = moved if len(offsets) == 1 else moved[i]
    return jnp.stack([held[offset] for offset in order])


def plane_sum(blocks):
    count = lax.axis_size("slab")
    bit = 2
    terms = None
    while bit < count:
        width = min(4, count // bit)
        sent = {g: [] for g in range(width)}
        for offset in sorted(blocks):
            sent[offset // bit % width].append(offset)
        received = {offset: [] for offset in sent[0]}
        for g in range(width - 1, 0, -1):
            pieces = [blocks[offset].astype(bf16) for offset in sent[g]]
            payload = pieces[0] if len(pieces) == 1 else jnp.concatenate(pieces, axis=0)
            moved = xor_permute(payload, "slab", g * bit)
            height = moved.shape[0] // len(pieces)
            for i, offset in enumerate(sent[0]):
                received[offset].append(moved[i * height : (i + 1) * height])
        terms = [blocks[0], *received[0]]
        blocks = {
            offset: sum((piece.astype(f32) for piece in received[offset]), blocks[offset].astype(f32))
            for offset in sent[0]
        }
        bit = bit * width
    return terms


def block(
    features,
    cotangent,
    frac_pos,
    k_vectors,
    k_filter,
    w_out,
    w_short,
    edge_src,
    edge_dst,
    distance,
    halo_idx,
):
    _, atoms, _ = features.shape
    kcount = k_filter.shape[0]
    count = lax.axis_size("slab")
    replicas = lax.axis_size("rep")
    norm = 1.0 / math.sqrt(kcount * atoms * count)
    scale = 1.0 / math.sqrt(replicas * atoms * count)
    share = kcount // count
    slab = lax.axis_index("slab").astype(jnp.int32)[None]

    near, far = plane_order(count)
    near, far = (tuple(offset for group in groups for offset in group) for groups in (near, far))
    flip = lambda offsets: tuple(offset ^ 1 for offset in offsets)
    orders = (flip(far), far, flip(near), near)
    order = halving_order(count)

    odda, odda_part, k_cols, positions, rows, cotan, own_filter, src, dst, dist, lists, w_out, w_short = first_tables(
        orders[0],
        slab,
        k_vectors,
        frac_pos,
        features,
        cotangent,
        k_filter,
        (edge_src, edge_dst, distance, halo_idx, w_out, w_short),
        share,
    )
    moveda = xor_permute(odda_part, "slab", 1)
    operands = (slab, k_cols, positions, rows, cotan, share)
    evena, evena_part = next_tables(f32, orders[1], *operands)
    oddb, oddb_part = next_tables(bf16, orders[2], *operands)
    movedb = xor_permute(oddb_part, "slab", 1)
    evenb, evenb_part = next_tables(f32, orders[3], *operands)
    blocks = {}
    for offsets, part, moved in ((far, evena_part, moveda), (near, evenb_part, movedb)):
        paired = part + moved.astype(f32)
        for i, offset in enumerate(offsets):
            blocks[offset] = paired[i * 2 * share : (i + 1) * 2 * share]
    parts = plane_sum(blocks)

    rows_t, to_prev, to_next = rim_features(rows, lists)
    lower_t = shifted(to_next, "slab", 1)
    upper_t = shifted(to_prev, "slab", -1)
    own_rows, low, up, wshort = edge_rows(src, dst, dist, cotan, rows_t, lists.shape[2])
    short_terms = (wshort, lower_t, upper_t, low, up)
    adj, gfilter, send, keep = own_share(order, norm, slab, own_filter, w_out, short_terms, parts)
    grads = keep + xor_permute(send, "slab", 1)

    from_above = shifted(low, "slab", -1)
    from_below = shifted(up, "slab", 1)
    base = short_range(own_rows, from_above, from_below, lists, cotan, w_short)

    terms = plane_sum({offset: grads[i] for i, offset in enumerate(order)})
    own_grad = sum((term.astype(f32) for term in terms[1:]), terms[0])

    adj_even = doubling_gather(adj[None])
    adj_odd = xor_permute(adj_even, "slab", 1)
    grad_features = back_project(orders, order, base, adj_even, adj_odd, (odda, evena, oddb, evenb))

    own_grad = sum_replicas(own_grad).astype(bf16)
    filter_sum = sum_replicas(gfilter)
    grad_filter = filter_sum / replicas
    grad_even = plane_gather(own_grad, order)
    grad_odd = xor_permute(grad_even, "slab", 1)
    grad_wout, grad_wshort = place_grads(order, scale, slab, grad_even, grad_odd)
    return (grad_features[None], grad_wout, grad_wshort, grad_filter)


def solution(mesh):
    return jax.shard_map(
        block,
        mesh=mesh,
        in_specs=(
            P("rep", "slab", None),
            P("rep", "slab", None),
            P("rep", None, "slab"),
            P(),
            P(),
            P(),
            P(),
            P("rep", "slab"),
            P("rep", "slab"),
            P("rep", "slab"),
            P("rep", "slab", None),
        ),
        out_specs=(P("rep", "slab", None), P(), P(), P("slab", None)),
        check_vma=False,
    )
```

```python
import functools
import math

import jax
import jax.numpy as jnp
from jax import lax
from jax.experimental import pallas as pl
from jax.experimental.pallas import tpu as pltpu
from jax.sharding import PartitionSpec as P


cutoff_radius = 5.0
f32, bf16 = jnp.float32, jnp.bfloat16

sin_coefs = (3.1415926401307073, -5.167710083507895, 2.550077523214559, -0.5982912856198396, 0.0776576603038396)
cos_coefs = (0.9999999532476077, -4.934792830619641, 4.058411352862562, -1.331876568080612, 0.21968961109715823)

VMEM = pl.BlockSpec(memory_space=pltpu.VMEM)
SMEM = pl.BlockSpec(memory_space=pltpu.SMEM)
HBM = pl.BlockSpec(memory_space=pltpu.HBM)


def params():
    return pltpu.CompilerParams(vmem_limit_bytes=48 * 1024 * 1024)


def xor_permute(value, axis, bits):
    count = lax.axis_size(axis)
    return lax.ppermute(value, axis, [(source, source ^ bits) for source in range(count)])


def shifted(value, axis, steps):
    count = lax.axis_size(axis)
    return lax.ppermute(value, axis, [(source, (source + steps) % count) for source in range(count)])


def halving_order(count):
    order, bit = [0], count // 2
    while bit > 1:
        order = order + [offset | bit for offset in order]
        bit //= 2
    return tuple(order)


def plane_order(count):
    width = min(4, count // 2)
    offsets = [[offset for offset in range(0, count, 2) if offset // 2 % width == g] for g in range(width)]
    return offsets[: width // 2], offsets[width // 2 :]


def horner(coefs, z):
    total = coefs[-1]
    for c in coefs[-2::-1]:
        total = total * z + c
    return total


def halves(value):
    high = value.astype(bf16)
    return high, (value - high.astype(f32)).astype(bf16)


def dot(left, right, left_dim=1, right_dim=0):
    return lax.dot_general(left, right, (((left_dim,), (right_dim,)), ((), ())), preferred_element_type=f32)


def table_blocks(order, slab, k_cols, positions, rows_ref, cot_ref, table_ref, part_ref):
    share = table_ref.shape[0] // (2 * len(order))
    channels = rows_ref.shape[1]
    for place, offset in enumerate(order):
        start = pl.multiple_of((slab ^ offset) * share, 8)
        turns = dot(k_cols[pl.ds(start, share), :].astype(bf16), positions)
        r = turns - jnp.floor(turns + 0.5)
        z = r * r
        s = r * horner(sin_coefs, z)
        c = horner(cos_coefs, z)
        table = jnp.concatenate([1.0 - 2.0 * s * s, 2.0 * s * c], axis=0).astype(bf16)
        at = pl.ds(place * 2 * share, 2 * share)
        table_ref[at, :] = table
        part_ref[at, :channels] = dot(table, rows_ref[...]).astype(part_ref.dtype)
        part_ref[at, channels:] = dot(table, cot_ref[...]).astype(part_ref.dtype)


def first_kernel(order, fetched, slab_ref, kv_hbm, pos_hbm, rows_hbm, cot_hbm, filter_hbm, *refs):
    sources, refs = refs[:fetched], refs[fetched:]
    table_ref, part_ref, k_cols, positions, rows_ref, cot_ref, filter_ref, *refs = refs
    copies_to, (kv_ref, pos_ref, k_rows, p_rows, sems) = refs[:fetched], refs[fetched:]
    slab = slab_ref[0]
    share = filter_ref.shape[0]
    filter_rows = pl.ds(pl.multiple_of(slab * share, 8), share)
    pairs = [
        (kv_hbm, kv_ref),
        (pos_hbm.at[:, 0], pos_ref),
        (rows_hbm.at[0], rows_ref),
        (cot_hbm.at[0], cot_ref),
        (filter_hbm.at[filter_rows, :], filter_ref),
        *zip(sources, copies_to),
    ]
    copies = [pltpu.make_async_copy(source, target, sems.at[i]) for i, (source, target) in enumerate(pairs)]
    for copy in copies:
        copy.start()
    k_rows[...] = jnp.zeros_like(k_rows)
    p_rows[...] = jnp.zeros_like(p_rows)
    copies[0].wait()
    copies[1].wait()
    pos = pos_ref[...]
    high = pos.astype(bf16).astype(f32)
    middle = (pos - high).astype(bf16).astype(f32)
    kv = kv_ref[...].astype(f32)
    for i, piece in enumerate((high, middle, pos - high - middle)):
        k_rows[3 * i : 3 * i + 3, :] = kv
        p_rows[3 * i : 3 * i + 3, :] = piece
    k_cols[...] = k_rows[...].T
    positions[...] = p_rows[...].astype(bf16)
    copies[2].wait()
    copies[3].wait()
    table_blocks(order, slab, k_cols, positions[...], rows_ref, cot_ref, table_ref, part_ref)
    for copy in copies[4:]:
        copy.wait()


def first_tables(order, slab, k_vectors, frac_pos, features, cotangent, k_filter, others, share):
    _, atoms, channels = features.shape
    kcount = k_vectors.shape[1]
    height = 2 * share * len(order)
    operands = (k_vectors, frac_pos.transpose(1, 0, 2), features, cotangent, k_filter, *others)
    shapes = [
        ((height, atoms), bf16),
        ((height, 2 * channels), bf16),
        ((kcount, 16), f32),
        ((16, atoms), bf16),
        ((atoms, channels), bf16),
        ((atoms, channels), bf16),
        ((share, channels), f32),
    ] + [(other.shape, other.dtype) for other in others]
    return pl.pallas_call(
        functools.partial(first_kernel, order, len(others)),
        name="first",
        out_shape=tuple(jax.ShapeDtypeStruct(shape, dtype) for shape, dtype in shapes),
        in_specs=[SMEM] + [HBM] * (5 + len(others)),
        out_specs=(VMEM,) * len(shapes),
        scratch_shapes=[
            pltpu.VMEM((3, kcount), jnp.int32),
            pltpu.VMEM((3, atoms), f32),
            pltpu.VMEM((16, kcount), f32),
            pltpu.VMEM((16, atoms), f32),
            pltpu.SemaphoreType.DMA((5 + len(others),)),
        ],
        compiler_params=params(),
        cost_estimate=pl.CostEstimate(
            flops=4 * height * atoms * channels, bytes_accessed=4 * height * atoms, transcendentals=0
        ),
    )(slab, *(pltpu.with_memory_space_constraint(value, pltpu.HBM) for value in operands))


def second_kernel(order, slab_ref, k_cols, positions, rows_ref, cot_ref, table_ref, part_ref):
    table_blocks(order, slab_ref[0], k_cols, positions[...], rows_ref, cot_ref, table_ref, part_ref)


def next_tables(dtype, order, slab, k_cols, positions, rows, cotan, share):
    atoms, channels = rows.shape
    height = 2 * share * len(order)
    return pl.pallas_call(
        functools.partial(second_kernel, order),
        out_shape=(
            jax.ShapeDtypeStruct((height, atoms), bf16),
            jax.ShapeDtypeStruct((height, 2 * channels), dtype),
        ),
        in_specs=[SMEM] + [VMEM] * 4,
        out_specs=(VMEM, VMEM),
        compiler_params=params(),
        cost_estimate=pl.CostEstimate(
            flops=4 * height * atoms * channels, bytes_accessed=4 * height * atoms, transcendentals=0
        ),
    )(slab, k_cols, positions, rows, cotan)


def edge_kernel(block, src_ref, dst_ref, dist_ref, cot_ref, own_ref, low_ref, up_ref, total):
    atoms, _ = cot_ref.shape
    rim = low_ref.shape[0]
    edges = src_ref.shape[1]
    cot_t = cot_ref[...].T
    for start in range(0, edges, block):
        at = slice(start, start + block)
        source, target = src_ref[:, at], dst_ref[:, at]
        weight = jnp.maximum(1.0 - dist_ref[:, at] / cutoff_radius, 0.0)
        weight = weight * weight
        pick = lax.broadcasted_iota(jnp.int32, (atoms, block), 0) == target
        taken = dot(cot_t, pick.astype(f32).astype(bf16))
        weighted = (taken * weight).astype(bf16)
        put = lax.broadcasted_iota(jnp.int32, (total.shape[0], block), 0) == source
        part = dot(put.astype(f32).astype(bf16), weighted, 1, 1)
        total[...] = part if start == 0 else total[...] + part
    own_ref[...] = total[:atoms, :]
    low_ref[...] = total[atoms : atoms + rim, :].astype(bf16)
    up_ref[...] = total[atoms + rim :, :].astype(bf16)


def edge_rows(sources, targets, lengths, cotan, rim):
    atoms, channels = cotan.shape
    edges = sources.shape[1]
    rows = atoms + 2 * rim
    block = math.gcd(edges, 512)
    return pl.pallas_call(
        functools.partial(edge_kernel, block),
        name="edges",
        out_shape=(
            jax.ShapeDtypeStruct((atoms, channels), f32),
            jax.ShapeDtypeStruct((rim, channels), bf16),
            jax.ShapeDtypeStruct((rim, channels), bf16),
        ),
        in_specs=[VMEM] * 4,
        out_specs=(VMEM,) * 3,
        scratch_shapes=[pltpu.VMEM((rows, channels), f32)],
        compiler_params=params(),
        cost_estimate=pl.CostEstimate(
            flops=2 * edges * (rows + atoms) * channels, bytes_accessed=edges * 12, transcendentals=0
        ),
    )(sources, targets, lengths, cotan)


def split_blocks(order, slab, value, send_ref, keep_ref, blocks):
    count, height, _ = blocks.shape
    for i in range(count):
        blocks[i] = value[i * height : (i + 1) * height, :]
    for place, offset in enumerate(order):
        keep_ref[place] = blocks[slab ^ offset]
        send_ref[place] = blocks[slab ^ offset ^ 1]


def short_kernel(
    order, slab_ref, own_ref, above_ref, below_ref, lists_ref, rows_ref, cot_ref, w_ref, base_ref, send_ref, keep_ref, blocks
):
    atoms = own_ref.shape[0]
    lists = lists_ref[0]
    shape = (atoms, lists.shape[1])
    row_at = lax.broadcasted_iota(jnp.int32, shape, 0)
    to_lower = (row_at == lists[0:1, :]).astype(f32).astype(bf16)
    to_upper = (row_at == lists[1:2, :]).astype(f32).astype(bf16)
    owned = own_ref[...] + dot(to_upper, above_ref[...]) + dot(to_lower, below_ref[...])
    high, low = halves(owned)
    w = w_ref[...]
    base_ref[...] = cot_ref[...].astype(f32) + (dot(high, w, 1, 1) + dot(low, w, 1, 1))
    rows = rows_ref[...].T
    split_blocks(order, slab_ref[0], dot(rows, high) + dot(rows, low), send_ref, keep_ref, blocks)


def short_range(order, slab, own, above, below, lists, rows, cotan, w_short):
    atoms, channels = rows.shape
    half = len(order)
    height = channels // (2 * half)
    return pl.pallas_call(
        functools.partial(short_kernel, order),
        name="short",
        out_shape=(
            jax.ShapeDtypeStruct((atoms, channels), f32),
            jax.ShapeDtypeStruct((half, height, channels), f32),
            jax.ShapeDtypeStruct((half, height, channels), f32),
        ),
        in_specs=[SMEM] + [VMEM] * 7,
        out_specs=(VMEM,) * 3,
        scratch_shapes=[pltpu.VMEM((2 * half, height, channels), f32)],
        compiler_params=params(),
        cost_estimate=pl.CostEstimate(
            flops=8 * atoms * channels * channels, bytes_accessed=8 * atoms * channels, transcendentals=0
        ),
    )(slab, own, above, below, lists, rows, cotan, w_short)


def share_kernel(order, norm, count, slab_ref, filter_ref, w_ref, *refs):
    parts, (adj_ref, gfilter_ref, send_ref, keep_ref, blocks) = refs[:count], refs[count:]
    channels = w_ref.shape[0]
    total = parts[0][...].astype(f32)
    for part in parts[1:]:
        total = total + part[...].astype(f32)
    structure = total[:, :channels]
    moved, moved_low = halves(total[:, channels:])
    response = dot(moved, w_ref[...], 1, 1) + dot(moved_low, w_ref[...], 1, 1)
    k_filter = filter_ref[...]
    double = jnp.concatenate([k_filter, k_filter], axis=0) * norm
    filtered, filtered_low = halves((structure * double).T)
    wout = dot(filtered, moved) + (dot(filtered, moved_low) + dot(filtered_low, moved))
    split_blocks(order, slab_ref[0], wout, send_ref, keep_ref, blocks)
    adj_ref[...] = (response * double).T.astype(bf16)
    product = structure * response
    share = k_filter.shape[0]
    gfilter_ref[...] = norm * (product[:share] + product[share:])


def own_share(order, norm, slab, k_filter, w_out, parts):
    height, channels = parts[0].shape[0], w_out.shape[0]
    half = len(order)
    rows = channels // (2 * half)
    return pl.pallas_call(
        functools.partial(share_kernel, order, norm, len(parts)),
        name="share",
        out_shape=(
            jax.ShapeDtypeStruct((channels, height), bf16),
            jax.ShapeDtypeStruct((height // 2, channels), f32),
            jax.ShapeDtypeStruct((half, rows, channels), f32),
            jax.ShapeDtypeStruct((half, rows, channels), f32),
        ),
        in_specs=[SMEM] + [VMEM] * (2 + len(parts)),
        out_specs=(VMEM,) * 4,
        scratch_shapes=[pltpu.VMEM((2 * half, rows, channels), f32)],
        compiler_params=params(),
        cost_estimate=pl.CostEstimate(
            flops=8 * height * channels * channels, bytes_accessed=16 * height * channels, transcendentals=0
        ),
    )(slab, k_filter, w_out, *parts)


def back_kernel(orders, order, base_ref, even_adj_ref, odd_adj_ref, *refs):
    table_refs, out_ref = refs[:-1], refs[-1]
    width = even_adj_ref.shape[2]
    total = None
    for offsets, table_ref in zip(orders, table_refs):
        for place, offset in enumerate(offsets):
            adj = (odd_adj_ref if offset & 1 else even_adj_ref)[order.index(offset & ~1)]
            part = dot(adj, table_ref[place * width : (place + 1) * width, :])
            total = part if total is None else total + part
    out_ref[...] = (base_ref[...] + total.T).astype(bf16)


def back_project(orders, order, base, even_adj, odd_adj, tables):
    atoms, channels = base.shape
    height = sum(table.shape[0] for table in tables)
    return pl.pallas_call(
        functools.partial(back_kernel, orders, order),
        name="back",
        out_shape=jax.ShapeDtypeStruct((atoms, channels), bf16),
        in_specs=[VMEM] * (3 + len(tables)),
        out_specs=VMEM,
        compiler_params=params(),
        cost_estimate=pl.CostEstimate(
            flops=2 * height * atoms * channels, bytes_accessed=2 * height * atoms, transcendentals=0
        ),
    )(base, even_adj, odd_adj, *tables)


def place_kernel(order, scale, slab_ref, even_ref, odd_ref, wout_ref, wshort_ref, blocks):
    count, height, _ = blocks.shape
    half = height // 2
    slab = slab_ref[0]
    for place, offset in enumerate(order):
        blocks[slab ^ offset] = even_ref[place].astype(f32) * scale
        blocks[slab ^ offset ^ 1] = odd_ref[place].astype(f32) * scale
    for i in range(count):
        wout_ref[i * half : (i + 1) * half, :] = blocks[i, :half, :]
        wshort_ref[i * half : (i + 1) * half, :] = blocks[i, half:, :]


def place_grads(order, scale, slab, even, odd):
    half, height, channels = even.shape
    return pl.pallas_call(
        functools.partial(place_kernel, order, scale),
        name="place",
        out_shape=(jax.ShapeDtypeStruct((channels, channels), f32),) * 2,
        in_specs=[SMEM, VMEM, VMEM],
        out_specs=(VMEM, VMEM),
        scratch_shapes=[pltpu.VMEM((2 * half, height, channels), f32)],
        compiler_params=params(),
    )(slab, even, odd)


def doubling_gather(blocks):
    count = lax.axis_size("slab")
    bit = count // 2
    while bit > 1:
        moved = xor_permute(blocks, "slab", bit)
        blocks = jnp.concatenate([blocks, moved], axis=0)
        bit = bit // 2
    return blocks


def sum_replicas(value):
    bit = 1
    while bit < lax.axis_size("rep"):
        sent = value.astype(bf16)
        moved = xor_permute(sent, "rep", bit)
        value = sent.astype(f32) + moved.astype(f32)
        bit = 2 * bit
    return value


def sum_replicas_direct(value):
    count = lax.axis_size("rep")
    terms = [value.astype(bf16)]
    for offset in range(count - 1, 0, -1):
        terms.insert(1, xor_permute(terms[0], "rep", offset))
    terms = [term.astype(f32) for term in terms]
    while len(terms) > 1:
        terms = [terms[i] + terms[i + 1] for i in range(0, len(terms), 2)]
    return terms[0]


def plane_gather(block, order):
    count = lax.axis_size("slab")
    planes, bit = [], 2
    while bit < count:
        planes.append((bit, min(4, count // bit)))
        bit *= planes[-1][1]
    held = {0: block}
    for bit, width in reversed(planes):
        offsets = sorted(held)
        payload = held[0] if len(held) == 1 else jnp.stack([held[offset] for offset in offsets])
        for g in range(width - 1, 0, -1):
            moved = xor_permute(payload, "slab", g * bit)
            for i, offset in enumerate(offsets):
                held[offset ^ g * bit] = moved if len(offsets) == 1 else moved[i]
    return jnp.stack([held[offset] for offset in order])


def plane_sum(blocks):
    count = lax.axis_size("slab")
    bit = 2
    terms = None
    while bit < count:
        width = min(4, count // bit)
        sent = {g: [] for g in range(width)}
        for offset in sorted(blocks):
            sent[offset // bit % width].append(offset)
        received = {offset: [] for offset in sent[0]}
        for g in range(width - 1, 0, -1):
            pieces = [blocks[offset].astype(bf16) for offset in sent[g]]
            payload = pieces[0] if len(pieces) == 1 else jnp.concatenate(pieces, axis=0)
            moved = xor_permute(payload, "slab", g * bit)
            height = moved.shape[0] // len(pieces)
            for i, offset in enumerate(sent[0]):
                received[offset].append(moved[i * height : (i + 1) * height])
        terms = [blocks[0], *received[0]]
        blocks = {
            offset: sum((piece.astype(f32) for piece in received[offset]), blocks[offset].astype(f32))
            for offset in sent[0]
        }
        bit = bit * width
    return terms


def block(
    features,
    cotangent,
    frac_pos,
    k_vectors,
    k_filter,
    w_out,
    w_short,
    edge_src,
    edge_dst,
    distance,
    halo_idx,
):
    _, atoms, _ = features.shape
    kcount = k_filter.shape[0]
    count = lax.axis_size("slab")
    replicas = lax.axis_size("rep")
    norm = 1.0 / math.sqrt(kcount * atoms * count)
    scale = 1.0 / math.sqrt(replicas * atoms * count)
    share = kcount // count
    slab = lax.axis_index("slab").astype(jnp.int32)[None]

    near, far = plane_order(count)
    near, far = (tuple(offset for group in groups for offset in group) for groups in (near, far))
    flip = lambda offsets: tuple(offset ^ 1 for offset in offsets)
    orders = (flip(far), far, flip(near), near)
    order = halving_order(count)

    odda, odda_part, k_cols, positions, rows, cotan, own_filter, src, dst, dist, lists, w_out, w_short = first_tables(
        orders[0],
        slab,
        k_vectors,
        frac_pos,
        features,
        cotangent,
        k_filter,
        (edge_src, edge_dst, distance, halo_idx, w_out, w_short),
        share,
    )
    moveda = xor_permute(odda_part, "slab", 1)
    operands = (slab, k_cols, positions, rows, cotan, share)
    evena, evena_part = next_tables(f32, orders[1], *operands)
    oddb, oddb_part = next_tables(bf16, orders[2], *operands)
    movedb = xor_permute(oddb_part, "slab", 1)
    evenb, evenb_part = next_tables(f32, orders[3], *operands)
    blocks = {}
    for offsets, part, moved in ((far, evena_part, moveda), (near, evenb_part, movedb)):
        paired = part + moved.astype(f32)
        for i, offset in enumerate(offsets):
            blocks[offset] = paired[i * 2 * share : (i + 1) * 2 * share]
    parts = plane_sum(blocks)

    own_rows, lower, upper = edge_rows(src, dst, dist, cotan, lists.shape[2])
    from_above = shifted(lower, "slab", -1)
    from_below = shifted(upper, "slab", 1)
    adj, gfilter, wout_send, wout_keep = own_share(order, norm, slab, own_filter, w_out, parts)
    wout_moved = xor_permute(wout_send, "slab", 1)
    base, wshort_send, wshort_keep = short_range(
        order, slab, own_rows, from_above, from_below, lists, rows, cotan, w_short
    )
    wshort_moved = xor_permute(wshort_send, "slab", 1)
    grads = jnp.concatenate([wout_keep + wout_moved, wshort_keep + wshort_moved], axis=1)
    terms = plane_sum({offset: grads[i] for i, offset in enumerate(order)})
    own_grad = sum((term.astype(f32) for term in terms[1:]), terms[0])

    adj_even = doubling_gather(adj[None])
    adj_odd = xor_permute(adj_even, "slab", 1)
    grad_features = back_project(orders, order, base, adj_even, adj_odd, (odda, evena, oddb, evenb))

    own_grad = sum_replicas_direct(own_grad).astype(bf16)
    filter_sum = sum_replicas(gfilter)
    grad_filter = filter_sum / replicas
    grad_even = plane_gather(own_grad, order)
    grad_odd = xor_permute(grad_even, "slab", 1)
    grad_wout, grad_wshort = place_grads(order, scale, slab, grad_even, grad_odd)
    return (grad_features[None], grad_wout, grad_wshort, grad_filter)


def solution(mesh):
    return jax.shard_map(
        block,
        mesh=mesh,
        in_specs=(
            P("rep", "slab", None),
            P("rep", "slab", None),
            P("rep", None, "slab"),
            P(),
            P(),
            P(),
            P(),
            P("rep", "slab"),
            P("rep", "slab"),
            P("rep", "slab"),
            P("rep", "slab", None),
        ),
        out_specs=(P("rep", "slab", None), P(), P(), P("slab", None)),
        check_vma=False,
    )
```

```python
import functools
import math

import jax
import jax.numpy as jnp
from jax import lax
from jax.experimental import pallas as pl
from jax.experimental.pallas import tpu as pltpu
from jax.sharding import PartitionSpec as P


cutoff_radius = 5.0
f32, bf16 = jnp.float32, jnp.bfloat16

sin_coefs = (3.1415926401307073, -5.167710083507895, 2.550077523214559, -0.5982912856198396, 0.0776576603038396)
cos_coefs = (0.9999999532476077, -4.934792830619641, 4.058411352862562, -1.331876568080612, 0.21968961109715823)

VMEM = pl.BlockSpec(memory_space=pltpu.VMEM)
SMEM = pl.BlockSpec(memory_space=pltpu.SMEM)
HBM = pl.BlockSpec(memory_space=pltpu.HBM)


def params():
    return pltpu.CompilerParams(vmem_limit_bytes=48 * 1024 * 1024)


def xor_permute(value, axis, bits):
    count = lax.axis_size(axis)
    return lax.ppermute(value, axis, [(source, source ^ bits) for source in range(count)])


def shifted(value, axis, steps):
    count = lax.axis_size(axis)
    return lax.ppermute(value, axis, [(source, (source + steps) % count) for source in range(count)])


def halving_order(count):
    order, bit = [0], count // 2
    while bit > 1:
        order = order + [offset | bit for offset in order]
        bit //= 2
    return tuple(order)


def plane_order(count):
    width = min(4, count // 2)
    offsets = [[offset for offset in range(0, count, 2) if offset // 2 % width == g] for g in range(width)]
    return offsets[:-1], offsets[-1:]


def horner(coefs, z):
    total = coefs[-1]
    for c in coefs[-2::-1]:
        total = total * z + c
    return total


def halves(value):
    high = value.astype(bf16)
    return high, (value - high.astype(f32)).astype(bf16)


def dot(left, right, left_dim=1, right_dim=0):
    return lax.dot_general(left, right, (((left_dim,), (right_dim,)), ((), ())), preferred_element_type=f32)


def table_blocks(order, slab, k_cols, positions, rows_ref, cot_ref, table_ref, part_ref):
    share = table_ref.shape[0] // (2 * len(order))
    channels = rows_ref.shape[1]
    for place, offset in enumerate(order):
        start = pl.multiple_of((slab ^ offset) * share, 8)
        turns = dot(k_cols[pl.ds(start, share), :].astype(bf16), positions)
        r = turns - jnp.floor(turns + 0.5)
        z = r * r
        s = r * horner(sin_coefs, z)
        c = horner(cos_coefs, z)
        table = jnp.concatenate([1.0 - 2.0 * s * s, 2.0 * s * c], axis=0).astype(bf16)
        at = pl.ds(place * 2 * share, 2 * share)
        table_ref[at, :] = table
        part_ref[at, :channels] = dot(table, rows_ref[...]).astype(part_ref.dtype)
        part_ref[at, channels:] = dot(table, cot_ref[...]).astype(part_ref.dtype)


def first_kernel(order, fetched, slab_ref, kv_hbm, pos_hbm, rows_hbm, cot_hbm, filter_hbm, *refs):
    sources, refs = refs[:fetched], refs[fetched:]
    table_ref, part_ref, k_cols, positions, rows_ref, cot_ref, filter_ref, *refs = refs
    copies_to, (kv_ref, pos_ref, k_rows, p_rows, sems) = refs[:fetched], refs[fetched:]
    slab = slab_ref[0]
    share = filter_ref.shape[0]
    filter_rows = pl.ds(pl.multiple_of(slab * share, 8), share)
    pairs = [
        (kv_hbm, kv_ref),
        (pos_hbm.at[:, 0], pos_ref),
        (rows_hbm.at[0], rows_ref),
        (cot_hbm.at[0], cot_ref),
        (filter_hbm.at[filter_rows, :], filter_ref),
        *zip(sources, copies_to),
    ]
    copies = [pltpu.make_async_copy(source, target, sems.at[i]) for i, (source, target) in enumerate(pairs)]
    for copy in copies:
        copy.start()
    k_rows[...] = jnp.zeros_like(k_rows)
    p_rows[...] = jnp.zeros_like(p_rows)
    copies[0].wait()
    copies[1].wait()
    pos = pos_ref[...]
    high = pos.astype(bf16).astype(f32)
    middle = (pos - high).astype(bf16).astype(f32)
    kv = kv_ref[...].astype(f32)
    for i, piece in enumerate((high, middle, pos - high - middle)):
        k_rows[3 * i : 3 * i + 3, :] = kv
        p_rows[3 * i : 3 * i + 3, :] = piece
    k_cols[...] = k_rows[...].T
    positions[...] = p_rows[...].astype(bf16)
    copies[2].wait()
    copies[3].wait()
    table_blocks(order, slab, k_cols, positions[...], rows_ref, cot_ref, table_ref, part_ref)
    for copy in copies[4:]:
        copy.wait()


def first_tables(order, slab, k_vectors, frac_pos, features, cotangent, k_filter, others, share):
    _, atoms, channels = features.shape
    kcount = k_vectors.shape[1]
    height = 2 * share * len(order)
    operands = (k_vectors, frac_pos.transpose(1, 0, 2), features, cotangent, k_filter, *others)
    shapes = [
        ((height, atoms), bf16),
        ((height, 2 * channels), bf16),
        ((kcount, 16), f32),
        ((16, atoms), bf16),
        ((atoms, channels), bf16),
        ((atoms, channels), bf16),
        ((share, channels), f32),
    ] + [(other.shape, other.dtype) for other in others]
    return pl.pallas_call(
        functools.partial(first_kernel, order, len(others)),
        name="first",
        out_shape=tuple(jax.ShapeDtypeStruct(shape, dtype) for shape, dtype in shapes),
        in_specs=[SMEM] + [HBM] * (5 + len(others)),
        out_specs=(VMEM,) * len(shapes),
        scratch_shapes=[
            pltpu.VMEM((3, kcount), jnp.int32),
            pltpu.VMEM((3, atoms), f32),
            pltpu.VMEM((16, kcount), f32),
            pltpu.VMEM((16, atoms), f32),
            pltpu.SemaphoreType.DMA((5 + len(others),)),
        ],
        compiler_params=params(),
        cost_estimate=pl.CostEstimate(
            flops=4 * height * atoms * channels, bytes_accessed=4 * height * atoms, transcendentals=0
        ),
    )(slab, *(pltpu.with_memory_space_constraint(value, pltpu.HBM) for value in operands))


def second_kernel(order, slab_ref, k_cols, positions, rows_ref, cot_ref, table_ref, part_ref):
    table_blocks(order, slab_ref[0], k_cols, positions[...], rows_ref, cot_ref, table_ref, part_ref)


def next_tables(dtype, order, slab, k_cols, positions, rows, cotan, share):
    atoms, channels = rows.shape
    height = 2 * share * len(order)
    return pl.pallas_call(
        functools.partial(second_kernel, order),
        out_shape=(
            jax.ShapeDtypeStruct((height, atoms), bf16),
            jax.ShapeDtypeStruct((height, 2 * channels), dtype),
        ),
        in_specs=[SMEM] + [VMEM] * 4,
        out_specs=(VMEM, VMEM),
        compiler_params=params(),
        cost_estimate=pl.CostEstimate(
            flops=4 * height * atoms * channels, bytes_accessed=4 * height * atoms, transcendentals=0
        ),
    )(slab, k_cols, positions, rows, cotan)


def one_hot(row_count, indices):
    rows = lax.broadcasted_iota(jnp.int32, (row_count, indices.shape[1]), 0)
    return (rows == indices).astype(f32).astype(bf16)


def rims_kernel(rows_ref, lists_ref, rows_t_ref, prev_ref, next_ref):
    atoms = rows_ref.shape[0]
    lists = lists_ref[0]
    rows_t = rows_ref[...].T
    rows_t_ref[...] = rows_t
    prev_ref[...] = dot(rows_t, one_hot(atoms, lists[0:1, :])).astype(bf16)
    next_ref[...] = dot(rows_t, one_hot(atoms, lists[1:2, :])).astype(bf16)


def rim_features(rows, lists):
    atoms, channels = rows.shape
    rim = lists.shape[2]
    return pl.pallas_call(
        rims_kernel,
        name="rims",
        out_shape=(
            jax.ShapeDtypeStruct((channels, atoms), bf16),
            jax.ShapeDtypeStruct((channels, rim), bf16),
            jax.ShapeDtypeStruct((channels, rim), bf16),
        ),
        in_specs=[VMEM] * 2,
        out_specs=(VMEM,) * 3,
        compiler_params=params(),
        cost_estimate=pl.CostEstimate(
            flops=4 * atoms * channels * rim, bytes_accessed=4 * atoms * channels, transcendentals=0
        ),
    )(rows, lists)


def edge_kernel(block, src_ref, dst_ref, dist_ref, cot_ref, rows_t_ref, own_ref, low_ref, up_ref, grad_ref, total):
    atoms, _ = cot_ref.shape
    rim = low_ref.shape[0]
    edges = src_ref.shape[1]
    cot_t = cot_ref[...].T
    for start in range(0, edges, block):
        at = slice(start, start + block)
        weight = jnp.maximum(1.0 - dist_ref[:, at] / cutoff_radius, 0.0)
        weight = weight * weight
        taken = dot(cot_t, one_hot(atoms, dst_ref[:, at]))
        weighted = (taken * weight).astype(bf16)
        part = dot(one_hot(total.shape[0], src_ref[:, at]), weighted, 1, 1)
        total[...] = part if start == 0 else total[...] + part
    own = total[:atoms, :]
    own_ref[...] = own
    low_ref[...] = total[atoms : atoms + rim, :].astype(bf16)
    up_ref[...] = total[atoms + rim :, :].astype(bf16)
    high, low = halves(own)
    grad_ref[...] = dot(rows_t_ref[...], high) + dot(rows_t_ref[...], low)


def edge_rows(sources, targets, lengths, cotan, rows_t, rim):
    atoms, channels = cotan.shape
    edges = sources.shape[1]
    rows = atoms + 2 * rim
    block = math.gcd(edges, 2048)
    return pl.pallas_call(
        functools.partial(edge_kernel, block),
        name="edges",
        out_shape=(
            jax.ShapeDtypeStruct((atoms, channels), f32),
            jax.ShapeDtypeStruct((rim, channels), bf16),
            jax.ShapeDtypeStruct((rim, channels), bf16),
            jax.ShapeDtypeStruct((channels, channels), f32),
        ),
        in_specs=[VMEM] * 5,
        out_specs=(VMEM,) * 4,
        scratch_shapes=[pltpu.VMEM((rows, channels), f32)],
        compiler_params=params(),
        cost_estimate=pl.CostEstimate(
            flops=2 * edges * (rows + atoms) * channels, bytes_accessed=edges * 12, transcendentals=0
        ),
    )(sources, targets, lengths, cotan, rows_t)


def split_blocks(order, slab, values, send_ref, keep_ref, blocks):
    count, height, _ = blocks.shape
    height = height // len(values)
    for i in range(count):
        for j, value in enumerate(values):
            blocks[i, j * height : (j + 1) * height] = value[i * height : (i + 1) * height, :]
    for place, offset in enumerate(order):
        keep_ref[place] = blocks[slab ^ offset]
        send_ref[place] = blocks[slab ^ offset ^ 1]


def short_kernel(own_ref, above_ref, below_ref, lists_ref, cot_ref, w_ref, base_ref):
    atoms = own_ref.shape[0]
    lists = lists_ref[0]
    owned = own_ref[...] + dot(one_hot(atoms, lists[1:2, :]), above_ref[...])
    owned = owned + dot(one_hot(atoms, lists[0:1, :]), below_ref[...])
    high, low = halves(owned)
    w = w_ref[...]
    base_ref[...] = cot_ref[...].astype(f32) + (dot(high, w, 1, 1) + dot(low, w, 1, 1))


def short_range(own, above, below, lists, cotan, w_short):
    atoms, channels = cotan.shape
    return pl.pallas_call(
        short_kernel,
        name="short",
        out_shape=jax.ShapeDtypeStruct((atoms, channels), f32),
        in_specs=[VMEM] * 6,
        out_specs=VMEM,
        compiler_params=params(),
        cost_estimate=pl.CostEstimate(
            flops=8 * atoms * channels * channels, bytes_accessed=8 * atoms * channels, transcendentals=0
        ),
    )(own, above, below, lists, cotan, w_short)


def share_kernel(
    order, norm, count, slab_ref, filter_ref, w_ref, grad_ref, lower_t, upper_t, low_ref, up_ref, *refs
):
    parts, (adj_ref, gfilter_ref, send_ref, keep_ref, blocks) = refs[:count], refs[count:]
    channels = w_ref.shape[0]
    total = parts[0][...].astype(f32)
    for part in parts[1:]:
        total = total + part[...].astype(f32)
    structure = total[:, :channels]
    moved, moved_low = halves(total[:, channels:])
    response = dot(moved, w_ref[...], 1, 1) + dot(moved_low, w_ref[...], 1, 1)
    k_filter = filter_ref[...]
    double = jnp.concatenate([k_filter, k_filter], axis=0) * norm
    filtered, filtered_low = halves((structure * double).T)
    wout = dot(filtered, moved) + (dot(filtered, moved_low) + dot(filtered_low, moved))
    wshort = grad_ref[...] + (dot(lower_t[...], low_ref[...]) + dot(upper_t[...], up_ref[...]))
    split_blocks(order, slab_ref[0], (wout, wshort), send_ref, keep_ref, blocks)
    adj_ref[...] = (response * double).T.astype(bf16)
    product = structure * response
    share = k_filter.shape[0]
    gfilter_ref[...] = norm * (product[:share] + product[share:])


def own_share(order, norm, slab, k_filter, w_out, short_terms, parts):
    height, channels = parts[0].shape[0], w_out.shape[0]
    half = len(order)
    rows = 2 * channels // (2 * half)
    return pl.pallas_call(
        functools.partial(share_kernel, order, norm, len(parts)),
        name="share",
        out_shape=(
            jax.ShapeDtypeStruct((channels, height), bf16),
            jax.ShapeDtypeStruct((height // 2, channels), f32),
            jax.ShapeDtypeStruct((half, rows, channels), f32),
            jax.ShapeDtypeStruct((half, rows, channels), f32),
        ),
        in_specs=[SMEM] + [VMEM] * (2 + len(short_terms) + len(parts)),
        out_specs=(VMEM,) * 4,
        scratch_shapes=[pltpu.VMEM((2 * half, rows, channels), f32)],
        compiler_params=params(),
        cost_estimate=pl.CostEstimate(
            flops=8 * height * channels * channels, bytes_accessed=16 * height * channels, transcendentals=0
        ),
    )(slab, k_filter, w_out, *short_terms, *parts)


def back_kernel(orders, order, base_ref, even_adj_ref, odd_adj_ref, *refs):
    table_refs, out_ref = refs[:-1], refs[-1]
    width = even_adj_ref.shape[2]
    total = None
    for offsets, table_ref in zip(orders, table_refs):
        for place, offset in enumerate(offsets):
            adj = (odd_adj_ref if offset & 1 else even_adj_ref)[order.index(offset & ~1)]
            part = dot(adj, table_ref[place * width : (place + 1) * width, :])
            total = part if total is None else total + part
    out_ref[...] = (base_ref[...] + total.T).astype(bf16)


def back_project(orders, order, base, even_adj, odd_adj, tables):
    atoms, channels = base.shape
    height = sum(table.shape[0] for table in tables)
    return pl.pallas_call(
        functools.partial(back_kernel, orders, order),
        name="back",
        out_shape=jax.ShapeDtypeStruct((atoms, channels), bf16),
        in_specs=[VMEM] * (3 + len(tables)),
        out_specs=VMEM,
        compiler_params=params(),
        cost_estimate=pl.CostEstimate(
            flops=2 * height * atoms * channels, bytes_accessed=2 * height * atoms, transcendentals=0
        ),
    )(base, even_adj, odd_adj, *tables)


def place_kernel(order, scale, slab_ref, even_ref, odd_ref, wout_ref, wshort_ref, blocks):
    count, height, _ = blocks.shape
    half = height // 2
    slab = slab_ref[0]
    for place, offset in enumerate(order):
        blocks[slab ^ offset] = even_ref[place].astype(f32) * scale
        blocks[slab ^ offset ^ 1] = odd_ref[place].astype(f32) * scale
    for i in range(count):
        wout_ref[i * half : (i + 1) * half, :] = blocks[i, :half, :]
        wshort_ref[i * half : (i + 1) * half, :] = blocks[i, half:, :]


def place_grads(order, scale, slab, even, odd):
    half, height, channels = even.shape
    return pl.pallas_call(
        functools.partial(place_kernel, order, scale),
        name="place",
        out_shape=(jax.ShapeDtypeStruct((channels, channels), f32),) * 2,
        in_specs=[SMEM, VMEM, VMEM],
        out_specs=(VMEM, VMEM),
        scratch_shapes=[pltpu.VMEM((2 * half, height, channels), f32)],
        compiler_params=params(),
    )(slab, even, odd)


def doubling_gather(blocks):
    count = lax.axis_size("slab")
    bit = count // 2
    while bit > 1:
        moved = xor_permute(blocks, "slab", bit)
        blocks = jnp.concatenate([blocks, moved], axis=0)
        bit = bit // 2
    return blocks


def sum_replicas(value):
    bit = 1
    while bit < lax.axis_size("rep"):
        sent = value.astype(bf16)
        moved = xor_permute(sent, "rep", bit)
        value = sent.astype(f32) + moved.astype(f32)
        bit = 2 * bit
    return value


def sum_replicas_direct(value):
    count = lax.axis_size("rep")
    terms = [value.astype(bf16)]
    for offset in range(count - 1, 0, -1):
        terms.insert(1, xor_permute(terms[0], "rep", offset))
    terms = [term.astype(f32) for term in terms]
    while len(terms) > 1:
        terms = [terms[i] + terms[i + 1] for i in range(0, len(terms), 2)]
    return terms[0]


def folded_sum(blocks):
    count = lax.axis_size("slab")
    bit = 2
    terms = None
    while bit < count:
        width = min(4, count // bit)
        sent = [[offset for offset in sorted(blocks) if offset // bit % width == g] for g in range(width)]
        half = blocks[0].shape[1] // 2

        def move(g, pieces):
            payload = pieces[0] if len(pieces) == 1 else jnp.concatenate(pieces, axis=0)
            moved = xor_permute(payload, "slab", g * bit)
            return jnp.split(moved, len(pieces), axis=0)

        if width == 4:
            first = move(1, [blocks[offset][:, :half].astype(bf16) for offset in sent[3]])
            second = move(2, [blocks[offset][:, half:].astype(bf16) for offset in sent[3]])
            for i, offset in enumerate(sent[2]):
                left = blocks[offset][:, :half] + first[i].astype(f32)
                blocks[offset] = jnp.concatenate([left, blocks[offset][:, half:]], axis=1)
            for i, offset in enumerate(sent[1]):
                right = blocks[offset][:, half:] + second[i].astype(f32)
                blocks[offset] = jnp.concatenate([blocks[offset][:, :half], right], axis=1)
        received = [move(g, [blocks[offset].astype(bf16) for offset in sent[g]]) for g in range(1, min(width, 3))]
        terms = [blocks[0], *(moved[0] for moved in received)]
        blocks = {
            offset: sum((moved[i].astype(f32) for moved in received), blocks[offset])
            for i, offset in enumerate(sent[0])
        }
        bit = bit * width
    return terms


def plane_gather(block, order):
    count = lax.axis_size("slab")
    planes, bit = [], 2
    while bit < count:
        planes.append((bit, min(4, count // bit)))
        bit *= planes[-1][1]
    held = {0: block}
    for bit, width in reversed(planes):
        offsets = sorted(held)
        payload = held[0] if len(held) == 1 else jnp.stack([held[offset] for offset in offsets])
        for g in range(width - 1, 0, -1):
            moved = xor_permute(payload, "slab", g * bit)
            for i, offset in enumerate(offsets):
                held[offset ^ g * bit] = moved if len(offsets) == 1 else moved[i]
    return jnp.stack([held[offset] for offset in order])


def plane_sum(blocks):
    count = lax.axis_size("slab")
    bit = 2
    terms = None
    while bit < count:
        width = min(4, count // bit)
        sent = {g: [] for g in range(width)}
        for offset in sorted(blocks):
            sent[offset // bit % width].append(offset)
        received = {offset: [] for offset in sent[0]}
        for g in range(width - 1, 0, -1):
            pieces = [blocks[offset].astype(bf16) for offset in sent[g]]
            payload = pieces[0] if len(pieces) == 1 else jnp.concatenate(pieces, axis=0)
            moved = xor_permute(payload, "slab", g * bit)
            height = moved.shape[0] // len(pieces)
            for i, offset in enumerate(sent[0]):
                received[offset].append(moved[i * height : (i + 1) * height])
        terms = [blocks[0], *received[0]]
        blocks = {
            offset: sum((piece.astype(f32) for piece in received[offset]), blocks[offset].astype(f32))
            for offset in sent[0]
        }
        bit = bit * width
    return terms


def block(
    features,
    cotangent,
    frac_pos,
    k_vectors,
    k_filter,
    w_out,
    w_short,
    edge_src,
    edge_dst,
    distance,
    halo_idx,
):
    _, atoms, _ = features.shape
    kcount = k_filter.shape[0]
    count = lax.axis_size("slab")
    replicas = lax.axis_size("rep")
    norm = 1.0 / math.sqrt(kcount * atoms * count)
    scale = 1.0 / math.sqrt(replicas * atoms * count)
    share = kcount // count
    slab = lax.axis_index("slab").astype(jnp.int32)[None]

    near, far = plane_order(count)
    near, far = (tuple(offset for group in groups for offset in group) for groups in (near, far))
    flip = lambda offsets: tuple(offset ^ 1 for offset in offsets)
    orders = (flip(far), far, flip(near), near)
    order = halving_order(count)

    odda, odda_part, k_cols, positions, rows, cotan, own_filter, src, dst, dist, lists, w_out, w_short = first_tables(
        orders[0],
        slab,
        k_vectors,
        frac_pos,
        features,
        cotangent,
        k_filter,
        (edge_src, edge_dst, distance, halo_idx, w_out, w_short),
        share,
    )
    moveda = xor_permute(odda_part, "slab", 1)
    operands = (slab, k_cols, positions, rows, cotan, share)
    evena, evena_part = next_tables(f32, orders[1], *operands)
    oddb, oddb_part = next_tables(bf16, orders[2], *operands)
    movedb = xor_permute(oddb_part, "slab", 1)
    evenb, evenb_part = next_tables(f32, orders[3], *operands)
    blocks = {}
    for offsets, part, moved in ((far, evena_part, moveda), (near, evenb_part, movedb)):
        paired = part + moved.astype(f32)
        for i, offset in enumerate(offsets):
            blocks[offset] = paired[i * 2 * share : (i + 1) * 2 * share]
    parts = folded_sum(blocks)

    rows_t, to_prev, to_next = rim_features(rows, lists)
    lower_t = shifted(to_next, "slab", 1)
    upper_t = shifted(to_prev, "slab", -1)
    own_rows, low, up, wshort = edge_rows(src, dst, dist, cotan, rows_t, lists.shape[2])
    short_terms = (wshort, lower_t, upper_t, low, up)
    adj, gfilter, send, keep = own_share(order, norm, slab, own_filter, w_out, short_terms, parts)
    grads = keep + xor_permute(send, "slab", 1)

    from_above = shifted(low, "slab", -1)
    from_below = shifted(up, "slab", 1)
    base = short_range(own_rows, from_above, from_below, lists, cotan, w_short)

    terms = plane_sum({offset: grads[i] for i, offset in enumerate(order)})
    own_grad = sum((term.astype(f32) for term in terms[1:]), terms[0])

    adj_even = doubling_gather(adj[None])
    adj_odd = xor_permute(adj_even, "slab", 1)
    grad_features = back_project(orders, order, base, adj_even, adj_odd, (odda, evena, oddb, evenb))

    own_grad = sum_replicas_direct(own_grad).astype(bf16)
    filter_sum = sum_replicas(gfilter)
    grad_filter = filter_sum / replicas
    grad_even = plane_gather(own_grad, order)
    grad_odd = xor_permute(grad_even, "slab", 1)
    grad_wout, grad_wshort = place_grads(order, scale, slab, grad_even, grad_odd)
    return (grad_features[None], grad_wout, grad_wshort, grad_filter)


def solution(mesh):
    return jax.shard_map(
        block,
        mesh=mesh,
        in_specs=(
            P("rep", "slab", None),
            P("rep", "slab", None),
            P("rep", None, "slab"),
            P(),
            P(),
            P(),
            P(),
            P("rep", "slab"),
            P("rep", "slab"),
            P("rep", "slab"),
            P("rep", "slab", None),
        ),
        out_specs=(P("rep", "slab", None), P(), P(), P("slab", None)),
        check_vma=False,
    )
```

```python
import functools
import math

import jax
import jax.numpy as jnp
from jax import lax
from jax.experimental import pallas as pl
from jax.experimental.pallas import tpu as pltpu
from jax.sharding import PartitionSpec as P


cutoff_radius = 5.0
f32, bf16 = jnp.float32, jnp.bfloat16

sin_coefs = (3.1415926401307073, -5.167710083507895, 2.550077523214559, -0.5982912856198396, 0.0776576603038396)
cos_coefs = (0.9999999532476077, -4.934792830619641, 4.058411352862562, -1.331876568080612, 0.21968961109715823)

VMEM = pl.BlockSpec(memory_space=pltpu.VMEM)
SMEM = pl.BlockSpec(memory_space=pltpu.SMEM)
HBM = pl.BlockSpec(memory_space=pltpu.HBM)


def params():
    return pltpu.CompilerParams(vmem_limit_bytes=48 * 1024 * 1024)


def xor_permute(value, axis, bits):
    count = lax.axis_size(axis)
    return lax.ppermute(value, axis, [(source, source ^ bits) for source in range(count)])


def shifted(value, axis, steps):
    count = lax.axis_size(axis)
    return lax.ppermute(value, axis, [(source, (source + steps) % count) for source in range(count)])


def halving_order(count):
    order, bit = [0], count // 2
    while bit > 1:
        order = order + [offset | bit for offset in order]
        bit //= 2
    return tuple(order)


def plane_order(count):
    width = min(4, count // 2)
    offsets = [[offset for offset in range(0, count, 2) if offset // 2 % width == g] for g in range(width)]
    return offsets[:-1], offsets[-1:]


def horner(coefs, z):
    total = coefs[-1]
    for c in coefs[-2::-1]:
        total = total * z + c
    return total


def halves(value):
    high = value.astype(bf16)
    return high, (value - high.astype(f32)).astype(bf16)


def dot(left, right, left_dim=1, right_dim=0):
    return lax.dot_general(left, right, (((left_dim,), (right_dim,)), ((), ())), preferred_element_type=f32)


def table_blocks(order, slab, k_cols, positions, rows_ref, cot_ref, table_ref, part_ref):
    share = table_ref.shape[0] // (2 * len(order))
    channels = rows_ref.shape[1]
    for place, offset in enumerate(order):
        start = pl.multiple_of((slab ^ offset) * share, 8)
        turns = dot(k_cols[pl.ds(start, share), :].astype(bf16), positions)
        r = turns - jnp.floor(turns + 0.5)
        z = r * r
        s = r * horner(sin_coefs, z)
        c = horner(cos_coefs, z)
        table = jnp.concatenate([1.0 - 2.0 * s * s, 2.0 * s * c], axis=0).astype(bf16)
        at = pl.ds(place * 2 * share, 2 * share)
        table_ref[at, :] = table
        part_ref[at, :channels] = dot(table, rows_ref[...]).astype(part_ref.dtype)
        part_ref[at, channels:] = dot(table, cot_ref[...]).astype(part_ref.dtype)


def first_kernel(order, fetched, slab_ref, kv_hbm, pos_hbm, rows_hbm, cot_hbm, filter_hbm, *refs):
    sources, refs = refs[:fetched], refs[fetched:]
    table_ref, part_ref, k_cols, positions, rows_ref, cot_ref, filter_ref, *refs = refs
    copies_to, (kv_ref, pos_ref, k_rows, p_rows, sems) = refs[:fetched], refs[fetched:]
    slab = slab_ref[0]
    share = filter_ref.shape[0]
    filter_rows = pl.ds(pl.multiple_of(slab * share, 8), share)
    pairs = [
        (kv_hbm, kv_ref),
        (pos_hbm.at[:, 0], pos_ref),
        (rows_hbm.at[0], rows_ref),
        (cot_hbm.at[0], cot_ref),
        (filter_hbm.at[filter_rows, :], filter_ref),
        *zip(sources, copies_to),
    ]
    copies = [pltpu.make_async_copy(source, target, sems.at[i]) for i, (source, target) in enumerate(pairs)]
    for copy in copies:
        copy.start()
    k_rows[...] = jnp.zeros_like(k_rows)
    p_rows[...] = jnp.zeros_like(p_rows)
    copies[0].wait()
    copies[1].wait()
    pos = pos_ref[...]
    high = pos.astype(bf16).astype(f32)
    middle = (pos - high).astype(bf16).astype(f32)
    kv = kv_ref[...].astype(f32)
    for i, piece in enumerate((high, middle, pos - high - middle)):
        k_rows[3 * i : 3 * i + 3, :] = kv
        p_rows[3 * i : 3 * i + 3, :] = piece
    k_cols[...] = k_rows[...].T
    positions[...] = p_rows[...].astype(bf16)
    copies[2].wait()
    copies[3].wait()
    table_blocks(order, slab, k_cols, positions[...], rows_ref, cot_ref, table_ref, part_ref)
    for copy in copies[4:]:
        copy.wait()


def first_tables(order, slab, k_vectors, frac_pos, features, cotangent, k_filter, others, share):
    _, atoms, channels = features.shape
    kcount = k_vectors.shape[1]
    height = 2 * share * len(order)
    operands = (k_vectors, frac_pos.transpose(1, 0, 2), features, cotangent, k_filter, *others)
    shapes = [
        ((height, atoms), bf16),
        ((height, 2 * channels), bf16),
        ((kcount, 16), f32),
        ((16, atoms), bf16),
        ((atoms, channels), bf16),
        ((atoms, channels), bf16),
        ((share, channels), f32),
    ] + [(other.shape, other.dtype) for other in others]
    return pl.pallas_call(
        functools.partial(first_kernel, order, len(others)),
        name="first",
        out_shape=tuple(jax.ShapeDtypeStruct(shape, dtype) for shape, dtype in shapes),
        in_specs=[SMEM] + [HBM] * (5 + len(others)),
        out_specs=(VMEM,) * len(shapes),
        scratch_shapes=[
            pltpu.VMEM((3, kcount), jnp.int32),
            pltpu.VMEM((3, atoms), f32),
            pltpu.VMEM((16, kcount), f32),
            pltpu.VMEM((16, atoms), f32),
            pltpu.SemaphoreType.DMA((5 + len(others),)),
        ],
        compiler_params=params(),
        cost_estimate=pl.CostEstimate(
            flops=4 * height * atoms * channels, bytes_accessed=4 * height * atoms, transcendentals=0
        ),
    )(slab, *(pltpu.with_memory_space_constraint(value, pltpu.HBM) for value in operands))


def second_kernel(order, slab_ref, k_cols, positions, rows_ref, cot_ref, table_ref, part_ref):
    table_blocks(order, slab_ref[0], k_cols, positions[...], rows_ref, cot_ref, table_ref, part_ref)


def next_tables(dtype, order, slab, k_cols, positions, rows, cotan, share):
    atoms, channels = rows.shape
    height = 2 * share * len(order)
    return pl.pallas_call(
        functools.partial(second_kernel, order),
        out_shape=(
            jax.ShapeDtypeStruct((height, atoms), bf16),
            jax.ShapeDtypeStruct((height, 2 * channels), dtype),
        ),
        in_specs=[SMEM] + [VMEM] * 4,
        out_specs=(VMEM, VMEM),
        compiler_params=params(),
        cost_estimate=pl.CostEstimate(
            flops=4 * height * atoms * channels, bytes_accessed=4 * height * atoms, transcendentals=0
        ),
    )(slab, k_cols, positions, rows, cotan)


def one_hot(row_count, indices):
    rows = lax.broadcasted_iota(jnp.int32, (row_count, indices.shape[1]), 0)
    return (rows == indices).astype(f32).astype(bf16)


def rims_kernel(rows_ref, lists_ref, rows_t_ref, prev_ref, next_ref):
    atoms = rows_ref.shape[0]
    lists = lists_ref[0]
    rows_t = rows_ref[...].T
    rows_t_ref[...] = rows_t
    prev_ref[...] = dot(rows_t, one_hot(atoms, lists[0:1, :])).astype(bf16)
    next_ref[...] = dot(rows_t, one_hot(atoms, lists[1:2, :])).astype(bf16)


def rim_features(rows, lists):
    atoms, channels = rows.shape
    rim = lists.shape[2]
    return pl.pallas_call(
        rims_kernel,
        name="rims",
        out_shape=(
            jax.ShapeDtypeStruct((channels, atoms), bf16),
            jax.ShapeDtypeStruct((channels, rim), bf16),
            jax.ShapeDtypeStruct((channels, rim), bf16),
        ),
        in_specs=[VMEM] * 2,
        out_specs=(VMEM,) * 3,
        compiler_params=params(),
        cost_estimate=pl.CostEstimate(
            flops=4 * atoms * channels * rim, bytes_accessed=4 * atoms * channels, transcendentals=0
        ),
    )(rows, lists)


def edge_kernel(block, src_ref, dst_ref, dist_ref, cot_ref, rows_t_ref, own_ref, low_ref, up_ref, grad_ref, total):
    atoms, _ = cot_ref.shape
    rim = low_ref.shape[0]
    edges = src_ref.shape[1]
    cot_t = cot_ref[...].T
    for start in range(0, edges, block):
        at = slice(start, start + block)
        weight = jnp.maximum(1.0 - dist_ref[:, at] / cutoff_radius, 0.0)
        weight = weight * weight
        taken = dot(cot_t, one_hot(atoms, dst_ref[:, at]))
        weighted = (taken * weight).astype(bf16)
        part = dot(one_hot(total.shape[0], src_ref[:, at]), weighted, 1, 1)
        total[...] = part if start == 0 else total[...] + part
    own = total[:atoms, :]
    own_ref[...] = own
    low_ref[...] = total[atoms : atoms + rim, :].astype(bf16)
    up_ref[...] = total[atoms + rim :, :].astype(bf16)
    high, low = halves(own)
    grad_ref[...] = dot(rows_t_ref[...], high) + dot(rows_t_ref[...], low)


def edge_rows(sources, targets, lengths, cotan, rows_t, rim):
    atoms, channels = cotan.shape
    edges = sources.shape[1]
    rows = atoms + 2 * rim
    block = math.gcd(edges, 2048)
    return pl.pallas_call(
        functools.partial(edge_kernel, block),
        name="edges",
        out_shape=(
            jax.ShapeDtypeStruct((atoms, channels), f32),
            jax.ShapeDtypeStruct((rim, channels), bf16),
            jax.ShapeDtypeStruct((rim, channels), bf16),
            jax.ShapeDtypeStruct((channels, channels), f32),
        ),
        in_specs=[VMEM] * 5,
        out_specs=(VMEM,) * 4,
        scratch_shapes=[pltpu.VMEM((rows, channels), f32)],
        compiler_params=params(),
        cost_estimate=pl.CostEstimate(
            flops=2 * edges * (rows + atoms) * channels, bytes_accessed=edges * 12, transcendentals=0
        ),
    )(sources, targets, lengths, cotan, rows_t)


def split_blocks(order, slab, values, send_ref, keep_ref, blocks):
    count, height, _ = blocks.shape
    height = height // len(values)
    for i in range(count):
        for j, value in enumerate(values):
            blocks[i, j * height : (j + 1) * height] = value[i * height : (i + 1) * height, :]
    for place, offset in enumerate(order):
        keep_ref[place] = blocks[slab ^ offset]
        send_ref[place] = blocks[slab ^ offset ^ 1]


def short_kernel(own_ref, above_ref, below_ref, lists_ref, cot_ref, w_ref, base_ref):
    atoms = own_ref.shape[0]
    lists = lists_ref[0]
    owned = own_ref[...] + dot(one_hot(atoms, lists[1:2, :]), above_ref[...])
    owned = owned + dot(one_hot(atoms, lists[0:1, :]), below_ref[...])
    high, low = halves(owned)
    w = w_ref[...]
    base_ref[...] = cot_ref[...].astype(f32) + (dot(high, w, 1, 1) + dot(low, w, 1, 1))


def short_range(own, above, below, lists, cotan, w_short):
    atoms, channels = cotan.shape
    return pl.pallas_call(
        short_kernel,
        name="short",
        out_shape=jax.ShapeDtypeStruct((atoms, channels), f32),
        in_specs=[VMEM] * 6,
        out_specs=VMEM,
        compiler_params=params(),
        cost_estimate=pl.CostEstimate(
            flops=8 * atoms * channels * channels, bytes_accessed=8 * atoms * channels, transcendentals=0
        ),
    )(own, above, below, lists, cotan, w_short)


def share_kernel(
    order, norm, count, slab_ref, filter_ref, w_ref, grad_ref, lower_t, upper_t, low_ref, up_ref, *refs
):
    parts, (adj_ref, gfilter_ref, send_ref, keep_ref, blocks) = refs[:count], refs[count:]
    channels = w_ref.shape[0]
    total = parts[0][...].astype(f32)
    for part in parts[1:]:
        total = total + part[...].astype(f32)
    structure = total[:, :channels]
    moved, moved_low = halves(total[:, channels:])
    response = dot(moved, w_ref[...], 1, 1) + dot(moved_low, w_ref[...], 1, 1)
    k_filter = filter_ref[...]
    double = jnp.concatenate([k_filter, k_filter], axis=0) * norm
    filtered, filtered_low = halves((structure * double).T)
    wout = dot(filtered, moved) + (dot(filtered, moved_low) + dot(filtered_low, moved))
    wshort = grad_ref[...] + (dot(lower_t[...], low_ref[...]) + dot(upper_t[...], up_ref[...]))
    split_blocks(order, slab_ref[0], (wout, wshort), send_ref, keep_ref, blocks)
    adj_ref[...] = (response * double).T.astype(bf16)
    product = structure * response
    share = k_filter.shape[0]
    gfilter_ref[...] = norm * (product[:share] + product[share:])


def own_share(order, norm, slab, k_filter, w_out, short_terms, parts):
    height, channels = parts[0].shape[0], w_out.shape[0]
    half = len(order)
    rows = 2 * channels // (2 * half)
    return pl.pallas_call(
        functools.partial(share_kernel, order, norm, len(parts)),
        name="share",
        out_shape=(
            jax.ShapeDtypeStruct((channels, height), bf16),
            jax.ShapeDtypeStruct((height // 2, channels), f32),
            jax.ShapeDtypeStruct((half, rows, channels), f32),
            jax.ShapeDtypeStruct((half, rows, channels), f32),
        ),
        in_specs=[SMEM] + [VMEM] * (2 + len(short_terms) + len(parts)),
        out_specs=(VMEM,) * 4,
        scratch_shapes=[pltpu.VMEM((2 * half, rows, channels), f32)],
        compiler_params=params(),
        cost_estimate=pl.CostEstimate(
            flops=8 * height * channels * channels, bytes_accessed=16 * height * channels, transcendentals=0
        ),
    )(slab, k_filter, w_out, *short_terms, *parts)


def back_kernel(orders, order, base_ref, even_adj_ref, odd_adj_ref, *refs):
    table_refs, out_ref = refs[:-1], refs[-1]
    width = even_adj_ref.shape[2]
    total = None
    for offsets, table_ref in zip(orders, table_refs):
        for place, offset in enumerate(offsets):
            adj = (odd_adj_ref if offset & 1 else even_adj_ref)[order.index(offset & ~1)]
            part = dot(adj, table_ref[place * width : (place + 1) * width, :])
            total = part if total is None else total + part
    out_ref[...] = (base_ref[...] + total.T).astype(bf16)


def back_project(orders, order, base, even_adj, odd_adj, tables):
    atoms, channels = base.shape
    height = sum(table.shape[0] for table in tables)
    return pl.pallas_call(
        functools.partial(back_kernel, orders, order),
        name="back",
        out_shape=jax.ShapeDtypeStruct((atoms, channels), bf16),
        in_specs=[VMEM] * (3 + len(tables)),
        out_specs=VMEM,
        compiler_params=params(),
        cost_estimate=pl.CostEstimate(
            flops=2 * height * atoms * channels, bytes_accessed=2 * height * atoms, transcendentals=0
        ),
    )(base, even_adj, odd_adj, *tables)


def place_kernel(order, scale, slab_ref, even_ref, odd_ref, wout_ref, wshort_ref, blocks):
    count, height, _ = blocks.shape
    half = height // 2
    slab = slab_ref[0]
    for place, offset in enumerate(order):
        blocks[slab ^ offset] = even_ref[place].astype(f32) * scale
        blocks[slab ^ offset ^ 1] = odd_ref[place].astype(f32) * scale
    for i in range(count):
        wout_ref[i * half : (i + 1) * half, :] = blocks[i, :half, :]
        wshort_ref[i * half : (i + 1) * half, :] = blocks[i, half:, :]


def place_grads(order, scale, slab, even, odd):
    half, height, channels = even.shape
    return pl.pallas_call(
        functools.partial(place_kernel, order, scale),
        name="place",
        out_shape=(jax.ShapeDtypeStruct((channels, channels), f32),) * 2,
        in_specs=[SMEM, VMEM, VMEM],
        out_specs=(VMEM, VMEM),
        scratch_shapes=[pltpu.VMEM((2 * half, height, channels), f32)],
        compiler_params=params(),
    )(slab, even, odd)


def sum_replicas(value):
    bit = 1
    while bit < lax.axis_size("rep"):
        sent = value.astype(bf16)
        moved = xor_permute(sent, "rep", bit)
        value = sent.astype(f32) + moved.astype(f32)
        bit = 2 * bit
    return value


def sum_replicas_direct(value):
    count = lax.axis_size("rep")
    terms = [value.astype(bf16)]
    for offset in range(count - 1, 0, -1):
        terms.insert(1, xor_permute(terms[0], "rep", offset))
    terms = [term.astype(f32) for term in terms]
    while len(terms) > 1:
        terms = [terms[i] + terms[i + 1] for i in range(0, len(terms), 2)]
    return terms[0]


def folded_sum(blocks):
    count = lax.axis_size("slab")
    bit = 2
    terms = None
    while bit < count:
        width = min(4, count // bit)
        sent = [[offset for offset in sorted(blocks) if offset // bit % width == g] for g in range(width)]
        half = blocks[0].shape[1] // 2

        def move(g, pieces):
            payload = pieces[0] if len(pieces) == 1 else jnp.concatenate(pieces, axis=0)
            moved = xor_permute(payload, "slab", g * bit)
            return jnp.split(moved, len(pieces), axis=0)

        if width == 4:
            first = move(1, [blocks[offset][:, :half].astype(bf16) for offset in sent[3]])
            second = move(2, [blocks[offset][:, half:].astype(bf16) for offset in sent[3]])
            for i, offset in enumerate(sent[2]):
                left = blocks[offset][:, :half] + first[i].astype(f32)
                blocks[offset] = jnp.concatenate([left, blocks[offset][:, half:]], axis=1)
            for i, offset in enumerate(sent[1]):
                right = blocks[offset][:, half:] + second[i].astype(f32)
                blocks[offset] = jnp.concatenate([blocks[offset][:, :half], right], axis=1)
        received = [move(g, [blocks[offset].astype(bf16) for offset in sent[g]]) for g in range(1, min(width, 3))]
        terms = [blocks[0], *(moved[0] for moved in received)]
        blocks = {
            offset: sum((moved[i].astype(f32) for moved in received), blocks[offset])
            for i, offset in enumerate(sent[0])
        }
        bit = bit * width
    return terms


def plane_gather(block, order):
    count = lax.axis_size("slab")
    planes, bit = [], 2
    while bit < count:
        planes.append((bit, min(4, count // bit)))
        bit *= planes[-1][1]
    held = {0: block}
    for bit, width in reversed(planes):
        offsets = sorted(held)
        payload = held[0] if len(held) == 1 else jnp.stack([held[offset] for offset in offsets])
        for g in range(width - 1, 0, -1):
            moved = xor_permute(payload, "slab", g * bit)
            for i, offset in enumerate(offsets):
                held[offset ^ g * bit] = moved if len(offsets) == 1 else moved[i]
    return jnp.stack([held[offset] for offset in order])


def plane_sum(blocks):
    count = lax.axis_size("slab")
    bit = 2
    terms = None
    while bit < count:
        width = min(4, count // bit)
        sent = {g: [] for g in range(width)}
        for offset in sorted(blocks):
            sent[offset // bit % width].append(offset)
        received = {offset: [] for offset in sent[0]}
        for g in range(width - 1, 0, -1):
            pieces = [blocks[offset].astype(bf16) for offset in sent[g]]
            payload = pieces[0] if len(pieces) == 1 else jnp.concatenate(pieces, axis=0)
            moved = xor_permute(payload, "slab", g * bit)
            height = moved.shape[0] // len(pieces)
            for i, offset in enumerate(sent[0]):
                received[offset].append(moved[i * height : (i + 1) * height])
        terms = [blocks[0], *received[0]]
        blocks = {
            offset: sum((piece.astype(f32) for piece in received[offset]), blocks[offset].astype(f32))
            for offset in sent[0]
        }
        bit = bit * width
    return terms


def block(
    features,
    cotangent,
    frac_pos,
    k_vectors,
    k_filter,
    w_out,
    w_short,
    edge_src,
    edge_dst,
    distance,
    halo_idx,
):
    _, atoms, _ = features.shape
    kcount = k_filter.shape[0]
    count = lax.axis_size("slab")
    replicas = lax.axis_size("rep")
    norm = 1.0 / math.sqrt(kcount * atoms * count)
    scale = 1.0 / math.sqrt(replicas * atoms * count)
    share = kcount // count
    slab = lax.axis_index("slab").astype(jnp.int32)[None]

    near, far = plane_order(count)
    near, far = (tuple(offset for group in groups for offset in group) for groups in (near, far))
    flip = lambda offsets: tuple(offset ^ 1 for offset in offsets)
    orders = (flip(far), far, flip(near), near)
    order = halving_order(count)

    odda, odda_part, k_cols, positions, rows, cotan, own_filter, src, dst, dist, lists, w_out, w_short = first_tables(
        orders[0],
        slab,
        k_vectors,
        frac_pos,
        features,
        cotangent,
        k_filter,
        (edge_src, edge_dst, distance, halo_idx, w_out, w_short),
        share,
    )
    moveda = xor_permute(odda_part, "slab", 1)
    operands = (slab, k_cols, positions, rows, cotan, share)
    evena, evena_part = next_tables(f32, orders[1], *operands)
    oddb, oddb_part = next_tables(bf16, orders[2], *operands)
    movedb = xor_permute(oddb_part, "slab", 1)
    evenb, evenb_part = next_tables(f32, orders[3], *operands)
    blocks = {}
    for offsets, part, moved in ((far, evena_part, moveda), (near, evenb_part, movedb)):
        paired = part + moved.astype(f32)
        for i, offset in enumerate(offsets):
            blocks[offset] = paired[i * 2 * share : (i + 1) * 2 * share]
    parts = folded_sum(blocks)

    rows_t, to_prev, to_next = rim_features(rows, lists)
    lower_t = shifted(to_next, "slab", 1)
    upper_t = shifted(to_prev, "slab", -1)
    own_rows, low, up, wshort = edge_rows(src, dst, dist, cotan, rows_t, lists.shape[2])
    short_terms = (wshort, lower_t, upper_t, low, up)
    adj, gfilter, send, keep = own_share(order, norm, slab, own_filter, w_out, short_terms, parts)
    grads = keep + xor_permute(send, "slab", 1)

    from_above = shifted(low, "slab", -1)
    from_below = shifted(up, "slab", 1)
    base = short_range(own_rows, from_above, from_below, lists, cotan, w_short)

    terms = plane_sum({offset: grads[i] for i, offset in enumerate(order)})
    own_grad = sum((term.astype(f32) for term in terms[1:]), terms[0])

    adj_even = plane_gather(adj, order)
    adj_odd = xor_permute(adj_even, "slab", 1)
    grad_features = back_project(orders, order, base, adj_even, adj_odd, (odda, evena, oddb, evenb))

    own_grad = sum_replicas_direct(own_grad).astype(bf16)
    filter_sum = sum_replicas(gfilter)
    grad_filter = filter_sum / replicas
    grad_even = plane_gather(own_grad, order)
    grad_odd = xor_permute(grad_even, "slab", 1)
    grad_wout, grad_wshort = place_grads(order, scale, slab, grad_even, grad_odd)
    return (grad_features[None], grad_wout, grad_wshort, grad_filter)


def solution(mesh):
    return jax.shard_map(
        block,
        mesh=mesh,
        in_specs=(
            P("rep", "slab", None),
            P("rep", "slab", None),
            P("rep", None, "slab"),
            P(),
            P(),
            P(),
            P(),
            P("rep", "slab"),
            P("rep", "slab"),
            P("rep", "slab"),
            P("rep", "slab", None),
        ),
        out_specs=(P("rep", "slab", None), P(), P(), P("slab", None)),
        check_vma=False,
    )
```

```python
import functools
import math

import jax
import jax.numpy as jnp
from jax import lax
from jax.experimental import pallas as pl
from jax.experimental.pallas import tpu as pltpu
from jax.sharding import PartitionSpec as P


cutoff_radius = 5.0
f32, bf16 = jnp.float32, jnp.bfloat16

sin_coefs = (3.1415926401307073, -5.167710083507895, 2.550077523214559, -0.5982912856198396, 0.0776576603038396)
cos_coefs = (0.9999999532476077, -4.934792830619641, 4.058411352862562, -1.331876568080612, 0.21968961109715823)

VMEM = pl.BlockSpec(memory_space=pltpu.VMEM)
SMEM = pl.BlockSpec(memory_space=pltpu.SMEM)
HBM = pl.BlockSpec(memory_space=pltpu.HBM)


def params():
    return pltpu.CompilerParams(vmem_limit_bytes=48 * 1024 * 1024)


def xor_permute(value, axis, bits):
    count = lax.axis_size(axis)
    return lax.ppermute(value, axis, [(source, source ^ bits) for source in range(count)])


def across_chips(value):
    count = lax.axis_size("slab")
    return lax.ppermute(value, "slab", [(source, (source + 2 * (source % 2) - 1) % count) for source in range(count)])


def halving_order(count):
    order, bit = [0], count // 2
    while bit > 1:
        order = order + [offset | bit for offset in order]
        bit //= 2
    return tuple(order)


def plane_order(count):
    width = min(4, count // 2)
    offsets = [[offset for offset in range(0, count, 2) if offset // 2 % width == g] for g in range(width)]
    return offsets[:-1], offsets[-1:]


def horner(coefs, z):
    total = coefs[-1]
    for c in coefs[-2::-1]:
        total = total * z + c
    return total


def halves(value):
    high = value.astype(bf16)
    return high, (value - high.astype(f32)).astype(bf16)


def dot(left, right, left_dim=1, right_dim=0):
    return lax.dot_general(left, right, (((left_dim,), (right_dim,)), ((), ())), preferred_element_type=f32)


def table_blocks(order, slab, k_cols, positions, rows_ref, cot_ref, table_ref, part_ref):
    share = table_ref.shape[0] // (2 * len(order))
    channels = rows_ref.shape[1]
    for place, offset in enumerate(order):
        start = pl.multiple_of((slab ^ offset) * share, 8)
        turns = dot(k_cols[pl.ds(start, share), :].astype(bf16), positions)
        r = turns - jnp.floor(turns + 0.5)
        z = r * r
        s = r * horner(sin_coefs, z)
        c = horner(cos_coefs, z)
        table = jnp.concatenate([1.0 - 2.0 * s * s, 2.0 * s * c], axis=0).astype(bf16)
        at = pl.ds(place * 2 * share, 2 * share)
        table_ref[at, :] = table
        part_ref[at, :channels] = dot(table, rows_ref[...]).astype(part_ref.dtype)
        part_ref[at, channels:] = dot(table, cot_ref[...]).astype(part_ref.dtype)


def first_kernel(order, fetched, slab_ref, kv_hbm, pos_hbm, rows_hbm, cot_hbm, filter_hbm, *refs):
    sources, refs = refs[:fetched], refs[fetched:]
    table_ref, part_ref, k_cols, positions, rows_ref, cot_ref, filter_ref, *refs = refs
    copies_to, (kv_ref, pos_ref, k_rows, p_rows, sems) = refs[:fetched], refs[fetched:]
    slab = slab_ref[0]
    share = filter_ref.shape[0]
    filter_rows = pl.ds(pl.multiple_of(slab * share, 8), share)
    pairs = [
        (kv_hbm, kv_ref),
        (pos_hbm.at[:, 0], pos_ref),
        (rows_hbm.at[0], rows_ref),
        (cot_hbm.at[0], cot_ref),
        (filter_hbm.at[filter_rows, :], filter_ref),
        *zip(sources, copies_to),
    ]
    copies = [pltpu.make_async_copy(source, target, sems.at[i]) for i, (source, target) in enumerate(pairs)]
    for copy in copies:
        copy.start()
    k_rows[...] = jnp.zeros_like(k_rows)
    p_rows[...] = jnp.zeros_like(p_rows)
    copies[0].wait()
    copies[1].wait()
    pos = pos_ref[...]
    high = pos.astype(bf16).astype(f32)
    middle = (pos - high).astype(bf16).astype(f32)
    kv = kv_ref[...].astype(f32)
    for i, piece in enumerate((high, middle, pos - high - middle)):
        k_rows[3 * i : 3 * i + 3, :] = kv
        p_rows[3 * i : 3 * i + 3, :] = piece
    k_cols[...] = k_rows[...].T
    positions[...] = p_rows[...].astype(bf16)
    copies[2].wait()
    copies[3].wait()
    table_blocks(order, slab, k_cols, positions[...], rows_ref, cot_ref, table_ref, part_ref)
    for copy in copies[4:]:
        copy.wait()


def first_tables(order, slab, k_vectors, frac_pos, features, cotangent, k_filter, others, share):
    _, atoms, channels = features.shape
    kcount = k_vectors.shape[1]
    height = 2 * share * len(order)
    operands = (k_vectors, frac_pos.transpose(1, 0, 2), features, cotangent, k_filter, *others)
    shapes = [
        ((height, atoms), bf16),
        ((height, 2 * channels), bf16),
        ((kcount, 16), f32),
        ((16, atoms), bf16),
        ((atoms, channels), bf16),
        ((atoms, channels), bf16),
        ((share, channels), f32),
    ] + [(other.shape, other.dtype) for other in others]
    return pl.pallas_call(
        functools.partial(first_kernel, order, len(others)),
        name="first",
        out_shape=tuple(jax.ShapeDtypeStruct(shape, dtype) for shape, dtype in shapes),
        in_specs=[SMEM] + [HBM] * (5 + len(others)),
        out_specs=(VMEM,) * len(shapes),
        scratch_shapes=[
            pltpu.VMEM((3, kcount), jnp.int32),
            pltpu.VMEM((3, atoms), f32),
            pltpu.VMEM((16, kcount), f32),
            pltpu.VMEM((16, atoms), f32),
            pltpu.SemaphoreType.DMA((5 + len(others),)),
        ],
        compiler_params=params(),
        cost_estimate=pl.CostEstimate(
            flops=4 * height * atoms * channels, bytes_accessed=4 * height * atoms, transcendentals=0
        ),
    )(slab, *(pltpu.with_memory_space_constraint(value, pltpu.HBM) for value in operands))


def second_kernel(order, slab_ref, k_cols, positions, rows_ref, cot_ref, table_ref, part_ref):
    table_blocks(order, slab_ref[0], k_cols, positions[...], rows_ref, cot_ref, table_ref, part_ref)


def next_tables(dtype, order, slab, k_cols, positions, rows, cotan, share):
    atoms, channels = rows.shape
    height = 2 * share * len(order)
    return pl.pallas_call(
        functools.partial(second_kernel, order),
        out_shape=(
            jax.ShapeDtypeStruct((height, atoms), bf16),
            jax.ShapeDtypeStruct((height, 2 * channels), dtype),
        ),
        in_specs=[SMEM] + [VMEM] * 4,
        out_specs=(VMEM, VMEM),
        compiler_params=params(),
        cost_estimate=pl.CostEstimate(
            flops=4 * height * atoms * channels, bytes_accessed=4 * height * atoms, transcendentals=0
        ),
    )(slab, k_cols, positions, rows, cotan)


def one_hot(row_count, indices):
    rows = lax.broadcasted_iota(jnp.int32, (row_count, indices.shape[1]), 0)
    return (rows == indices).astype(f32).astype(bf16)


def rim_lists(slab_ref, lists_ref):
    core = slab_ref[0] & 1
    lists = lists_ref[0]
    before, after = lists[0:1, :], lists[1:2, :]
    return jnp.where(core == 0, after, before), jnp.where(core == 0, before, after)


def rims_kernel(slab_ref, rows_ref, lists_ref, rows_t_ref, pair_ref, cross_ref):
    atoms = rows_ref.shape[0]
    pair, cross = rim_lists(slab_ref, lists_ref)
    rows_t = rows_ref[...].T
    rows_t_ref[...] = rows_t
    pair_ref[...] = dot(rows_t, one_hot(atoms, pair)).astype(bf16)
    cross_ref[...] = dot(rows_t, one_hot(atoms, cross)).astype(bf16)


def rim_features(slab, rows, lists):
    atoms, channels = rows.shape
    rim = lists.shape[2]
    return pl.pallas_call(
        rims_kernel,
        name="rims",
        out_shape=(
            jax.ShapeDtypeStruct((channels, atoms), bf16),
            jax.ShapeDtypeStruct((channels, rim), bf16),
            jax.ShapeDtypeStruct((channels, rim), bf16),
        ),
        in_specs=[SMEM] + [VMEM] * 2,
        out_specs=(VMEM,) * 3,
        compiler_params=params(),
        cost_estimate=pl.CostEstimate(
            flops=4 * atoms * channels * rim, bytes_accessed=4 * atoms * channels, transcendentals=0
        ),
    )(slab, rows, lists)


def edge_kernel(
    block, slab_ref, src_ref, dst_ref, dist_ref, cot_ref, rows_t_ref, own_ref, pair_ref, cross_ref, grad_ref, total
):
    atoms, _ = cot_ref.shape
    rim = pair_ref.shape[0]
    core = slab_ref[0] & 1
    edges = src_ref.shape[1]
    cot_t = cot_ref[...].T
    for start in range(0, edges, block):
        at = slice(start, start + block)
        weight = jnp.maximum(1.0 - dist_ref[:, at] / cutoff_radius, 0.0)
        weight = weight * weight
        taken = dot(cot_t, one_hot(atoms, dst_ref[:, at]))
        weighted = (taken * weight).astype(bf16)
        part = dot(one_hot(total.shape[0], src_ref[:, at]), weighted, 1, 1)
        total[...] = part if start == 0 else total[...] + part
    own = total[:atoms, :]
    own_ref[...] = own
    pair_ref[...] = total[pl.ds(pl.multiple_of(atoms + (1 - core) * rim, 8), rim), :].astype(bf16)
    cross_ref[...] = total[pl.ds(pl.multiple_of(atoms + core * rim, 8), rim), :].astype(bf16)
    high, low = halves(own)
    grad_ref[...] = dot(rows_t_ref[...], high) + dot(rows_t_ref[...], low)


def edge_rows(slab, sources, targets, lengths, cotan, rows_t, rim):
    atoms, channels = cotan.shape
    edges = sources.shape[1]
    rows = atoms + 2 * rim
    block = math.gcd(edges, 2048)
    return pl.pallas_call(
        functools.partial(edge_kernel, block),
        name="edges",
        out_shape=(
            jax.ShapeDtypeStruct((atoms, channels), f32),
            jax.ShapeDtypeStruct((rim, channels), bf16),
            jax.ShapeDtypeStruct((rim, channels), bf16),
            jax.ShapeDtypeStruct((channels, channels), f32),
        ),
        in_specs=[SMEM] + [VMEM] * 5,
        out_specs=(VMEM,) * 4,
        scratch_shapes=[pltpu.VMEM((rows, channels), f32)],
        compiler_params=params(),
        cost_estimate=pl.CostEstimate(
            flops=2 * edges * (rows + atoms) * channels, bytes_accessed=edges * 12, transcendentals=0
        ),
    )(slab, sources, targets, lengths, cotan, rows_t)


def split_blocks(order, slab, values, send_ref, keep_ref, blocks):
    count, height, _ = blocks.shape
    height = height // len(values)
    for i in range(count):
        for j, value in enumerate(values):
            blocks[i, j * height : (j + 1) * height] = value[i * height : (i + 1) * height, :]
    for place, offset in enumerate(order):
        keep_ref[place] = blocks[slab ^ offset]
        send_ref[place] = blocks[slab ^ offset ^ 1]


def short_kernel(slab_ref, own_ref, pair_ref, cross_ref, lists_ref, cot_ref, w_ref, base_ref):
    atoms = own_ref.shape[0]
    pair, cross = rim_lists(slab_ref, lists_ref)
    owned = own_ref[...] + dot(one_hot(atoms, pair), pair_ref[...])
    owned = owned + dot(one_hot(atoms, cross), cross_ref[...])
    high, low = halves(owned)
    w = w_ref[...]
    base_ref[...] = cot_ref[...].astype(f32) + (dot(high, w, 1, 1) + dot(low, w, 1, 1))


def short_range(slab, own, pair, cross, lists, cotan, w_short):
    atoms, channels = cotan.shape
    return pl.pallas_call(
        short_kernel,
        name="short",
        out_shape=jax.ShapeDtypeStruct((atoms, channels), f32),
        in_specs=[SMEM] + [VMEM] * 6,
        out_specs=VMEM,
        compiler_params=params(),
        cost_estimate=pl.CostEstimate(
            flops=8 * atoms * channels * channels, bytes_accessed=8 * atoms * channels, transcendentals=0
        ),
    )(slab, own, pair, cross, lists, cotan, w_short)


def share_kernel(
    order, norm, count, slab_ref, filter_ref, w_ref, grad_ref, pair_t, cross_t, pair_ref, cross_ref, *refs
):
    parts, (adj_ref, gfilter_ref, send_ref, keep_ref, blocks) = refs[:count], refs[count:]
    channels = w_ref.shape[0]
    total = parts[0][...].astype(f32)
    for part in parts[1:]:
        total = total + part[...].astype(f32)
    structure = total[:, :channels]
    moved, moved_low = halves(total[:, channels:])
    response = dot(moved, w_ref[...], 1, 1) + dot(moved_low, w_ref[...], 1, 1)
    k_filter = filter_ref[...]
    double = jnp.concatenate([k_filter, k_filter], axis=0) * norm
    filtered, filtered_low = halves((structure * double).T)
    wout = dot(filtered, moved) + (dot(filtered, moved_low) + dot(filtered_low, moved))
    wshort = grad_ref[...] + (dot(pair_t[...], pair_ref[...]) + dot(cross_t[...], cross_ref[...]))
    split_blocks(order, slab_ref[0], (wout, wshort), send_ref, keep_ref, blocks)
    adj_ref[...] = (response * double).T.astype(bf16)
    product = structure * response
    share = k_filter.shape[0]
    gfilter_ref[...] = norm * (product[:share] + product[share:])


def own_share(order, norm, slab, k_filter, w_out, short_terms, parts):
    height, channels = parts[0].shape[0], w_out.shape[0]
    half = len(order)
    rows = 2 * channels // (2 * half)
    return pl.pallas_call(
        functools.partial(share_kernel, order, norm, len(parts)),
        name="share",
        out_shape=(
            jax.ShapeDtypeStruct((channels, height), bf16),
            jax.ShapeDtypeStruct((height // 2, channels), f32),
            jax.ShapeDtypeStruct((half, rows, channels), f32),
            jax.ShapeDtypeStruct((half, rows, channels), f32),
        ),
        in_specs=[SMEM] + [VMEM] * (2 + len(short_terms) + len(parts)),
        out_specs=(VMEM,) * 4,
        scratch_shapes=[pltpu.VMEM((2 * half, rows, channels), f32)],
        compiler_params=params(),
        cost_estimate=pl.CostEstimate(
            flops=8 * height * channels * channels, bytes_accessed=16 * height * channels, transcendentals=0
        ),
    )(slab, k_filter, w_out, *short_terms, *parts)


def back_kernel(orders, order, base_ref, even_adj_ref, odd_adj_ref, *refs):
    table_refs, out_ref = refs[:-1], refs[-1]
    width = even_adj_ref.shape[2]
    total = None
    for offsets, table_ref in zip(orders, table_refs):
        for place, offset in enumerate(offsets):
            adj = (odd_adj_ref if offset & 1 else even_adj_ref)[order.index(offset & ~1)]
            part = dot(adj, table_ref[place * width : (place + 1) * width, :])
            total = part if total is None else total + part
    out_ref[...] = (base_ref[...] + total.T).astype(bf16)


def back_project(orders, order, base, even_adj, odd_adj, tables):
    atoms, channels = base.shape
    height = sum(table.shape[0] for table in tables)
    return pl.pallas_call(
        functools.partial(back_kernel, orders, order),
        name="back",
        out_shape=jax.ShapeDtypeStruct((atoms, channels), bf16),
        in_specs=[VMEM] * (3 + len(tables)),
        out_specs=VMEM,
        compiler_params=params(),
        cost_estimate=pl.CostEstimate(
            flops=2 * height * atoms * channels, bytes_accessed=2 * height * atoms, transcendentals=0
        ),
    )(base, even_adj, odd_adj, *tables)


def place_kernel(order, scale, slab_ref, even_ref, odd_ref, wout_ref, wshort_ref, blocks):
    count, height, _ = blocks.shape
    half = height // 2
    slab = slab_ref[0]
    for place, offset in enumerate(order):
        blocks[slab ^ offset] = even_ref[place].astype(f32) * scale
        blocks[slab ^ offset ^ 1] = odd_ref[place].astype(f32) * scale
    for i in range(count):
        wout_ref[i * half : (i + 1) * half, :] = blocks[i, :half, :]
        wshort_ref[i * half : (i + 1) * half, :] = blocks[i, half:, :]


def place_grads(order, scale, slab, even, odd):
    half, height, channels = even.shape
    return pl.pallas_call(
        functools.partial(place_kernel, order, scale),
        name="place",
        out_shape=(jax.ShapeDtypeStruct((channels, channels), f32),) * 2,
        in_specs=[SMEM, VMEM, VMEM],
        out_specs=(VMEM, VMEM),
        scratch_shapes=[pltpu.VMEM((2 * half, height, channels), f32)],
        compiler_params=params(),
    )(slab, even, odd)


def sum_replicas(value):
    bit = 1
    while bit < lax.axis_size("rep"):
        sent = value.astype(bf16)
        moved = xor_permute(sent, "rep", bit)
        value = sent.astype(f32) + moved.astype(f32)
        bit = 2 * bit
    return value


def sum_replicas_direct(value):
    count = lax.axis_size("rep")
    terms = [value.astype(bf16)]
    for offset in range(count - 1, 0, -1):
        terms.insert(1, xor_permute(terms[0], "rep", offset))
    terms = [term.astype(f32) for term in terms]
    while len(terms) > 1:
        terms = [terms[i] + terms[i + 1] for i in range(0, len(terms), 2)]
    return terms[0]


def folded_sum(blocks):
    count = lax.axis_size("slab")
    bit = 2
    terms = None
    while bit < count:
        width = min(4, count // bit)
        sent = [[offset for offset in sorted(blocks) if offset // bit % width == g] for g in range(width)]
        half = blocks[0].shape[1] // 2

        def move(g, pieces):
            payload = pieces[0] if len(pieces) == 1 else jnp.concatenate(pieces, axis=0)
            moved = xor_permute(payload, "slab", g * bit)
            return jnp.split(moved, len(pieces), axis=0)

        if width == 4:
            first = move(1, [blocks[offset][:, :half].astype(bf16) for offset in sent[3]])
            second = move(2, [blocks[offset][:, half:].astype(bf16) for offset in sent[3]])
            for i, offset in enumerate(sent[2]):
                left = blocks[offset][:, :half] + first[i].astype(f32)
                blocks[offset] = jnp.concatenate([left, blocks[offset][:, half:]], axis=1)
            for i, offset in enumerate(sent[1]):
                right = blocks[offset][:, half:] + second[i].astype(f32)
                blocks[offset] = jnp.concatenate([blocks[offset][:, :half], right], axis=1)
        received = [move(g, [blocks[offset].astype(bf16) for offset in sent[g]]) for g in range(1, min(width, 3))]
        terms = [blocks[0], *(moved[0] for moved in received)]
        blocks = {
            offset: sum((moved[i].astype(f32) for moved in received), blocks[offset])
            for i, offset in enumerate(sent[0])
        }
        bit = bit * width
    return terms


def plane_gather(block, order):
    count = lax.axis_size("slab")
    planes, bit = [], 2
    while bit < count:
        planes.append((bit, min(4, count // bit)))
        bit *= planes[-1][1]
    held = {0: block}
    for bit, width in reversed(planes):
        offsets = sorted(held)
        payload = held[0] if len(held) == 1 else jnp.stack([held[offset] for offset in offsets])
        for g in range(width - 1, 0, -1):
            moved = xor_permute(payload, "slab", g * bit)
            for i, offset in enumerate(offsets):
                held[offset ^ g * bit] = moved if len(offsets) == 1 else moved[i]
    return jnp.stack([held[offset] for offset in order])


def plane_sum(blocks):
    count = lax.axis_size("slab")
    bit = 2
    terms = None
    while bit < count:
        width = min(4, count // bit)
        sent = {g: [] for g in range(width)}
        for offset in sorted(blocks):
            sent[offset // bit % width].append(offset)
        received = {offset: [] for offset in sent[0]}
        for g in range(width - 1, 0, -1):
            pieces = [blocks[offset].astype(bf16) for offset in sent[g]]
            payload = pieces[0] if len(pieces) == 1 else jnp.concatenate(pieces, axis=0)
            moved = xor_permute(payload, "slab", g * bit)
            height = moved.shape[0] // len(pieces)
            for i, offset in enumerate(sent[0]):
                received[offset].append(moved[i * height : (i + 1) * height])
        terms = [blocks[0], *received[0]]
        blocks = {
            offset: sum((piece.astype(f32) for piece in received[offset]), blocks[offset].astype(f32))
            for offset in sent[0]
        }
        bit = bit * width
    return terms


def block(
    features,
    cotangent,
    frac_pos,
    k_vectors,
    k_filter,
    w_out,
    w_short,
    edge_src,
    edge_dst,
    distance,
    halo_idx,
):
    _, atoms, _ = features.shape
    kcount = k_filter.shape[0]
    count = lax.axis_size("slab")
    replicas = lax.axis_size("rep")
    norm = 1.0 / math.sqrt(kcount * atoms * count)
    scale = 1.0 / math.sqrt(replicas * atoms * count)
    share = kcount // count
    slab = lax.axis_index("slab").astype(jnp.int32)[None]

    near, far = plane_order(count)
    near, far = (tuple(offset for group in groups for offset in group) for groups in (near, far))
    flip = lambda offsets: tuple(offset ^ 1 for offset in offsets)
    orders = (flip(far), far, flip(near), near)
    order = halving_order(count)

    odda, odda_part, k_cols, positions, rows, cotan, own_filter, src, dst, dist, lists, w_out, w_short = first_tables(
        orders[0],
        slab,
        k_vectors,
        frac_pos,
        features,
        cotangent,
        k_filter,
        (edge_src, edge_dst, distance, halo_idx, w_out, w_short),
        share,
    )
    moveda = xor_permute(odda_part, "slab", 1)
    operands = (slab, k_cols, positions, rows, cotan, share)
    evena, evena_part = next_tables(f32, orders[1], *operands)
    oddb, oddb_part = next_tables(bf16, orders[2], *operands)
    movedb = xor_permute(oddb_part, "slab", 1)
    evenb, evenb_part = next_tables(f32, orders[3], *operands)
    blocks = {}
    for offsets, part, moved in ((far, evena_part, moveda), (near, evenb_part, movedb)):
        paired = part + moved.astype(f32)
        for i, offset in enumerate(offsets):
            blocks[offset] = paired[i * 2 * share : (i + 1) * 2 * share]
    parts = folded_sum(blocks)

    rows_t, to_pair, to_cross = rim_features(slab, rows, lists)
    cross_t = across_chips(to_cross)
    pair_t = xor_permute(to_pair, "slab", 1)
    own_rows, pair_rows, cross_rows, wshort = edge_rows(slab, src, dst, dist, cotan, rows_t, lists.shape[2])
    short_terms = (wshort, pair_t, cross_t, pair_rows, cross_rows)
    adj, gfilter, send, keep = own_share(order, norm, slab, own_filter, w_out, short_terms, parts)
    grads = keep + xor_permute(send, "slab", 1)

    from_cross = across_chips(cross_rows)
    from_pair = xor_permute(pair_rows, "slab", 1)
    base = short_range(slab, own_rows, from_pair, from_cross, lists, cotan, w_short)

    terms = plane_sum({offset: grads[i] for i, offset in enumerate(order)})
    own_grad = sum((term.astype(f32) for term in terms[1:]), terms[0])

    adj_even = plane_gather(adj, order)
    adj_odd = xor_permute(adj_even, "slab", 1)
    grad_features = back_project(orders, order, base, adj_even, adj_odd, (odda, evena, oddb, evenb))

    own_grad = sum_replicas_direct(own_grad).astype(bf16)
    filter_sum = sum_replicas(gfilter)
    grad_filter = filter_sum / replicas
    grad_even = plane_gather(own_grad, order)
    grad_odd = xor_permute(grad_even, "slab", 1)
    grad_wout, grad_wshort = place_grads(order, scale, slab, grad_even, grad_odd)
    return (grad_features[None], grad_wout, grad_wshort, grad_filter)


def solution(mesh):
    return jax.shard_map(
        block,
        mesh=mesh,
        in_specs=(
            P("rep", "slab", None),
            P("rep", "slab", None),
            P("rep", None, "slab"),
            P(),
            P(),
            P(),
            P(),
            P("rep", "slab"),
            P("rep", "slab"),
            P("rep", "slab"),
            P("rep", "slab", None),
        ),
        out_specs=(P("rep", "slab", None), P(), P(), P("slab", None)),
        check_vma=False,
    )
```
